32 devices in a mesh: groups: 2 (over x), seq: 16 (over z, y, core).
Axes of the slice: x: 2, y: 2, z: 4, core: 2. Of those that a mesh axis runs over, the one named last changes fastest.
Arguments:
- hidden: bfloat16 [64, 16384], P('groups', 'seq'), parts along dimension 0, may hold values from -6 to 6
- w_query: bfloat16 [16384, 8192], P('seq'), may hold values from -0.046875 to 0.046875
- w_key: bfloat16 [16384, 512], P('seq'), may hold values from -0.25 to 0.25
- w_value: bfloat16 [16384, 512], P('seq'), may hold values from -0.1875 to 0.1875
- w_out: bfloat16 [8192, 16384], P(None, 'seq'), may hold values from -0.0625 to 0.0625
- prefix_keys: bfloat16 [65536, 512], P(('groups', 'seq')), parts along dimension 0, may hold values from -6 to 6
- prefix_values: bfloat16 [65536, 512], P(('groups', 'seq')), parts along dimension 0, may hold values from -6 to 6
- key_scales: float32 [512, 4], P(('groups', 'seq')), parts along dimension 0, may hold values from 1 to 2.5
- value_scales: float32 [512, 4], P(('groups', 'seq')), parts along dimension 0, may hold values from 0.5 to 2
- demo_keys: bfloat16 [32, 2048, 512], P('groups', 'seq'), parts along dimension 0, may hold values from -200 to 200
- demo_values: bfloat16 [32, 2048, 512], P('groups', 'seq'), parts along dimension 0, may hold values from -12 to 12
- task_ids: int32 [64], P('groups'), parts along dimension 0, may hold values from 0 to 15
- demo_lengths: int32 [32], P('groups'), parts along dimension 0, may hold values from 1 to 2048, 16384 in all
- offsets: int32 [64], P('groups'), parts along dimension 0, may hold values from 0 to 31
Outputs:
- mixed: bfloat16 [64, 16384], P('groups', 'seq'), parts along dimension 0
The draws below stay inside these ranges and needn't reach their ends.
There are 2 independent parts, one for each index of `groups`. The reference program is written for one: setup_inputs(seed, part) draws one part's arguments, and reference() takes and returns one part's arrays. A program takes and returns all parts, laid end to end along the dimension named above; an argument that names none is the same for every part. Nothing has to cross between parts.
Inputs may be any that keep to these rules, and one draw needn't show every extreme that they name: `demo_lengths`: the largest is exactly 2048.
All inputs are finite; a program needn't handle non-finite values.
Results may differ from the reference program's by a relative error of at most 0.007.
The reference program's roundings to bfloat16 on the way count: a program that leaves them out, or rounds other values in their place, can miss the bound.
Values may be sent and summed in bfloat16 or wider, within the bound.
A program may use at most 128 MiB of HBM per device.

```python
import math
import jax
import jax.numpy as jnp
import numpy as np
from jax import lax

D = 16384
HEADS = 64
KVH = 4
HD = 128
TASKS = 16
DEMO = 2048
BLK = 128
QTOK = 32
PREFIX = 32768


def draw_demo_keys(key, part):
    shape = (TASKS, DEMO, KVH * HD)
    return jnp.clip(3.5 * jax.random.normal(key, shape, jnp.float32), -21.0, 21.0).astype(jnp.bfloat16)


def with_ends(entries, key, least, top_value):
    index_at = [jax.random.randint(jax.random.fold_in(key, axis), (), 0, length) for axis, length in enumerate(entries.shape)]
    main_axis = entries.shape.index(max(entries.shape))
    beside = index_at[:main_axis] + [(index_at[main_axis] + 1) % entries.shape[main_axis]] + index_at[main_axis + 1:]
    return entries.at[tuple(index_at)].set(least).at[tuple(beside)].set(top_value)


def block_scale(stream_key, extent, shards, low, top_value):
    gain = 1.0
    for dim, shards_of in shards:
        heights = jax.random.uniform(jax.random.fold_in(jax.random.fold_in(stream_key, 6), dim), (shards_of,), jnp.float32, low / len(shards), top_value / len(shards))
        gain = gain * jnp.repeat(jnp.exp(heights), extent[dim] // shards_of).reshape((-1,) + (1,) * (len(extent) - 1 - dim))
    return gain


def profile(count, total, limit, slope):
    loads = [(1 << 20) // math.isqrt(grade ** slope) + 1 for grade in range(2, count + 1)]
    rest, counts = total - limit - (count - 1), [1] * (count - 1)
    while rest > 0:
        movable = [i for i in range(count - 1) if counts[i] < limit]
        mass, left = sum([loads[i] for i in movable]), rest
        for i in movable:
            extra = min(limit - counts[i], max(1, left * loads[i] // mass), rest)
            counts[i] = counts[i] + extra
            rest = rest - extra
    return np.array([limit] + counts)


def ragged_sizes(stream_key, number_of, total, bound, lean):
    if number_of == 2:
        one = jax.random.randint(stream_key, (), max(1, total - bound), min(bound, total - 1) + 1)
        return jnp.stack([one, total - one])
    tallies = jnp.asarray(profile(number_of, total, bound, lean), jnp.int32)
    couples = (number_of - 1) // 2
    source_of, receiver = tallies[1:1 + 2 * couples:2], tallies[2:2 + 2 * couples:2]
    margin = jnp.minimum(source_of - 1, bound - receiver)
    moved = jax.random.randint(jax.random.fold_in(stream_key, 1), (couples,), 0, 1 << 20) % (margin + 1)
    tallies = tallies.at[1:1 + 2 * couples:2].set(source_of - moved).at[2:2 + 2 * couples:2].set(receiver + moved)
    return tallies[jax.random.permutation(jax.random.fold_in(stream_key, 2), number_of)]


def centred(stream_key, dims, spread, limit, split=(), held_as=jnp.bfloat16):
    loudness = block_scale(stream_key, dims, split, -0.22, 0.18) if split else 1.0
    result = jax.random.normal(stream_key, dims, jnp.float32) * spread * loudness
    return jnp.minimum(jnp.maximum(result, -limit), limit).astype(held_as)


def setup_inputs(seed: int = 0, part: int = 0) -> dict:
    keys = jax.random.split(jax.random.key(seed), 15)
    part_keys = jax.random.split(jax.random.fold_in(keys[14], part), 15)
    hidden = centred(part_keys[0], (QTOK, D), 1.0, 6.0, ((1, 16),))
    w_query = centred(keys[1], (D, HEADS * HD), D ** -0.5, 0.046875, ((0, 16),))
    w_key = centred(keys[2], (D, KVH * HD), (D // 25) ** -0.5, 0.25, ((0, 16),))
    w_value = centred(keys[3], (D, KVH * HD), (D // 16) ** -0.5, 0.1875, ((0, 16),))
    w_out = centred(keys[4], (HEADS * HD, D), (HEADS * HD) ** -0.5, 0.0625, ((1, 16),))
    prefix_keys = centred(part_keys[5], (PREFIX, KVH * HD), 1.0, 6.0, ((0, 16),))
    prefix_values = centred(part_keys[6], (PREFIX, KVH * HD), 1.0, 6.0, ((0, 16),))
    key_scales = jnp.clip(jnp.exp(math.log(2.5) - 0.916290732 * jax.random.uniform(part_keys[7], (PREFIX // BLK, KVH), jnp.float32) ** block_scale(part_keys[7], (PREFIX // BLK, KVH), ((0, 16),), -0.2, 0.2)), 1.0, 2.5)
    value_scales = jnp.clip(jnp.exp(math.log(2.0) - 1.3862944 * jax.random.uniform(part_keys[8], (PREFIX // BLK, KVH), jnp.float32) ** block_scale(part_keys[8], (PREFIX // BLK, KVH), ((0, 16),), -0.2, 0.2)), 0.5, 2.0)
    demo_keys = draw_demo_keys(jax.random.fold_in(jax.random.fold_in(keys[14], part), 71), part)
    demo_values = centred(part_keys[10], (TASKS, DEMO, KVH * HD), 2.0, 12.0, ((1, 16),))
    task_ids = with_ends(jax.random.randint(part_keys[11], (QTOK,), 0, TASKS), jax.random.fold_in(part_keys[11], 1), 0, TASKS - 1).astype(jnp.int32)
    demo_lengths = ragged_sizes(part_keys[12], TASKS, TASKS * DEMO // 2, DEMO, 2).astype(jnp.int32)
    offsets = with_ends(jax.random.randint(part_keys[13], (QTOK,), 0, 32), jax.random.fold_in(part_keys[13], 1), 0, 31).astype(jnp.int32)
    return {"hidden": hidden, "w_query": w_query, "w_key": w_key, "w_value": w_value, "w_out": w_out, "prefix_keys": prefix_keys, "prefix_values": prefix_values, "key_scales": key_scales, "value_scales": value_scales, "demo_keys": demo_keys, "demo_values": demo_values, "task_ids": task_ids, "demo_lengths": demo_lengths, "offsets": offsets}


NEG = -1e+30

def one_head(args):
    q_rows, p_keys, p_vals, k_scale, v_scale, d_keys, d_vals, s_keys, s_vals, d_mask, s_mask = args
    inv = 1.0 / math.sqrt(HD)
    s_pre = jnp.dot(q_rows, p_keys.T, preferred_element_type=jnp.float32) * (k_scale[None, :] * inv)
    s_demo = jnp.where(d_mask, jnp.dot(q_rows, d_keys.T, preferred_element_type=jnp.float32) * inv, NEG)
    s_self = jnp.where(s_mask, jnp.dot(q_rows, s_keys.T, preferred_element_type=jnp.float32) * inv, NEG)
    top = jnp.maximum(jnp.maximum(lax.optimization_barrier(jnp.max(s_pre, axis=1)), lax.optimization_barrier(jnp.max(s_demo, axis=1))), lax.optimization_barrier(jnp.max(s_self, axis=1)))
    e_pre = jnp.exp(s_pre - top[:, None])
    e_demo = jnp.exp(s_demo - top[:, None])
    e_self = jnp.exp(s_self - top[:, None])
    total = lax.optimization_barrier(jnp.sum(e_pre, axis=1)) + lax.optimization_barrier(jnp.sum(e_demo, axis=1)) + lax.optimization_barrier(jnp.sum(e_self, axis=1))
    acc = jnp.dot((e_pre * v_scale[None, :]).astype(jnp.bfloat16), p_vals, preferred_element_type=jnp.float32)
    acc = acc + jnp.dot(e_demo.astype(jnp.bfloat16), d_vals, preferred_element_type=jnp.float32)
    acc = acc + jnp.dot(e_self.astype(jnp.bfloat16), s_vals, preferred_element_type=jnp.float32)
    return (acc / total[:, None]).astype(jnp.bfloat16)

def reference(hidden, w_query, w_key, w_value, w_out, prefix_keys, prefix_values, key_scales, value_scales, demo_keys, demo_values, task_ids, demo_lengths, offsets):
    group = HEADS // KVH
    query = jnp.dot(hidden, w_query, preferred_element_type=jnp.float32).astype(jnp.bfloat16)
    s_keys = jnp.dot(hidden, w_key, preferred_element_type=jnp.float32).astype(jnp.bfloat16)
    s_vals = jnp.dot(hidden, w_value, preferred_element_type=jnp.float32).astype(jnp.bfloat16)
    q_heads = query.reshape(QTOK, KVH, group, HD).transpose(1, 0, 2, 3).reshape(KVH, QTOK * group, HD)
    p_keys = prefix_keys.reshape(PREFIX, KVH, HD).transpose(1, 0, 2)
    p_vals = prefix_values.reshape(PREFIX, KVH, HD).transpose(1, 0, 2)
    k_scale = jnp.repeat(key_scales, BLK, axis=0).T
    v_scale = jnp.repeat(value_scales, BLK, axis=0).T
    d_keys = demo_keys.reshape(TASKS * DEMO, KVH, HD).transpose(1, 0, 2)
    d_vals = demo_values.reshape(TASKS * DEMO, KVH, HD).transpose(1, 0, 2)
    sk = s_keys.reshape(QTOK, KVH, HD).transpose(1, 0, 2)
    sv = s_vals.reshape(QTOK, KVH, HD).transpose(1, 0, 2)
    demo_task = jnp.repeat(jnp.arange(TASKS, dtype=jnp.int32), DEMO)
    demo_pos = jnp.tile(jnp.arange(DEMO, dtype=jnp.int32), TASKS)
    live = demo_pos < demo_lengths[demo_task]
    d_mask = (task_ids[:, None] == demo_task[None, :]) & live[None, :]
    s_mask = (task_ids[:, None] == task_ids[None, :]) & (offsets[None, :] <= offsets[:, None])
    d_mask = jnp.repeat(d_mask, group, axis=0)
    s_mask = jnp.repeat(s_mask, group, axis=0)

    def run(h):
        return one_head((q_heads[h], p_keys[h], p_vals[h], k_scale[h], v_scale[h], d_keys[h], d_vals[h], sk[h], sv[h], d_mask, s_mask))
    heads_out = lax.map(run, jnp.arange(KVH, dtype=jnp.int32))
    attended = heads_out.reshape(KVH, QTOK, group, HD).transpose(1, 0, 2, 3).reshape(QTOK, HEADS * HD)
    return jnp.dot(attended, w_out, preferred_element_type=jnp.float32).astype(jnp.bfloat16)
```

```python
import functools
import math
import types

import jax
import jax.numpy as jnp
from jax import lax
from jax.experimental import pallas as pl
from jax.experimental.pallas import tpu as pltpu
from jax.sharding import PartitionSpec as P

HD = 128
NEG = -1e30
SIDES = 2
STAT = 8
F32 = jnp.float32
BF16 = jnp.bfloat16


def nt(a, b):
    return lax.dot_general(a, b, (((1,), (1,)), ((), ())), preferred_element_type=F32)


def nn(a, b):
    return jnp.dot(a, b, preferred_element_type=F32)


def loop(n, step):
    def wrapped(i, carry):
        step(i)
        return carry

    lax.fori_loop(0, n, wrapped, 0)


def remote(src, dst, send, recv, dev):
    return pltpu.make_async_remote_copy(
        src_ref=src,
        dst_ref=dst,
        send_sem=send,
        recv_sem=recv,
        device_id={"seq": dev},
        device_id_type=pl.DeviceIdType.MESH,
    )


def kernel(cfg, names, *refs):
    r = types.SimpleNamespace(**dict(zip(names, refs)))
    kvh, group, half, devices = cfg.kvh, cfg.group, cfg.half, cfg.devices
    tq, tz, qtok, blk, rows = cfg.tq, cfg.tz, cfg.qtok, cfg.blk, cfg.rows
    nch, cw = cfg.nch, cfg.cw
    index = lax.axis_index("seq")
    chip, core = index // 2, lax.rem(index, 2)
    far, near = chip // SIDES, lax.rem(chip, SIDES)
    const = math.log2(math.e) / math.sqrt(HD)

    def device(f, n, c):
        return (f * SIDES + n) * 2 + c

    partner = device(far, near, 1 - core)
    across = device(far, 1 - near, core)

    def up(i):
        return lax.rem(far + i, half)

    def down(i):
        return lax.rem(far - i + half, half)

    def load_wq(k):
        src = r.wq.at[:, pl.ds(pl.multiple_of(k * cw, HD), cw)]
        return pltpu.make_async_copy(src, r.wqb.at[k], r.s_wq.at[k])

    def load_wo(h):
        deep = group * HD
        src = r.wo.at[pl.ds(pl.multiple_of(h * deep, HD), deep), :]
        return pltpu.make_async_copy(src, r.wob.at[h], r.s_wo.at[h])

    def load_cache(h):
        lanes = pl.ds(pl.multiple_of(h * HD, HD), HD)
        return (
            pltpu.make_async_copy(r.pk.at[:, lanes], r.pkb.at[h], r.s_pk.at[h]),
            pltpu.make_async_copy(r.dk.at[:, :, lanes], r.dkb.at[h], r.s_dk.at[h]),
            pltpu.make_async_copy(r.pv.at[:, lanes], r.pvb.at[h], r.s_pv.at[h]),
            pltpu.make_async_copy(r.dv.at[:, :, lanes], r.dvb.at[h], r.s_dv.at[h]),
        )

    small = [
        pltpu.make_async_copy(src, dst, r.s_in.at[i])
        for i, (src, dst) in enumerate(((r.hid, r.hidb), (r.wk, r.wkb), (r.wv, r.wvb)))
    ]
    small[0].start()
    loop(nch, lambda k: load_wq(k).start())
    small[1].start()
    small[2].start()
    loop((kvh - 1) * nch, lambda k: load_wq(k + nch).start())

    barrier = pltpu.get_barrier_semaphore()

    def greet(k):
        pl.semaphore_signal(
            barrier,
            inc=1,
            device_id={"seq": lax.rem(index + 1 + k, devices)},
            device_id_type=pl.DeviceIdType.MESH,
        )

    loop(devices - 1, greet)

    lane_d = lax.broadcasted_iota(jnp.int32, (1, cfg.demo_dev), 1)
    lane_t = lax.broadcasted_iota(jnp.int32, (1, qtok), 1)

    def spread(t, carry):
        here = lane_t == t
        return tuple(jnp.where(here, v[t], old) for v, old in zip((r.tasks, r.offs), carry))

    zero = jnp.zeros((1, qtok), jnp.int32)
    task_all, off_all = lax.fori_loop(0, qtok, spread, (zero, zero))
    mine = lax.rem(lane_t, devices) == index

    def mask(t):
        task = r.tasks[t]
        left = r.lens[task] - index * cfg.demo_dev
        r.dmask[pl.ds(t, 1), :] = jnp.where(lane_d < left, 0.0, NEG)
        keep = mine & (task_all == task) & (off_all <= r.offs[t])
        r.smask[pl.ds(t, 1), :] = jnp.where(keep, 0.0, NEG)

    loop(qtok, mask)
    r.gs[...] = jnp.zeros_like(r.gs)
    r.acc[...] = jnp.zeros_like(r.acc)
    small[0].wait()

    def project(h):
        def chunk(n):
            k = h * nch + n
            load_wq(k).wait()
            res = nn(r.hidb[...], r.wqb[k])
            per = cw // HD
            for c in range(2):
                for s in range(SIDES):
                    at = (c * SIDES + s) * tq
                    for u in range(per):
                        r.part[h, c, s, n * per + u] = res[at : at + tq, u * HD : (u + 1) * HD]

        loop(nch, chunk)

    def project_kv():
        for copy in small[1:]:
            copy.wait()
        for e, w in enumerate((r.wkb, r.wvb)):
            res = nn(r.hidb[...], w[...])
            for c in range(2):
                for s in range(SIDES):
                    at = (c * SIDES + s) * tq
                    for h in range(kvh):
                        r.kpart[c, s, 2 * h + e] = res[at : at + tq, h * HD : (h + 1) * HD]

    def pair(h):
        return remote(r.part.at[h, 1 - core], r.recv1.at[h], r.s1.at[h], r.r1.at[h], partner)

    def pair_kv():
        return remote(r.kpart.at[1 - core], r.krecv1, r.ks1.at[0], r.kr1.at[0], partner)

    def cross(h):
        return remote(r.ysum.at[h], r.yrecv.at[h], r.sy.at[h], r.ry.at[h], across)

    def cross_kv():
        return remote(r.kysum, r.kyrecv, r.ksy.at[0], r.kry.at[0], across)

    def long(h, i):
        return remote(
            r.zbuf.at[h, pl.ds(up(i) * tz, tz)], r.zrecv.at[h, i - 1],
            r.sz.at[h, i - 1], r.rz.at[h, i - 1], device(up(i), near, core),
        )

    def long_kv(i):
        return remote(
            r.kz.at[pl.ds(up(i) * cfg.kuz, cfg.kuz)], r.kzrecv.at[i - 1],
            r.ksz.at[i - 1], r.krz.at[i - 1], device(up(i), near, core),
        )

    def side(k):
        return lax.rem(near + lax.rem(k, 2), 2)

    def spreading(buf, send, recv, k):
        dev = device(up(k // 2), side(k), core)
        piece = buf.at[core, near, far]
        return remote(piece, piece, send.at[k], recv.at[k], dev)

    def landing(buf, send, recv, k):
        dev = device(up(k // 2), side(k), core)
        piece = buf.at[core, side(k), down(k // 2)]
        return remote(piece, piece, send.at[k], recv.at[k], dev)

    def forward(buf, send, recv):
        return remote(buf.at[core], buf.at[core], send, recv, partner)

    def arrived(buf, send, recv):
        return remote(buf.at[1 - core], buf.at[1 - core], send, recv, partner)

    chips = SIDES * half

    def spread_out(buf, send, recv):
        loop(chips - 1, lambda k: spreading(buf, send, recv, k + 1).start())

    def pass_on(buf, send, recv, fsend, frecv):
        loop(chips - 1, lambda k: landing(buf, send, recv, k + 1).wait_recv())
        forward(buf, fsend, frecv).start()

    def q_gather(h):
        return r.gat.at[h], r.sg.at[h], r.rg.at[h]

    def kv_gather():
        return r.gkv, r.ksg, r.krg

    def o_gather(h):
        return r.agat.at[h], r.sa.at[h], r.ra.at[h]

    def stage_b(h):
        pair(h).wait_recv()
        r.ysum[h] = r.part[h, core, 1 - near] + r.recv1[h, 1 - near]
        cross(h).start()
        r.own[h] = r.part[h, core, near] + r.recv1[h, near]

    def stage_b_kv():
        pair_kv().wait_recv()
        r.kysum[...] = r.kpart[core, 1 - near] + r.krecv1[1 - near]
        cross_kv().start()
        r.kown[...] = r.kpart[core, near] + r.krecv1[near]

    def stage_c(h):
        cross(h).wait_recv()
        r.zbuf[h] = jnp.swapaxes(r.own[h] + r.yrecv[h], 0, 1)
        loop(half - 1, lambda i: long(h, i + 1).start())

    def stage_c_kv():
        cross_kv().wait_recv()
        r.kz[...] = r.kown[...] + r.kyrecv[...]
        loop(half - 1, lambda i: long_kv(i + 1).start())

    def stage_d(h):
        total = r.zbuf[h, pl.ds(far * tz, tz)]
        for i in range(1, half):
            long(h, i).wait_recv()
            total = total + r.zrecv[h, i - 1]
        r.gat[h, core, near, far] = total.astype(BF16)
        spread_out(*q_gather(h))

    def stage_d_kv():
        total = r.kz[pl.ds(far * cfg.kuz, cfg.kuz)]
        for i in range(1, half):
            long_kv(i).wait_recv()
            total = total + r.kzrecv[i - 1]
        r.gkv[core, near, far] = total.astype(BF16)
        spread_out(*kv_gather())

    def stage_e(h):
        pass_on(*q_gather(h), r.sf.at[h], r.rf.at[h])

    def front(i):
        @pl.when(i < kvh)
        def _():
            project(i)
            pair(i).start()

        @pl.when(i < kvh + 1)
        def _():
            stage_b(i - 1)

        @pl.when(i == 1)
        def _():
            stage_b_kv()

        @pl.when((i >= 3) & (i < kvh + 3))
        def _():
            stage_c(i - 3)

        @pl.when(i == 3)
        def _():
            stage_c_kv()

            def caches(h):
                for copy in load_cache(h):
                    copy.start()

            loop(kvh, caches)
            loop(kvh, lambda h: load_wo(h).start())

        @pl.when(i >= 5)
        def _():
            stage_d(i - 5)

        @pl.when(i == 5)
        def _():
            stage_d_kv()

    project(0)
    pl.semaphore_wait(barrier, devices - 1)
    pair(0).start()
    project_kv()
    pair_kv().start()
    loop(kvh + 4, lambda i: front(i + 1))
    stage_e(0)
    pass_on(*kv_gather(), r.ksf.at[0], r.krf.at[0])
    arrived(r.gkv, r.ksf.at[0], r.krf.at[0]).wait_recv()

    def out_send(h, b, k):
        c, s = b // SIDES, b % SIDES
        dev = device(up(k), s, c)
        return (
            remote(
                r.oval.at[h, b, up(k)], r.rval.at[h, index],
                r.so.at[h, b * half + k], r.ro.at[h, index], dev,
            ),
            remote(
                r.ostat.at[h, b], r.rstat.at[h, index],
                r.st.at[h, b * half + k], r.rt.at[h, index], dev,
            ),
        )

    def is_me(b, k):
        return (k == 0) & (core == b // SIDES) & (near == b % SIDES)

    def out_from(h, dev):
        return (
            remote(r.oval.at[h, 0, 0], r.rval.at[h, dev], r.so.at[h, 0], r.ro.at[h, dev], dev),
            remote(r.ostat.at[h, 0], r.rstat.at[h, dev], r.st.at[h, 0], r.rt.at[h, dev], dev),
        )

    width = 2 * blk
    steps = cfg.pre_dev // width
    blocks = 2 * SIDES

    def attend(h, between):
        def query(b):
            return r.gat[h, b // SIDES, b % SIDES].reshape(rows, HD)

        def self_kv(e):
            unit = 2 * h + e
            f, j = unit // cfg.kuz, lax.rem(unit, cfg.kuz)
            return jnp.concatenate(
                [r.gkv[c, s, f, j] for c in range(2) for s in range(SIDES)], axis=0
            )

        self_k, self_v = self_kv(0), self_kv(1)

        def score(b, j, q, run):
            s = nt(q, r.pkb[h, j * width : (j + 1) * width, :])
            for e in range(2):
                at = 2 * j + e
                x = s[:, e * blk : (e + 1) * blk] * (r.ks[h, at] * const)
                r.scr[b % 2][:, at * blk : (at + 1) * blk] = x
                run = jnp.maximum(run, x)
            return run

        def small_scores(b, q):
            demo, bias = [], []
            for t in range(tq):
                tok = b * tq + t
                k = r.dkb[h, r.tasks[tok]]
                s = nt(q[t * group : (t + 1) * group], k) * const
                demo.append(s + r.dmask[tok : tok + 1, :])
                bias.append(jnp.broadcast_to(r.smask[tok : tok + 1, :], (group, qtok)))
            own = nt(q, self_k) * const + jnp.concatenate(bias, axis=0)
            return jnp.concatenate(demo, axis=0), own

        def first(b):
            return jnp.full((rows, blk), NEG, F32)

        q = query(0)
        run = first(0)
        for j in range(steps):
            run = score(0, j, q, run)
        for b in range(blocks):
            s_demo, s_self = small_scores(b, q)
            top = jnp.maximum(
                jnp.max(run, axis=1, keepdims=True),
                jnp.maximum(
                    jnp.max(s_demo, axis=1, keepdims=True), jnp.max(s_self, axis=1, keepdims=True)
                ),
            )
            e_demo, e_self = jnp.exp2(s_demo - top), jnp.exp2(s_self - top)
            total = jnp.sum(e_demo, axis=1, keepdims=True) + jnp.sum(e_self, axis=1, keepdims=True)
            w_demo, w_self = e_demo.astype(BF16), e_self.astype(BF16)
            sums = jnp.zeros((rows, blk), F32)
            if b + 1 < blocks:
                q = query(b + 1)
                run = first(b + 1)
            for j in range(steps):
                for e in range(2):
                    at = 2 * j + e
                    lanes = slice(at * blk, (at + 1) * blk)
                    x = jnp.exp2(r.scr[b % 2][:, lanes] - top)
                    sums = sums + x
                    r.wts[b % 2][:, lanes] = (x * r.vs[h, at]).astype(BF16)
                if b + 1 < blocks:
                    run = score(b + 1, j, q, run)
            total = total + jnp.sum(sums, axis=1, keepdims=True)
            value = nn(r.wts[b % 2][...], r.pvb[h]) + nn(w_self, self_v)
            value = value + jnp.concatenate(
                [
                    nn(w_demo[t * group : (t + 1) * group], r.dvb[h, r.tasks[b * tq + t]])
                    for t in range(tq)
                ],
                axis=0,
            )
            lane = lax.broadcasted_iota(jnp.int32, (rows, HD), 1)
            r.ostat[h, b] = jnp.where(lane == 0, top, total).T[:STAT]
            r.oval[h, b] = value.astype(BF16).reshape(half, tz * group, HD)

            def ship(k):
                @pl.when(jnp.logical_not(is_me(b, k)))
                def _():
                    for copy in out_send(h, b, k):
                        copy.start()

            loop(half, ship)
            between(b)

    def join(h):
        def take(k):
            for copy in out_from(h, lax.rem(index + 1 + k, devices)):
                copy.wait_recv()

        loop(devices - 1, take)
        mine_b = core * SIDES + near
        stats = [r.ostat[h, mine_b]]
        for k in range(1, devices):
            stats.append(r.rstat[h, lax.rem(index + k, devices)])
        top = functools.reduce(jnp.maximum, [s[:1] for s in stats])
        factors = [jnp.exp2(s[:1] - top) for s in stats]
        total = functools.reduce(jnp.add, [s[1:2] * f for s, f in zip(stats, factors)])
        for k, f in enumerate(factors):
            r.gs[k : k + 1, :] = f / total
        r.gt[...] = r.gs[...].T
        col = r.gt[pl.ds(pl.multiple_of(far * (tz * group), 8), tz * group), :]
        value = r.oval[h, mine_b, far].astype(F32) * col[:, 0:1]
        for k in range(1, devices):
            got = r.rval[h, lax.rem(index + k, devices)].astype(F32)
            value = value + got * col[:, k : k + 1]
        r.agat[h, core, near, far] = value.astype(BF16).reshape(tz, group, HD)
        spread_out(*o_gather(h))

    def relay(h):
        pass_on(*o_gather(h), r.sh.at[h], r.rh.at[h])

    def mix(h):
        arrived(r.agat.at[h], r.sh.at[h], r.rh.at[h]).wait_recv()
        load_wo(h).wait()
        r.flat[...] = r.agat[h].reshape(qtok * group, HD).astype(F32)
        left = jnp.concatenate(
            [r.flat[pl.ds(j, qtok, stride=group), :].astype(BF16) for j in range(group)], axis=1
        )
        r.acc[...] += nn(left, r.wob[h])

    def middle(h):
        arrived(r.gat.at[h], r.sf.at[h], r.rf.at[h]).wait_recv()
        def between(b):
            if b == 1:
                @pl.when(h + 1 < kvh)
                def _():
                    stage_e(h + 1)

                @pl.when(h == kvh - 1)
                def _():
                    join(0)

        attend(h, between)

    def cached(h):
        for copy in load_cache(h):
            copy.wait()

    loop(kvh, cached)
    loop(kvh, middle)

    def tail(i):
        @pl.when(i < kvh - 1)
        def _():
            join(i + 1)

        @pl.when((i >= 2) & (i < kvh + 2))
        def _():
            relay(i - 2)

        @pl.when(i >= 3)
        def _():
            mix(i - 3)

    loop(kvh + 3, tail)
    r.out[...] = r.acc[...].astype(BF16)

    def drain(h):
        pair(h).wait_send()
        cross(h).wait_send()
        loop(half - 1, lambda i: long(h, i + 1).wait_send())
        for buf, send, recv in (q_gather(h), o_gather(h)):
            loop(chips - 1, lambda k: spreading(buf, send, recv, k + 1).wait_send())
        forward(r.gat.at[h], r.sf.at[h], r.rf.at[h]).wait_send()
        forward(r.agat.at[h], r.sh.at[h], r.rh.at[h]).wait_send()
        for b in range(blocks):
            def shipped(k):
                @pl.when(jnp.logical_not(is_me(b, k)))
                def _():
                    for copy in out_send(h, b, k):
                        copy.wait_send()

            loop(half, shipped)

    loop(kvh, drain)
    pair_kv().wait_send()
    cross_kv().wait_send()
    loop(half - 1, lambda i: long_kv(i + 1).wait_send())
    buf, send, recv = kv_gather()
    loop(chips - 1, lambda k: spreading(buf, send, recv, k + 1).wait_send())
    forward(r.gkv, r.ksf.at[0], r.krf.at[0]).wait_send()


def body(
    hidden, w_query, w_key, w_value, w_out, prefix_keys, prefix_values, key_scales, value_scales,
    demo_keys, demo_values, task_ids, demo_lengths, offsets,
):
    devices = lax.axis_size("seq")
    chips = devices // 2
    half = chips // SIDES
    qtok, depth = hidden.shape
    kvh = prefix_keys.shape[1] // HD
    group = w_query.shape[1] // HD // kvh
    tasks, demo_dev = demo_keys.shape[:2]
    pre_dev = prefix_keys.shape[0]
    tq = qtok // (2 * SIDES)
    tz = tq // half
    ku = 2 * kvh
    kuz = ku // half
    rows = tq * group
    cols = w_out.shape[1]
    cw = 4 * HD
    nch = group * HD // cw
    cfg = types.SimpleNamespace(
        kvh=kvh, group=group, half=half, devices=devices, tq=tq, tz=tz, qtok=qtok,
        blk=pre_dev // key_scales.shape[0], rows=rows, nch=nch, cw=cw, demo_dev=demo_dev,
        pre_dev=pre_dev, kuz=kuz,
    )
    smem = pl.BlockSpec(memory_space=pltpu.SMEM)
    hbm = pl.BlockSpec(memory_space=pltpu.HBM)
    ins = ["tasks", "lens", "offs", "ks", "vs"]
    ins += ["hid", "wq", "wk", "wv", "wo", "pk", "pv", "dk", "dv"]
    v = pltpu.VMEM

    def dma(*shape):
        return pltpu.SemaphoreType.DMA(shape)

    scratch = dict(
        hidb=v(hidden.shape, BF16), wkb=v(w_key.shape, BF16), wvb=v(w_value.shape, BF16),
        wqb=v((kvh * nch, depth, cw), BF16), wob=v((kvh, group * HD, cols), BF16),
        pkb=v((kvh, pre_dev, HD), BF16), pvb=v((kvh, pre_dev, HD), BF16),
        dkb=v((kvh, tasks, demo_dev, HD), BF16), dvb=v((kvh, tasks, demo_dev, HD), BF16),
        part=v((kvh, 2, SIDES, group, tq, HD), F32), recv1=v((kvh, SIDES, group, tq, HD), F32),
        own=v((kvh, group, tq, HD), F32), ysum=v((kvh, group, tq, HD), F32),
        yrecv=v((kvh, group, tq, HD), F32), zbuf=v((kvh, tq, group, HD), F32),
        zrecv=v((kvh, half - 1, tz, group, HD), F32),
        gat=v((kvh, 2, SIDES, half, tz, group, HD), BF16),
        kpart=v((2, SIDES, ku, tq, HD), F32), krecv1=v((SIDES, ku, tq, HD), F32),
        kown=v((ku, tq, HD), F32), kysum=v((ku, tq, HD), F32), kyrecv=v((ku, tq, HD), F32),
        kz=v((ku, tq, HD), F32), kzrecv=v((half - 1, kuz, tq, HD), F32),
        gkv=v((2, SIDES, half, kuz, tq, HD), BF16),
        scr0=v((rows, pre_dev), F32), scr1=v((rows, pre_dev), F32),
        wts0=v((rows, pre_dev), BF16), wts1=v((rows, pre_dev), BF16),
        dmask=v((qtok, demo_dev), F32), smask=v((qtok, qtok), F32),
        oval=v((kvh, 2 * SIDES, half, tz * group, HD), BF16),
        ostat=v((kvh, 2 * SIDES, STAT, rows), F32),
        rval=v((kvh, devices, tz * group, HD), BF16), rstat=v((kvh, devices, STAT, rows), F32),
        gs=v((HD, rows), F32), gt=v((rows, HD), F32),
        agat=v((kvh, 2, SIDES, half, tz, group, HD), BF16),
        flat=v((qtok * group, HD), F32), acc=v((qtok, cols), F32),
        s_in=dma(3), s_wq=dma(kvh * nch), s_wo=dma(kvh),
        s_pk=dma(kvh), s_pv=dma(kvh), s_dk=dma(kvh), s_dv=dma(kvh),
        s1=dma(kvh), r1=dma(kvh), sy=dma(kvh), ry=dma(kvh),
        sz=dma(kvh, half - 1), rz=dma(kvh, half - 1), sg=dma(kvh, chips), rg=dma(kvh, chips),
        sf=dma(kvh), rf=dma(kvh),
        ks1=dma(1), kr1=dma(1), ksy=dma(1), kry=dma(1), ksz=dma(half - 1), krz=dma(half - 1),
        ksg=dma(chips), krg=dma(chips), ksf=dma(1), krf=dma(1),
        so=dma(kvh, devices), ro=dma(kvh, devices), st=dma(kvh, devices), rt=dma(kvh, devices),
        sa=dma(kvh, chips), ra=dma(kvh, chips), sh=dma(kvh), rh=dma(kvh),
    )
    names = [*ins, "out", *scratch]

    def run(*refs):
        named = dict(zip(names, refs))
        named["scr"] = (named["scr0"], named["scr1"])
        named["wts"] = (named["wts0"], named["wts1"])
        kernel(cfg, list(named), *named.values())

    return pl.pallas_call(
        run,
        name="fused",
        out_shape=jax.ShapeDtypeStruct((qtok, cols), BF16),
        in_specs=[smem] * 5 + [hbm] * 9,
        out_specs=pl.BlockSpec(memory_space=pltpu.VMEM),
        scratch_shapes=list(scratch.values()),
        compiler_params=pltpu.CompilerParams(
            collective_id=0, has_side_effects=True, vmem_limit_bytes=63 << 20
        ),
    )(
        task_ids, demo_lengths, offsets, key_scales.T, value_scales.T,
        hidden, w_query, w_key, w_value, w_out,
        prefix_keys, prefix_values, demo_keys, demo_values,
    )


def solution(mesh):
    placed = (
        P("groups", "seq"),
        P("seq", None),
        P("seq", None),
        P("seq", None),
        P(None, "seq"),
        P(("groups", "seq"), None),
        P(("groups", "seq"), None),
        P(("groups", "seq"), None),
        P(("groups", "seq"), None),
        P("groups", "seq", None),
        P("groups", "seq", None),
        P("groups"),
        P("groups"),
        P("groups"),
    )
    return jax.shard_map(
        body, mesh=mesh, in_specs=placed, out_specs=P("groups", "seq"), check_vma=False
    )
```

```python
import functools
import math
import types

import jax
import jax.numpy as jnp
from jax import lax
from jax.experimental import pallas as pl
from jax.experimental.pallas import tpu as pltpu
from jax.sharding import PartitionSpec as P

HD = 128
NEG = -1e30
SIDES = 2
STAT = 8
F32 = jnp.float32
BF16 = jnp.bfloat16


def nt(a, b):
    return lax.dot_general(a, b, (((1,), (1,)), ((), ())), preferred_element_type=F32)


def nn(a, b):
    return jnp.dot(a, b, preferred_element_type=F32)


def loop(n, step):
    def wrapped(i, carry):
        step(i)
        return carry

    lax.fori_loop(0, n, wrapped, 0)


def remote(src, dst, send, recv, dev):
    return pltpu.make_async_remote_copy(
        src_ref=src,
        dst_ref=dst,
        send_sem=send,
        recv_sem=recv,
        device_id={"seq": dev},
        device_id_type=pl.DeviceIdType.MESH,
    )


def kernel(cfg, names, *refs):
    r = types.SimpleNamespace(**dict(zip(names, refs)))
    kvh, group, half, devices = cfg.kvh, cfg.group, cfg.half, cfg.devices
    tq, tz, qtok, blk, rows = cfg.tq, cfg.tz, cfg.qtok, cfg.blk, cfg.rows
    nch, cw = cfg.nch, cfg.cw
    index = lax.axis_index("seq")
    chip, core = index // 2, lax.rem(index, 2)
    far, near = chip // SIDES, lax.rem(chip, SIDES)
    const = math.log2(math.e) / math.sqrt(HD)

    def device(f, n, c):
        return (f * SIDES + n) * 2 + c

    partner = device(far, near, 1 - core)
    across = device(far, 1 - near, core)

    def up(i):
        return lax.rem(far + i, half)

    def down(i):
        return lax.rem(far - i + half, half)

    def load_wq(k):
        src = r.wq.at[:, pl.ds(pl.multiple_of(k * cw, HD), cw)]
        return pltpu.make_async_copy(src, r.wqb.at[k], r.s_wq.at[k])

    def load_wo(h):
        deep = group * HD
        src = r.wo.at[pl.ds(pl.multiple_of(h * deep, HD), deep), :]
        return pltpu.make_async_copy(src, r.wob.at[h], r.s_wo.at[h])

    def load_cache(h):
        lanes = pl.ds(pl.multiple_of(h * HD, HD), HD)
        return (
            pltpu.make_async_copy(r.pk.at[:, lanes], r.pkb.at[h], r.c_pk.at[h]),
            pltpu.make_async_copy(r.dk.at[:, :, lanes], r.dkb.at[h], r.c_dk.at[h]),
            pltpu.make_async_copy(r.pv.at[:, lanes], r.pvb.at[h], r.c_pv.at[h]),
            pltpu.make_async_copy(r.dv.at[:, :, lanes], r.dvb.at[h], r.c_dv.at[h]),
        )

    small = [
        pltpu.make_async_copy(src, dst, r.s_in.at[i])
        for i, (src, dst) in enumerate(((r.hid, r.hidb), (r.wk, r.wkb), (r.wv, r.wvb)))
    ]
    small[0].start()
    loop(nch, lambda k: load_wq(k).start())
    small[1].start()
    small[2].start()
    loop((kvh - 1) * nch, lambda k: load_wq(k + nch).start())

    barrier = pltpu.get_barrier_semaphore()

    def hello(dev):
        pl.semaphore_signal(
            barrier, inc=1, device_id={"seq": dev}, device_id_type=pl.DeviceIdType.MESH
        )

    hello(partner)
    hello(across)
    loop(half - 1, lambda k: hello(device(up(k + 1), near, core)))

    lane_d = lax.broadcasted_iota(jnp.int32, (1, cfg.demo_dev), 1)
    lane_t = lax.broadcasted_iota(jnp.int32, (1, qtok), 1)

    def spread(t, carry):
        here = lane_t == t
        return tuple(jnp.where(here, v[t], old) for v, old in zip((r.tasks, r.offs), carry))

    zero = jnp.zeros((1, qtok), jnp.int32)
    task_all, off_all = lax.fori_loop(0, qtok, spread, (zero, zero))
    mine = lax.rem(lane_t, devices) == index

    def mask(t):
        task = r.tasks[t]
        left = r.lens[task] - index * cfg.demo_dev
        r.dmask[pl.ds(t, 1), :] = jnp.where(lane_d < left, 0.0, NEG)
        keep = mine & (task_all == task) & (off_all <= r.offs[t])
        r.smask[pl.ds(t, 1), :] = jnp.where(keep, 0.0, NEG)

    loop(qtok, mask)
    r.acc[...] = jnp.zeros_like(r.acc)
    small[0].wait()

    def project(h, first, n_chunks):
        def chunk(n):
            k = h * nch + first + n
            load_wq(k).wait()
            res = nn(r.hidb[...], r.wqb[k])
            per = cw // HD
            for c in range(2):
                for s in range(SIDES):
                    at = (c * SIDES + s) * tq
                    for u in range(per):
                        to = r.part.at[h, c, s, (first + n) * per + u]
                        to[...] = res[at : at + tq, u * HD : (u + 1) * HD]

        loop(n_chunks, chunk)

    def project_kv():
        for copy in small[1:]:
            copy.wait()
        for e, w in enumerate((r.wkb, r.wvb)):
            res = nn(r.hidb[...], w[...])
            for c in range(2):
                for s in range(SIDES):
                    at = (c * SIDES + s) * tq
                    for h in range(kvh):
                        r.kpart[c, s, 2 * h + e] = res[at : at + tq, h * HD : (h + 1) * HD]

    def pair(h):
        return remote(r.part.at[h, 1 - core], r.recv1.at[h], r.s1.at[h], r.r1.at[h], partner)

    def pair_kv():
        return remote(r.kpart.at[1 - core], r.krecv1, r.ks1.at[0], r.kr1.at[0], partner)

    def cross(h):
        return remote(r.ysum.at[h], r.yrecv.at[h], r.sy.at[h], r.ry.at[h], across)

    def cross_kv():
        return remote(r.kysum, r.kyrecv, r.ksy.at[0], r.kry.at[0], across)

    def long(h, i):
        return remote(
            r.zbuf.at[h, pl.ds(up(i) * tz, tz)], r.zrecv.at[h, i - 1],
            r.sz.at[h, i - 1], r.rz.at[h, i - 1], device(up(i), near, core),
        )

    def long_kv(i):
        return remote(
            r.kz.at[pl.ds(up(i) * cfg.kuz, cfg.kuz)], r.kzrecv.at[i - 1],
            r.ksz.at[i - 1], r.krz.at[i - 1], device(up(i), near, core),
        )

    def spreading(g, i):
        piece = g.buf.at[core, near, far]
        return remote(piece, piece, g.sz.at[i], g.rz.at[i], device(up(i), near, core))

    def landing(g, i):
        piece = g.buf.at[core, near, down(i)]
        return remote(piece, piece, g.sz.at[i], g.rz.at[i], device(up(i), near, core))

    def crossing(g, n):
        return remote(g.buf.at[core, n], g.buf.at[core, n], g.sy, g.ry, across)

    def passing(g, c):
        return remote(g.buf.at[c], g.buf.at[c], g.sp, g.rp, partner)

    def gather_far(g):
        loop(half - 1, lambda i: spreading(g, i + 1).start())

    def gather_side(g):
        loop(half - 1, lambda i: landing(g, i + 1).wait_recv())
        crossing(g, near).start()

    def gather_pair(g):
        crossing(g, 1 - near).wait_recv()
        passing(g, core).start()

    def gather_end(g):
        passing(g, 1 - core).wait_recv()

    def gather_sent(g):
        loop(half - 1, lambda i: spreading(g, i + 1).wait_send())
        crossing(g, near).wait_send()
        passing(g, core).wait_send()

    def gather(buf, sems, h):
        sz, rz, sy, ry, sp, rp = sems
        return types.SimpleNamespace(
            buf=buf, sz=sz.at[h], rz=rz.at[h], sy=sy.at[h], ry=ry.at[h], sp=sp.at[h], rp=rp.at[h]
        )

    def q_gather(h):
        return gather(r.gat.at[h], (r.qsz, r.qrz, r.qsy, r.qry, r.qsp, r.qrp), h)

    def kv_gather():
        return gather(r.gkv, (r.kgsz, r.kgrz, r.kgsy, r.kgry, r.kgsp, r.kgrp), 0)

    def o_gather(h):
        return gather(r.agat.at[h], (r.asz, r.arz, r.asy, r.ary, r.asp, r.arp), h)

    def stage_b(h):
        pair(h).wait_recv()
        r.ysum[h] = r.part[h, core, 1 - near] + r.recv1[h, 1 - near]
        cross(h).start()
        r.own[h] = r.part[h, core, near] + r.recv1[h, near]

    def stage_b_kv():
        pair_kv().wait_recv()
        r.kysum[...] = r.kpart[core, 1 - near] + r.krecv1[1 - near]
        cross_kv().start()
        r.kmine[...] = r.kpart[core, near] + r.krecv1[near]

    def stage_c(h):
        cross(h).wait_recv()
        r.zbuf[h] = jnp.swapaxes(r.own[h] + r.yrecv[h], 0, 1)
        loop(half - 1, lambda i: long(h, i + 1).start())

    def stage_c_kv():
        cross_kv().wait_recv()
        r.kz[...] = r.kmine[...] + r.kyrecv[...]
        loop(half - 1, lambda i: long_kv(i + 1).start())

    def stage_d(h):
        total = r.zbuf[h, pl.ds(far * tz, tz)]
        for i in range(1, half):
            long(h, i).wait_recv()
            total = total + r.zrecv[h, i - 1]
        r.gat[h, core, near, far] = total.astype(BF16)
        gather_far(q_gather(h))

    def stage_d_kv():
        total = r.kz[pl.ds(far * cfg.kuz, cfg.kuz)]
        for i in range(1, half):
            long_kv(i).wait_recv()
            total = total + r.kzrecv[i - 1]
        r.gkv[core, near, far] = total.astype(BF16)
        gather_far(kv_gather())

    first_row = lax.broadcasted_iota(jnp.int32, (STAT, rows), 0)

    def send_pair(h):
        to = (r.s_pv.at[h], r.r_pv.at[h]), (r.s_ps.at[h], r.r_ps.at[h])
        return (
            remote(r.pval.at[h, 1 - core], r.pgot.at[h], *to[0], partner),
            remote(r.pstat.at[h, 1 - core], r.pgots.at[h], *to[1], partner),
        )

    def send_side(h):
        return (
            remote(r.yval.at[h], r.ygot.at[h], r.s_yv.at[h], r.r_yv.at[h], across),
            remote(r.ystat.at[h], r.ygots.at[h], r.s_ys.at[h], r.r_ys.at[h], across),
        )

    def send_far(h, i):
        dev = device(up(i), near, core)
        k = i - 1
        return (
            remote(
                r.zval.at[h, up(i)], r.zgot.at[h, k], r.s_zv.at[h, k], r.r_zv.at[h, k], dev
            ),
            remote(
                r.kstat.at[h], r.zgots.at[h, k], r.s_zs.at[h, k], r.r_zs.at[h, k], dev
            ),
        )

    def start(copies):
        for copy in copies:
            copy.start()

    def receive(copies):
        for copy in copies:
            copy.wait_recv()

    def sent(copies):
        for copy in copies:
            copy.wait_send()

    def join(a, a_stat, b, b_stat):
        top = jnp.maximum(a_stat[:1], b_stat[:1])
        fa, fb = jnp.exp2(a_stat[:1] - top), jnp.exp2(b_stat[:1] - top)
        stat = jnp.where(first_row == 0, top, a_stat * fa + b_stat * fb)
        col = jnp.where(first_row == 0, fa, fb).T
        return a * col[:, 0:1] + b.astype(F32) * col[:, 1:2], stat

    def merge_pair(h):
        receive(send_pair(h))

        def both(n):
            return join(r.pval[h, core, n], r.pstat[h, core, n], r.pgot[h, n], r.pgots[h, n])

        value, stat = both(1 - near)
        r.yval[h] = value.astype(BF16)
        r.ystat[h] = stat
        start(send_side(h))
        r.kval[h], r.kown[h] = both(near)

    def merge_side(h):
        receive(send_side(h))
        value, stat = join(r.kval[h], r.kown[h], r.ygot[h], r.ygots[h])
        r.zval[h] = value.astype(BF16).reshape(half, tz * group, HD)
        r.kstat[h] = stat
        loop(half - 1, lambda i: start(send_far(h, i + 1)))
        r.kval[h] = value

    def merge_far(h):
        loop(half - 1, lambda i: receive(send_far(h, i + 1)))
        stats = [r.kstat[h], *[r.zgots[h, k] for k in range(half - 1)]]
        top = functools.reduce(jnp.maximum, [s[:1] for s in stats])
        factors = [jnp.exp2(s[:1] - top) for s in stats]
        total = functools.reduce(jnp.add, [s[1:2] * f for s, f in zip(stats, factors)])
        table = jnp.zeros((STAT, rows), F32)
        for k, f in enumerate(factors):
            table = jnp.where(first_row == k, f / total, table)
        r.gt[...] = table.T
        deep = tz * group
        here = pl.ds(pl.multiple_of(far * deep, 8), deep)
        col = r.gt[here, :]
        value = r.kval[h, here, :] * col[:, 0:1]
        for k in range(1, half):
            value = value + r.zgot[h, k - 1].astype(F32) * col[:, k : k + 1]
        r.agat[h, core, near, far] = value.astype(BF16).reshape(tz, group, HD)
        gather_far(o_gather(h))

    width = 2 * blk
    steps = cfg.pre_dev // width
    blocks = 2 * SIDES

    def attend(h):
        def query(b):
            return r.gat[h, b // SIDES, b % SIDES].reshape(rows, HD)

        def self_kv(e):
            unit = 2 * h + e
            f, j = unit // cfg.kuz, lax.rem(unit, cfg.kuz)
            return jnp.concatenate(
                [r.gkv[c, s, f, j] for c in range(2) for s in range(SIDES)], axis=0
            )

        self_k, self_v = self_kv(0), self_kv(1)

        def score(b, j, q, run):
            s = nt(q, r.pkb[h, j * width : (j + 1) * width, :])
            for e in range(2):
                at = 2 * j + e
                x = s[:, e * blk : (e + 1) * blk] * (r.ks[h, at] * const)
                r.scr[b % 2][:, at * blk : (at + 1) * blk] = x
                run = jnp.maximum(run, x)
            return run

        def small_scores(b, q):
            demo, bias = [], []
            for t in range(tq):
                tok = b * tq + t
                k = r.dkb[h, r.tasks[tok]]
                s = nt(q[t * group : (t + 1) * group], k) * const
                demo.append(s + r.dmask[tok : tok + 1, :])
                bias.append(jnp.broadcast_to(r.smask[tok : tok + 1, :], (group, qtok)))
            own = nt(q, self_k) * const + jnp.concatenate(bias, axis=0)
            return jnp.concatenate(demo, axis=0), own

        def first(b):
            return jnp.full((rows, blk), NEG, F32)

        q = query(0)
        run = first(0)
        for j in range(steps):
            run = score(0, j, q, run)
        for b in range(blocks):
            s_demo, s_self = small_scores(b, q)
            top = jnp.maximum(
                jnp.max(run, axis=1, keepdims=True),
                jnp.maximum(
                    jnp.max(s_demo, axis=1, keepdims=True), jnp.max(s_self, axis=1, keepdims=True)
                ),
            )
            e_demo, e_self = jnp.exp2(s_demo - top), jnp.exp2(s_self - top)
            total = jnp.sum(e_demo, axis=1, keepdims=True) + jnp.sum(e_self, axis=1, keepdims=True)
            w_demo, w_self = e_demo.astype(BF16), e_self.astype(BF16)
            sums = jnp.zeros((rows, blk), F32)
            if b + 1 < blocks:
                q = query(b + 1)
                run = first(b + 1)
            for j in range(steps):
                for e in range(2):
                    at = 2 * j + e
                    lanes = slice(at * blk, (at + 1) * blk)
                    x = jnp.exp2(r.scr[b % 2][:, lanes] - top)
                    sums = sums + x
                    r.wts[b % 2][:, lanes] = (x * r.vs[h, at]).astype(BF16)
                if b + 1 < blocks:
                    run = score(b + 1, j, q, run)
            total = total + jnp.sum(sums, axis=1, keepdims=True)
            value = nn(r.wts[b % 2][...], r.pvb[h]) + nn(w_self, self_v)
            value = value + jnp.concatenate(
                [
                    nn(w_demo[t * group : (t + 1) * group], r.dvb[h, r.tasks[b * tq + t]])
                    for t in range(tq)
                ],
                axis=0,
            )
            lane = lax.broadcasted_iota(jnp.int32, (rows, HD), 1)
            c, n = b // SIDES, b % SIDES
            r.pstat[h, c, n] = jnp.where(lane == 0, top, total).T[:STAT]
            r.pval[h, c, n] = value

        start(send_pair(h))

    def mix(h):
        gather_end(o_gather(h))
        load_wo(h).wait()
        r.flat[...] = r.agat[h].reshape(qtok * group, HD).astype(F32)
        left = jnp.concatenate(
            [r.flat[pl.ds(j, qtok, stride=group), :].astype(BF16) for j in range(group)], axis=1
        )
        r.acc[...] += nn(left, r.wob[h])

    def cached(h):
        for copy in load_cache(h):
            copy.wait()

    def rest(h):
        for copy in load_cache(h):
            copy.start()

    def later(h):
        load_wo(h).start()

    half_way = nch // 2

    def project_start(h):
        project(h, 0, half_way)

    def project_end(h):
        project(h, half_way, nch - half_way)
        pair(h).start()

        @pl.when(h == kvh - 1)
        def _():
            loop(kvh, rest)
            loop(kvh, later)

    def ready():
        loop(kvh, cached)
        gather_end(kv_gather())

    def turn(h):
        gather_end(q_gather(h))
        attend(h)

    stages = (
        (12, merge_side, None),
        (0, project_start, None),
        (1, stage_b, stage_b_kv),
        (0, project_end, None),
        (5, stage_d, stage_d_kv),
        (9, turn, ready),
        (7, lambda h: gather_side(q_gather(h)), lambda: gather_side(kv_gather())),
        (2, stage_c, stage_c_kv),
        (14, merge_far, None),
        (8, lambda h: gather_pair(q_gather(h)), lambda: gather_pair(kv_gather())),
        (16, lambda h: gather_side(o_gather(h)), None),
        (18, mix, None),
        (10, merge_pair, None),
        (17, lambda h: gather_pair(o_gather(h)), None),
    )

    def step(at):
        i = at + 1
        for late, stage, extra in stages:
            if extra is not None:
                pl.when(i == late)(extra)
            pl.when((i >= late) & (i < late + kvh))(functools.partial(stage, i - late))

    project(0, 0, nch)
    pl.semaphore_wait(barrier, 2 + half - 1)
    pair(0).start()
    project_kv()
    pair_kv().start()
    loop(kvh + 17, step)
    r.out[...] = r.acc[...].astype(BF16)

    def drain(h):
        pair(h).wait_send()
        cross(h).wait_send()
        loop(half - 1, lambda i: long(h, i + 1).wait_send())
        gather_sent(q_gather(h))
        gather_sent(o_gather(h))
        sent(send_pair(h))
        sent(send_side(h))
        loop(half - 1, lambda i: sent(send_far(h, i + 1)))

    loop(kvh, drain)
    pair_kv().wait_send()
    cross_kv().wait_send()
    loop(half - 1, lambda i: long_kv(i + 1).wait_send())
    gather_sent(kv_gather())


def body(
    hidden, w_query, w_key, w_value, w_out, prefix_keys, prefix_values, key_scales, value_scales,
    demo_keys, demo_values, task_ids, demo_lengths, offsets,
):
    devices = lax.axis_size("seq")
    chips = devices // 2
    half = chips // SIDES
    qtok, depth = hidden.shape
    kvh = prefix_keys.shape[1] // HD
    group = w_query.shape[1] // HD // kvh
    tasks, demo_dev = demo_keys.shape[:2]
    pre_dev = prefix_keys.shape[0]
    tq = qtok // (2 * SIDES)
    tz = tq // half
    ku = 2 * kvh
    kuz = ku // half
    rows = tq * group
    cols = w_out.shape[1]
    cw = 4 * HD
    nch = group * HD // cw
    cfg = types.SimpleNamespace(
        kvh=kvh, group=group, half=half, devices=devices, tq=tq, tz=tz, qtok=qtok,
        blk=pre_dev // key_scales.shape[0], rows=rows, nch=nch, cw=cw, demo_dev=demo_dev,
        pre_dev=pre_dev, kuz=kuz,
    )
    smem = pl.BlockSpec(memory_space=pltpu.SMEM)
    hbm = pl.BlockSpec(memory_space=pltpu.HBM)
    ins = ["tasks", "lens", "offs", "ks", "vs"]
    ins += ["hid", "wq", "wk", "wv", "wo", "pk", "pv", "dk", "dv"]
    v = pltpu.VMEM

    def dma(*shape):
        return pltpu.SemaphoreType.DMA(shape)

    scratch = dict(
        hidb=v(hidden.shape, BF16), wkb=v(w_key.shape, BF16), wvb=v(w_value.shape, BF16),
        wqb=v((kvh * nch, depth, cw), BF16), wob=v((kvh, group * HD, cols), BF16),
        pkb=v((kvh, pre_dev, HD), BF16), pvb=v((kvh, pre_dev, HD), BF16),
        dkb=v((kvh, tasks, demo_dev, HD), BF16), dvb=v((kvh, tasks, demo_dev, HD), BF16),
        part=v((kvh, 2, SIDES, group, tq, HD), F32), recv1=v((kvh, SIDES, group, tq, HD), F32),
        own=v((kvh, group, tq, HD), F32), ysum=v((kvh, group, tq, HD), F32),
        yrecv=v((kvh, group, tq, HD), F32), zbuf=v((kvh, tq, group, HD), F32),
        zrecv=v((kvh, half - 1, tz, group, HD), F32),
        gat=v((kvh, 2, SIDES, half, tz, group, HD), BF16),
        kpart=v((2, SIDES, ku, tq, HD), F32), krecv1=v((SIDES, ku, tq, HD), F32),
        kmine=v((ku, tq, HD), F32), kysum=v((ku, tq, HD), F32), kyrecv=v((ku, tq, HD), F32),
        kz=v((ku, tq, HD), F32), kzrecv=v((half - 1, kuz, tq, HD), F32),
        gkv=v((2, SIDES, half, kuz, tq, HD), BF16),
        scr0=v((rows, pre_dev), F32), scr1=v((rows, pre_dev), F32),
        wts0=v((rows, pre_dev), BF16), wts1=v((rows, pre_dev), BF16),
        dmask=v((qtok, demo_dev), F32), smask=v((qtok, qtok), F32),
        pval=v((kvh, 2, SIDES, rows, HD), F32), pstat=v((kvh, 2, SIDES, STAT, rows), F32),
        pgot=v((kvh, SIDES, rows, HD), F32), pgots=v((kvh, SIDES, STAT, rows), F32),
        yval=v((kvh, rows, HD), BF16), ystat=v((kvh, STAT, rows), F32),
        ygot=v((kvh, rows, HD), BF16), ygots=v((kvh, STAT, rows), F32),
        kval=v((kvh, rows, HD), F32), kown=v((kvh, STAT, rows), F32),
        kstat=v((kvh, STAT, rows), F32), zval=v((kvh, half, tz * group, HD), BF16),
        zgot=v((kvh, half - 1, tz * group, HD), BF16), zgots=v((kvh, half - 1, STAT, rows), F32),
        gt=v((rows, STAT), F32),
        agat=v((kvh, 2, SIDES, half, tz, group, HD), BF16),
        flat=v((qtok * group, HD), F32), acc=v((qtok, cols), F32),
        s_in=dma(3), s_wq=dma(kvh * nch), s_wo=dma(kvh),
        c_pk=dma(kvh), c_pv=dma(kvh), c_dk=dma(kvh), c_dv=dma(kvh),
        s1=dma(kvh), r1=dma(kvh), sy=dma(kvh), ry=dma(kvh),
        sz=dma(kvh, half - 1), rz=dma(kvh, half - 1),
        ks1=dma(1), kr1=dma(1), ksy=dma(1), kry=dma(1), ksz=dma(half - 1), krz=dma(half - 1),
        **{
            f"{g}{d}{e}": dma(n, half) if e == "z" else dma(n)
            for g, n in (("q", kvh), ("kg", 1), ("a", kvh))
            for d in "sr"
            for e in "zyp"
        },
        **{f"{d}_{e}": dma(kvh) for d in "sr" for e in ("pv", "ps", "yv", "ys")},
        **{f"{d}_{e}": dma(kvh, half - 1) for d in "sr" for e in ("zv", "zs")},
    )
    names = [*ins, "out", *scratch]

    def run(*refs):
        named = dict(zip(names, refs))
        named["scr"] = (named["scr0"], named["scr1"])
        named["wts"] = (named["wts0"], named["wts1"])
        kernel(cfg, list(named), *named.values())

    return pl.pallas_call(
        run,
        name="fused",
        out_shape=jax.ShapeDtypeStruct((qtok, cols), BF16),
        in_specs=[smem] * 5 + [hbm] * 9,
        out_specs=pl.BlockSpec(memory_space=pltpu.VMEM),
        scratch_shapes=list(scratch.values()),
        compiler_params=pltpu.CompilerParams(
            collective_id=0, has_side_effects=True, vmem_limit_bytes=63 << 20
        ),
    )(
        task_ids, demo_lengths, offsets, key_scales.T, value_scales.T,
        hidden, w_query, w_key, w_value, w_out,
        prefix_keys, prefix_values, demo_keys, demo_values,
    )


def solution(mesh):
    placed = (
        P("groups", "seq"),
        P("seq", None),
        P("seq", None),
        P("seq", None),
        P(None, "seq"),
        P(("groups", "seq"), None),
        P(("groups", "seq"), None),
        P(("groups", "seq"), None),
        P(("groups", "seq"), None),
        P("groups", "seq", None),
        P("groups", "seq", None),
        P("groups"),
        P("groups"),
        P("groups"),
    )
    return jax.shard_map(
        body, mesh=mesh, in_specs=placed, out_specs=P("groups", "seq"), check_vma=False
    )
```

```python
import functools
import math
import types

import jax
import jax.numpy as jnp
from jax import lax
from jax.experimental import pallas as pl
from jax.experimental.pallas import tpu as pltpu
from jax.sharding import PartitionSpec as P

HD = 128
NEG = -1e30
SIDES = 2
STAT = 8
F32 = jnp.float32
BF16 = jnp.bfloat16


def nt(a, b):
    return lax.dot_general(a, b, (((1,), (1,)), ((), ())), preferred_element_type=F32)


def nn(a, b):
    return jnp.dot(a, b, preferred_element_type=F32)


def loop(n, step):
    def wrapped(i, carry):
        step(i)
        return carry

    lax.fori_loop(0, n, wrapped, 0)


def remote(src, dst, send, recv, dev):
    return pltpu.make_async_remote_copy(
        src_ref=src,
        dst_ref=dst,
        send_sem=send,
        recv_sem=recv,
        device_id={"seq": dev},
        device_id_type=pl.DeviceIdType.MESH,
    )


def kernel(cfg, names, *refs):
    r = types.SimpleNamespace(**dict(zip(names, refs)))
    kvh, group, half, devices = cfg.kvh, cfg.group, cfg.half, cfg.devices
    tq, tz, qtok, blk, rows = cfg.tq, cfg.tz, cfg.qtok, cfg.blk, cfg.rows
    nch, cw = cfg.nch, cfg.cw
    index = lax.axis_index("seq")
    chip, core = index // 2, lax.rem(index, 2)
    far, near = chip // SIDES, lax.rem(chip, SIDES)
    const = math.log2(math.e) / math.sqrt(HD)

    def device(f, n, c):
        return (f * SIDES + n) * 2 + c

    partner = device(far, near, 1 - core)
    across = device(far, 1 - near, core)

    def up(i):
        return lax.rem(far + i, half)

    def down(i):
        return lax.rem(far - i + half, half)

    def load_wq(k):
        src = r.wq.at[:, pl.ds(pl.multiple_of(k * cw, HD), cw)]
        return pltpu.make_async_copy(src, r.wqb.at[k], r.s_wq.at[k])

    def load_wo(h):
        deep = group * HD
        src = r.wo.at[pl.ds(pl.multiple_of(h * deep, HD), deep), :]
        return pltpu.make_async_copy(src, r.wob.at[h], r.s_wo.at[h])

    def load_cache(h):
        lanes = pl.ds(pl.multiple_of(h * HD, HD), HD)
        return (
            pltpu.make_async_copy(r.pk.at[:, lanes], r.pkb.at[h], r.c_pk.at[h]),
            pltpu.make_async_copy(r.dk.at[:, :, lanes], r.dkb.at[h], r.c_dk.at[h]),
            pltpu.make_async_copy(r.pv.at[:, lanes], r.pvb.at[h], r.c_pv.at[h]),
            pltpu.make_async_copy(r.dv.at[:, :, lanes], r.dvb.at[h], r.c_dv.at[h]),
        )

    small = [
        pltpu.make_async_copy(src, dst, r.s_in.at[i])
        for i, (src, dst) in enumerate(((r.hid, r.hidb), (r.wk, r.wkb), (r.wv, r.wvb)))
    ]
    small[0].start()
    loop(nch, lambda k: load_wq(k).start())
    small[1].start()
    small[2].start()
    loop((kvh - 1) * nch, lambda k: load_wq(k + nch).start())

    barrier = pltpu.get_barrier_semaphore()

    def hello(dev):
        pl.semaphore_signal(
            barrier, inc=1, device_id={"seq": dev}, device_id_type=pl.DeviceIdType.MESH
        )

    hello(partner)
    chips = SIDES * half

    def side(k):
        return lax.rem(near + lax.rem(k, 2), 2)

    def chip_at(k):
        return device(up(k // 2), side(k), core)

    def chip_from(k):
        return down(k // 2), side(k)

    loop(chips - 1, lambda k: hello(chip_at(k + 1)))

    lane_d = lax.broadcasted_iota(jnp.int32, (1, cfg.demo_dev), 1)
    lane_t = lax.broadcasted_iota(jnp.int32, (1, qtok), 1)

    def spread(t, carry):
        here = lane_t == t
        return tuple(jnp.where(here, v[t], old) for v, old in zip((r.tasks, r.offs), carry))

    zero = jnp.zeros((1, qtok), jnp.int32)
    task_all, off_all = lax.fori_loop(0, qtok, spread, (zero, zero))
    mine = lax.rem(lane_t, devices) == index

    def mask(t):
        task = r.tasks[t]
        left = r.lens[task] - index * cfg.demo_dev
        r.dmask[pl.ds(t, 1), :] = jnp.where(lane_d < left, 0.0, NEG)
        keep = mine & (task_all == task) & (off_all <= r.offs[t])
        r.smask[pl.ds(t, 1), :] = jnp.where(keep, 0.0, NEG)

    loop(qtok, mask)
    r.acc[...] = jnp.zeros_like(r.acc)
    small[0].wait()

    def project(h):
        def chunk(n):
            k = h * nch + n
            load_wq(k).wait()
            res = nn(r.hidb[...], r.wqb[k])
            per = cw // HD
            for c in range(2):
                for s in range(SIDES):
                    at = (c * SIDES + s) * tq
                    for u in range(per):
                        r.part[h, c, s, n * per + u] = res[at : at + tq, u * HD : (u + 1) * HD]

        loop(nch, chunk)

    def project_kv():
        for copy in small[1:]:
            copy.wait()
        for e, w in enumerate((r.wkb, r.wvb)):
            res = nn(r.hidb[...], w[...])
            for c in range(2):
                for s in range(SIDES):
                    at = (c * SIDES + s) * tq
                    for h in range(kvh):
                        r.kpart[c, s, 2 * h + e] = res[at : at + tq, h * HD : (h + 1) * HD]

    def pair(h):
        return remote(r.part.at[h, 1 - core], r.recv1.at[h], r.s1.at[h], r.r1.at[h], partner)

    def pair_kv():
        return remote(r.kpart.at[1 - core], r.krecv1, r.ks1.at[0], r.kr1.at[0], partner)

    def cross(h):
        return remote(r.ysum.at[h], r.yrecv.at[h], r.sy.at[h], r.ry.at[h], across)

    def cross_kv():
        return remote(r.kysum, r.kyrecv, r.ksy.at[0], r.kry.at[0], across)

    def long(h, i):
        return remote(
            r.zbuf.at[h, pl.ds(up(i) * tz, tz)], r.zrecv.at[h, i - 1],
            r.sz.at[h, i - 1], r.rz.at[h, i - 1], device(up(i), near, core),
        )

    def long_kv(i):
        return remote(
            r.kz.at[pl.ds(up(i) * cfg.kuz, cfg.kuz)], r.kzrecv.at[i - 1],
            r.ksz.at[i - 1], r.krz.at[i - 1], device(up(i), near, core),
        )

    def spreading(buf, send, recv, k):
        piece = buf.at[core, near, far]
        return remote(piece, piece, send.at[k], recv.at[k], chip_at(k))

    def landing(buf, send, recv, k):
        piece = buf.at[core, side(k), down(k // 2)]
        return remote(piece, piece, send.at[k], recv.at[k], chip_at(k))

    def forward(buf, send, recv):
        return remote(buf.at[core], buf.at[core], send, recv, partner)

    def arrived(buf, send, recv):
        return remote(buf.at[1 - core], buf.at[1 - core], send, recv, partner)

    def spread_out(buf, send, recv):
        loop(chips - 1, lambda k: spreading(buf, send, recv, k + 1).start())

    def pass_on(buf, send, recv, fsend, frecv):
        loop(chips - 1, lambda k: landing(buf, send, recv, k + 1).wait_recv())
        forward(buf, fsend, frecv).start()

    def q_gather(h):
        return r.gat.at[h], r.sg.at[h], r.rg.at[h]

    def kv_gather():
        return r.gkv, r.ksg, r.krg

    def o_gather(h):
        return r.agat.at[h], r.sa.at[h], r.ra.at[h]

    def stage_b(h):
        pair(h).wait_recv()
        r.ysum[h] = r.part[h, core, 1 - near] + r.recv1[h, 1 - near]
        cross(h).start()
        r.own[h] = r.part[h, core, near] + r.recv1[h, near]

    def stage_b_kv():
        pair_kv().wait_recv()
        r.kysum[...] = r.kpart[core, 1 - near] + r.krecv1[1 - near]
        cross_kv().start()
        r.kown[...] = r.kpart[core, near] + r.krecv1[near]

    def stage_c(h):
        cross(h).wait_recv()
        r.zbuf[h] = jnp.swapaxes(r.own[h] + r.yrecv[h], 0, 1)
        loop(half - 1, lambda i: long(h, i + 1).start())

    def stage_c_kv():
        cross_kv().wait_recv()
        r.kz[...] = r.kown[...] + r.kyrecv[...]
        loop(half - 1, lambda i: long_kv(i + 1).start())

    def stage_d(h):
        total = r.zbuf[h, pl.ds(far * tz, tz)]
        for i in range(1, half):
            long(h, i).wait_recv()
            total = total + r.zrecv[h, i - 1]
        r.gat[h, core, near, far] = total.astype(BF16)
        spread_out(*q_gather(h))

    def stage_d_kv():
        total = r.kz[pl.ds(far * cfg.kuz, cfg.kuz)]
        for i in range(1, half):
            long_kv(i).wait_recv()
            total = total + r.kzrecv[i - 1]
        r.gkv[core, near, far] = total.astype(BF16)
        spread_out(*kv_gather())

    def stage_e(h):
        pass_on(*q_gather(h), r.sf.at[h], r.rf.at[h])

    def front(i):
        @pl.when(i < kvh)
        def _():
            project(i)
            pair(i).start()

        @pl.when(i < kvh + 1)
        def _():
            stage_b(i - 1)

        @pl.when(i == 1)
        def _():
            stage_b_kv()

        @pl.when((i >= 3) & (i < kvh + 3))
        def _():
            stage_c(i - 3)

        @pl.when(i == 3)
        def _():
            stage_c_kv()

            def caches(h):
                for copy in load_cache(h):
                    copy.start()

            loop(kvh, caches)
            loop(kvh, lambda h: load_wo(h).start())

        @pl.when(i >= 5)
        def _():
            stage_d(i - 5)

        @pl.when(i == 5)
        def _():
            stage_d_kv()

    project(0)
    pl.semaphore_wait(barrier, chips)
    pair(0).start()
    project_kv()
    pair_kv().start()
    loop(kvh + 4, lambda i: front(i + 1))
    stage_e(0)
    pass_on(*kv_gather(), r.ksf.at[0], r.krf.at[0])
    arrived(r.gkv, r.ksf.at[0], r.krf.at[0]).wait_recv()

    first_row = lax.broadcasted_iota(jnp.int32, (STAT, rows), 0) == 0
    deep = tz * group

    def send_pair(h):
        return (
            remote(
                r.pval.at[h, 1 - core], r.pgot.at[h], r.s_pv.at[h], r.r_pv.at[h], partner
            ),
            remote(
                r.pstat.at[h, 1 - core], r.pgots.at[h], r.s_ps.at[h], r.r_ps.at[h], partner
            ),
        )

    def send_own(h, k):
        return (
            remote(
                r.oval.at[h, side(k), up(k // 2)], r.ogot.at[h, k],
                r.s_ov.at[h, k], r.r_ov.at[h, k], chip_at(k),
            ),
            remote(
                r.ostat.at[h, side(k)], r.ogots.at[h, k],
                r.s_os.at[h, k], r.r_os.at[h, k], chip_at(k),
            ),
        )

    def start(copies):
        for copy in copies:
            copy.start()

    def receive(copies):
        for copy in copies:
            copy.wait_recv()

    def sent(copies):
        for copy in copies:
            copy.wait_send()

    def merge_pair(h):
        receive(send_pair(h))
        for n in range(SIDES):
            a, b = r.pstat[h, core, n], r.pgots[h, n]
            top = jnp.maximum(a[:1], b[:1])
            fa, fb = jnp.exp2(a[:1] - top), jnp.exp2(b[:1] - top)
            stat = jnp.where(first_row, top, a * fa + b * fb)
            col = jnp.where(first_row, fa, fb).T
            value = r.pval[h, core, n] * col[:, 0:1] + r.pgot[h, n] * col[:, 1:2]
            r.oval[h, n] = value.astype(BF16).reshape(half, deep, HD)
            r.ostat[h, n] = stat[:2]
        loop(chips - 1, lambda k: start(send_own(h, k + 1)))

    def merge_own(h):
        loop(chips - 1, lambda k: receive(send_own(h, k + 1)))
        stats = [r.ostat[h, near], *[r.ogots[h, k] for k in range(1, chips)]]
        top = functools.reduce(jnp.maximum, [s[:1] for s in stats])
        factors = [jnp.exp2(s[:1] - top) for s in stats]
        total = functools.reduce(jnp.add, [s[1:2] * f for s, f in zip(stats, factors)])
        depth = r.gt.shape[1]
        row = lax.broadcasted_iota(jnp.int32, (depth, rows), 0)
        table = jnp.zeros((depth, rows), F32)
        for k, f in enumerate(factors):
            table = jnp.where(row == k, f / total, table)
        r.gt[...] = table.T
        col = r.gt[pl.ds(pl.multiple_of(far * deep, 8), deep), :]
        value = r.oval[h, near, far].astype(F32) * col[:, 0:1]
        for k in range(1, chips):
            value = value + r.ogot[h, k].astype(F32) * col[:, k : k + 1]
        r.agat[h, core, near, far] = value.astype(BF16).reshape(tz, group, HD)
        spread_out(*o_gather(h))

    width = 2 * blk
    steps = cfg.pre_dev // width
    blocks = 2 * SIDES

    def attend(h, between):
        def query(b):
            return r.gat[h, b // SIDES, b % SIDES].reshape(rows, HD)

        def self_kv(e):
            unit = 2 * h + e
            f, j = unit // cfg.kuz, lax.rem(unit, cfg.kuz)
            return jnp.concatenate(
                [r.gkv[c, s, f, j] for c in range(2) for s in range(SIDES)], axis=0
            )

        self_k, self_v = self_kv(0), self_kv(1)

        def score(b, j, q, run):
            s = nt(q, r.pkb[h, j * width : (j + 1) * width, :])
            for e in range(2):
                at = 2 * j + e
                x = s[:, e * blk : (e + 1) * blk] * (r.ks[h, at] * const)
                r.scr[b % 2][:, at * blk : (at + 1) * blk] = x
                run = jnp.maximum(run, x)
            return run

        def small_scores(b, q):
            demo, bias = [], []
            for t in range(tq):
                tok = b * tq + t
                k = r.dkb[h, r.tasks[tok]]
                s = nt(q[t * group : (t + 1) * group], k) * const
                demo.append(s + r.dmask[tok : tok + 1, :])
                bias.append(jnp.broadcast_to(r.smask[tok : tok + 1, :], (group, qtok)))
            own = nt(q, self_k) * const + jnp.concatenate(bias, axis=0)
            return jnp.concatenate(demo, axis=0), own

        def first(b):
            return jnp.full((rows, blk), NEG, F32)

        q = query(0)
        run = first(0)
        for j in range(steps):
            run = score(0, j, q, run)
        for b in range(blocks):
            s_demo, s_self = small_scores(b, q)
            top = jnp.maximum(
                jnp.max(run, axis=1, keepdims=True),
                jnp.maximum(
                    jnp.max(s_demo, axis=1, keepdims=True), jnp.max(s_self, axis=1, keepdims=True)
                ),
            )
            e_demo, e_self = jnp.exp2(s_demo - top), jnp.exp2(s_self - top)
            total = jnp.sum(e_demo, axis=1, keepdims=True) + jnp.sum(e_self, axis=1, keepdims=True)
            w_demo, w_self = e_demo.astype(BF16), e_self.astype(BF16)
            sums = jnp.zeros((rows, blk), F32)
            if b + 1 < blocks:
                q = query(b + 1)
                run = first(b + 1)
            for j in range(steps):
                for e in range(2):
                    at = 2 * j + e
                    lanes = slice(at * blk, (at + 1) * blk)
                    x = jnp.exp2(r.scr[b % 2][:, lanes] - top)
                    sums = sums + x
                    r.wts[b % 2][:, lanes] = (x * r.vs[h, at]).astype(BF16)
                if b + 1 < blocks:
                    run = score(b + 1, j, q, run)
            total = total + jnp.sum(sums, axis=1, keepdims=True)
            value = nn(r.wts[b % 2][...], r.pvb[h]) + nn(w_self, self_v)
            value = value + jnp.concatenate(
                [
                    nn(w_demo[t * group : (t + 1) * group], r.dvb[h, r.tasks[b * tq + t]])
                    for t in range(tq)
                ],
                axis=0,
            )
            lane = lax.broadcasted_iota(jnp.int32, (rows, HD), 1)
            c, n = b // SIDES, b % SIDES
            r.pstat[h, c, n] = jnp.where(lane == 0, top, total).T[:STAT]
            r.pval[h, c, n] = value
            between(b)

        start(send_pair(h))

    def relay(h):
        pass_on(*o_gather(h), r.sh.at[h], r.rh.at[h])

    def mix(h):
        arrived(r.agat.at[h], r.sh.at[h], r.rh.at[h]).wait_recv()
        load_wo(h).wait()
        r.flat[...] = r.agat[h].reshape(qtok * group, HD).astype(F32)
        left = jnp.concatenate(
            [r.flat[pl.ds(j, qtok, stride=group), :].astype(BF16) for j in range(group)], axis=1
        )
        r.acc[...] += nn(left, r.wob[h])

    def middle(h):
        arrived(r.gat.at[h], r.sf.at[h], r.rf.at[h]).wait_recv()
        def between(b):
            if b == 0:
                @pl.when(h > 0)
                def _():
                    merge_pair(h - 1)

            if b == 1:
                @pl.when(h + 1 < kvh)
                def _():
                    stage_e(h + 1)

            if b == 2:
                @pl.when(h == kvh - 1)
                def _():
                    merge_own(0)

        attend(h, between)

    def cached(h):
        for copy in load_cache(h):
            copy.wait()

    loop(kvh, cached)
    loop(kvh, middle)
    merge_pair(kvh - 1)

    def tail(i):
        @pl.when((i >= 2) & (i < kvh))
        def _():
            merge_own(i - 1)

        @pl.when((i >= 3) & (i < kvh + 3))
        def _():
            relay(i - 3)

        @pl.when(i == 3)
        def _():
            merge_own(kvh - 1)

        @pl.when(i >= 4)
        def _():
            mix(i - 4)

    loop(kvh + 4, tail)
    r.out[...] = r.acc[...].astype(BF16)

    def drain(h):
        pair(h).wait_send()
        cross(h).wait_send()
        loop(half - 1, lambda i: long(h, i + 1).wait_send())
        for buf, send, recv in (q_gather(h), o_gather(h)):
            loop(chips - 1, lambda k: spreading(buf, send, recv, k + 1).wait_send())
        forward(r.gat.at[h], r.sf.at[h], r.rf.at[h]).wait_send()
        forward(r.agat.at[h], r.sh.at[h], r.rh.at[h]).wait_send()
        sent(send_pair(h))
        loop(chips - 1, lambda k: sent(send_own(h, k + 1)))

    loop(kvh, drain)
    pair_kv().wait_send()
    cross_kv().wait_send()
    loop(half - 1, lambda i: long_kv(i + 1).wait_send())
    buf, send, recv = kv_gather()
    loop(chips - 1, lambda k: spreading(buf, send, recv, k + 1).wait_send())
    forward(r.gkv, r.ksf.at[0], r.krf.at[0]).wait_send()


def body(
    hidden, w_query, w_key, w_value, w_out, prefix_keys, prefix_values, key_scales, value_scales,
    demo_keys, demo_values, task_ids, demo_lengths, offsets,
):
    devices = lax.axis_size("seq")
    chips = devices // 2
    half = chips // SIDES
    qtok, depth = hidden.shape
    kvh = prefix_keys.shape[1] // HD
    group = w_query.shape[1] // HD // kvh
    tasks, demo_dev = demo_keys.shape[:2]
    pre_dev = prefix_keys.shape[0]
    tq = qtok // (2 * SIDES)
    tz = tq // half
    ku = 2 * kvh
    kuz = ku // half
    rows = tq * group
    cols = w_out.shape[1]
    cw = 4 * HD
    nch = group * HD // cw
    cfg = types.SimpleNamespace(
        kvh=kvh, group=group, half=half, devices=devices, tq=tq, tz=tz, qtok=qtok,
        blk=pre_dev // key_scales.shape[0], rows=rows, nch=nch, cw=cw, demo_dev=demo_dev,
        pre_dev=pre_dev, kuz=kuz,
    )
    smem = pl.BlockSpec(memory_space=pltpu.SMEM)
    hbm = pl.BlockSpec(memory_space=pltpu.HBM)
    ins = ["tasks", "lens", "offs", "ks", "vs"]
    ins += ["hid", "wq", "wk", "wv", "wo", "pk", "pv", "dk", "dv"]
    v = pltpu.VMEM

    def dma(*shape):
        return pltpu.SemaphoreType.DMA(shape)

    scratch = dict(
        hidb=v(hidden.shape, BF16), wkb=v(w_key.shape, BF16), wvb=v(w_value.shape, BF16),
        wqb=v((kvh * nch, depth, cw), BF16), wob=v((kvh, group * HD, cols), BF16),
        pkb=v((kvh, pre_dev, HD), BF16), pvb=v((kvh, pre_dev, HD), BF16),
        dkb=v((kvh, tasks, demo_dev, HD), BF16), dvb=v((kvh, tasks, demo_dev, HD), BF16),
        part=v((kvh, 2, SIDES, group, tq, HD), F32), recv1=v((kvh, SIDES, group, tq, HD), F32),
        own=v((kvh, group, tq, HD), F32), ysum=v((kvh, group, tq, HD), F32),
        yrecv=v((kvh, group, tq, HD), F32), zbuf=v((kvh, tq, group, HD), F32),
        zrecv=v((kvh, half - 1, tz, group, HD), F32),
        gat=v((kvh, 2, SIDES, half, tz, group, HD), BF16),
        kpart=v((2, SIDES, ku, tq, HD), F32), krecv1=v((SIDES, ku, tq, HD), F32),
        kown=v((ku, tq, HD), F32), kysum=v((ku, tq, HD), F32), kyrecv=v((ku, tq, HD), F32),
        kz=v((ku, tq, HD), F32), kzrecv=v((half - 1, kuz, tq, HD), F32),
        gkv=v((2, SIDES, half, kuz, tq, HD), BF16),
        scr0=v((rows, pre_dev), F32), scr1=v((rows, pre_dev), F32),
        wts0=v((rows, pre_dev), BF16), wts1=v((rows, pre_dev), BF16),
        dmask=v((qtok, demo_dev), F32), smask=v((qtok, qtok), F32),
        pval=v((kvh, 2, SIDES, rows, HD), F32), pstat=v((kvh, 2, SIDES, STAT, rows), F32),
        pgot=v((kvh, SIDES, rows, HD), F32), pgots=v((kvh, SIDES, STAT, rows), F32),
        oval=v((kvh, SIDES, half, tz * group, HD), BF16), ostat=v((kvh, SIDES, 2, rows), F32),
        ogot=v((kvh, chips, tz * group, HD), BF16), ogots=v((kvh, chips, 2, rows), F32),
        gt=v((rows, max(STAT, chips)), F32),
        agat=v((kvh, 2, SIDES, half, tz, group, HD), BF16),
        flat=v((qtok * group, HD), F32), acc=v((qtok, cols), F32),
        s_in=dma(3), s_wq=dma(kvh * nch), s_wo=dma(kvh),
        c_pk=dma(kvh), c_pv=dma(kvh), c_dk=dma(kvh), c_dv=dma(kvh),
        s1=dma(kvh), r1=dma(kvh), sy=dma(kvh), ry=dma(kvh),
        sz=dma(kvh, half - 1), rz=dma(kvh, half - 1), sg=dma(kvh, chips), rg=dma(kvh, chips),
        sf=dma(kvh), rf=dma(kvh),
        ks1=dma(1), kr1=dma(1), ksy=dma(1), kry=dma(1), ksz=dma(half - 1), krz=dma(half - 1),
        ksg=dma(chips), krg=dma(chips), ksf=dma(1), krf=dma(1),
        **{f"{d}_{e}": dma(kvh) for d in "sr" for e in ("pv", "ps")},
        **{f"{d}_{e}": dma(kvh, chips) for d in "sr" for e in ("ov", "os")},
        sa=dma(kvh, chips), ra=dma(kvh, chips), sh=dma(kvh), rh=dma(kvh),
    )
    names = [*ins, "out", *scratch]

    def run(*refs):
        named = dict(zip(names, refs))
        named["scr"] = (named["scr0"], named["scr1"])
        named["wts"] = (named["wts0"], named["wts1"])
        kernel(cfg, list(named), *named.values())

    return pl.pallas_call(
        run,
        name="fused",
        out_shape=jax.ShapeDtypeStruct((qtok, cols), BF16),
        in_specs=[smem] * 5 + [hbm] * 9,
        out_specs=pl.BlockSpec(memory_space=pltpu.VMEM),
        scratch_shapes=list(scratch.values()),
        compiler_params=pltpu.CompilerParams(
            collective_id=0, has_side_effects=True, vmem_limit_bytes=63 << 20
        ),
    )(
        task_ids, demo_lengths, offsets, key_scales.T, value_scales.T,
        hidden, w_query, w_key, w_value, w_out,
        prefix_keys, prefix_values, demo_keys, demo_values,
    )


def solution(mesh):
    placed = (
        P("groups", "seq"),
        P("seq", None),
        P("seq", None),
        P("seq", None),
        P(None, "seq"),
        P(("groups", "seq"), None),
        P(("groups", "seq"), None),
        P(("groups", "seq"), None),
        P(("groups", "seq"), None),
        P("groups", "seq", None),
        P("groups", "seq", None),
        P("groups"),
        P("groups"),
        P("groups"),
    )
    return jax.shard_map(
        body, mesh=mesh, in_specs=placed, out_specs=P("groups", "seq"), check_vma=False
    )
```

```python
import functools
import math
import types

import jax
import jax.numpy as jnp
from jax import lax
from jax.experimental import pallas as pl
from jax.experimental.pallas import tpu as pltpu
from jax.sharding import PartitionSpec as P

HD = 128
NEG = -1e30
SIDES = 2
STAT = 8
F32 = jnp.float32
BF16 = jnp.bfloat16


def nt(a, b):
    return lax.dot_general(a, b, (((1,), (1,)), ((), ())), preferred_element_type=F32)


def nn(a, b):
    return jnp.dot(a, b, preferred_element_type=F32)


def loop(n, step):
    def wrapped(i, carry):
        step(i)
        return carry

    lax.fori_loop(0, n, wrapped, 0)


def remote(src, dst, send, recv, dev):
    return pltpu.make_async_remote_copy(
        src_ref=src,
        dst_ref=dst,
        send_sem=send,
        recv_sem=recv,
        device_id={"seq": dev},
        device_id_type=pl.DeviceIdType.MESH,
    )


def kernel(cfg, names, *refs):
    r = types.SimpleNamespace(**dict(zip(names, refs)))
    kvh, group, half, devices = cfg.kvh, cfg.group, cfg.half, cfg.devices
    tq, tz, qtok, blk, rows = cfg.tq, cfg.tz, cfg.qtok, cfg.blk, cfg.rows
    nch, cw = cfg.nch, cfg.cw
    index = lax.axis_index("seq")
    chip, core = index // 2, lax.rem(index, 2)
    far, near = chip // SIDES, lax.rem(chip, SIDES)
    const = math.log2(math.e) / math.sqrt(HD)

    def device(f, n, c):
        return (f * SIDES + n) * 2 + c

    partner = device(far, near, 1 - core)
    across = device(far, 1 - near, core)

    def up(i):
        return lax.rem(far + i, half)

    def down(i):
        return lax.rem(far - i + half, half)

    def load_wq(k):
        src = r.wq.at[:, pl.ds(pl.multiple_of(k * cw, HD), cw)]
        return pltpu.make_async_copy(src, r.wqb.at[k], r.s_wq.at[k])

    def load_wo(h):
        deep = group * HD
        src = r.wo.at[pl.ds(pl.multiple_of(h * deep, HD), deep), :]
        return pltpu.make_async_copy(src, r.wob.at[h], r.s_wo.at[h])

    def load_cache(h):
        lanes = pl.ds(pl.multiple_of(h * HD, HD), HD)
        return (
            pltpu.make_async_copy(r.pk.at[:, lanes], r.pkb.at[h], r.c_pk.at[h]),
            pltpu.make_async_copy(r.dk.at[:, :, lanes], r.dkb.at[h], r.c_dk.at[h]),
            pltpu.make_async_copy(r.pv.at[:, lanes], r.pvb.at[h], r.c_pv.at[h]),
            pltpu.make_async_copy(r.dv.at[:, :, lanes], r.dvb.at[h], r.c_dv.at[h]),
        )

    small = [
        pltpu.make_async_copy(src, dst, r.s_in.at[i])
        for i, (src, dst) in enumerate(((r.hid, r.hidb), (r.wk, r.wkb), (r.wv, r.wvb)))
    ]
    small[0].start()
    loop(nch, lambda k: load_wq(k).start())
    small[1].start()
    small[2].start()
    loop((kvh - 1) * nch, lambda k: load_wq(k + nch).start())

    barrier = pltpu.get_barrier_semaphore()

    def hello(dev):
        pl.semaphore_signal(
            barrier, inc=1, device_id={"seq": dev}, device_id_type=pl.DeviceIdType.MESH
        )

    hello(partner)
    chips = SIDES * half

    def side(k):
        return lax.rem(near + lax.rem(k, 2), 2)

    def chip_at(k):
        return device(up(k // 2), side(k), core)

    def chip_from(k):
        return down(k // 2), side(k)

    loop(chips - 1, lambda k: hello(chip_at(k + 1)))

    lane_d = lax.broadcasted_iota(jnp.int32, (1, cfg.demo_dev), 1)
    lane_t = lax.broadcasted_iota(jnp.int32, (1, qtok), 1)

    def spread(t, carry):
        here = lane_t == t
        return tuple(jnp.where(here, v[t], old) for v, old in zip((r.tasks, r.offs), carry))

    zero = jnp.zeros((1, qtok), jnp.int32)
    task_all, off_all = lax.fori_loop(0, qtok, spread, (zero, zero))
    mine = lax.rem(lane_t, devices) == index

    def mask(t):
        task = r.tasks[t]
        left = r.lens[task] - index * cfg.demo_dev
        r.dmask[pl.ds(t, 1), :] = jnp.where(lane_d < left, 0.0, NEG)
        keep = mine & (task_all == task) & (off_all <= r.offs[t])
        r.smask[pl.ds(t, 1), :] = jnp.where(keep, 0.0, NEG)

    loop(qtok, mask)
    r.acc[...] = jnp.zeros_like(r.acc)
    small[0].wait()

    def project(h):
        def chunk(n):
            k = h * nch + n
            load_wq(k).wait()
            res = nn(r.hidb[...], r.wqb[k])
            per = cw // HD
            for c in range(2):
                for s in range(SIDES):
                    at = (c * SIDES + s) * tq
                    for u in range(per):
                        r.part[h, c, s, n * per + u] = res[at : at + tq, u * HD : (u + 1) * HD]

        loop(nch, chunk)

    def project_kv():
        for copy in small[1:]:
            copy.wait()
        for e, w in enumerate((r.wkb, r.wvb)):
            res = nn(r.hidb[...], w[...])
            for c in range(2):
                for s in range(SIDES):
                    at = (c * SIDES + s) * tq
                    for h in range(kvh):
                        r.kpart[c, s, 2 * h + e] = res[at : at + tq, h * HD : (h + 1) * HD]

    def pair(h):
        return remote(r.part.at[h, 1 - core], r.recv1.at[h], r.s1.at[h], r.r1.at[h], partner)

    def pair_kv():
        return remote(r.kpart.at[1 - core], r.krecv1, r.ks1.at[0], r.kr1.at[0], partner)

    def cross(h):
        return remote(r.ysum.at[h], r.yrecv.at[h], r.sy.at[h], r.ry.at[h], across)

    def cross_kv():
        return remote(r.kysum, r.kyrecv, r.ksy.at[0], r.kry.at[0], across)

    def long(h, i):
        return remote(
            r.zbuf.at[h, pl.ds(up(i) * tz, tz)], r.zrecv.at[h, i - 1],
            r.sz.at[h, i - 1], r.rz.at[h, i - 1], device(up(i), near, core),
        )

    def long_kv(i):
        return remote(
            r.kz.at[pl.ds(up(i) * cfg.kuz, cfg.kuz)], r.kzrecv.at[i - 1],
            r.ksz.at[i - 1], r.krz.at[i - 1], device(up(i), near, core),
        )

    def spreading(buf, send, recv, k):
        piece = buf.at[core, near, far]
        return remote(piece, piece, send.at[k], recv.at[k], chip_at(k))

    def landing(buf, send, recv, k):
        piece = buf.at[core, side(k), down(k // 2)]
        return remote(piece, piece, send.at[k], recv.at[k], chip_at(k))

    def forward(buf, send, recv):
        return remote(buf.at[core], buf.at[core], send, recv, partner)

    def arrived(buf, send, recv):
        return remote(buf.at[1 - core], buf.at[1 - core], send, recv, partner)

    def spread_out(buf, send, recv):
        loop(chips - 1, lambda k: spreading(buf, send, recv, k + 1).start())

    def pass_on(buf, send, recv, fsend, frecv):
        loop(chips - 1, lambda k: landing(buf, send, recv, k + 1).wait_recv())
        forward(buf, fsend, frecv).start()

    def g_spread(g, i):
        piece = g.buf.at[core, near, far]
        return remote(piece, piece, g.sz.at[i], g.rz.at[i], device(up(i), near, core))

    def g_land(g, i):
        piece = g.buf.at[core, near, down(i)]
        return remote(piece, piece, g.sz.at[i], g.rz.at[i], device(up(i), near, core))

    def crossing(g, n):
        return remote(g.buf.at[core, n], g.buf.at[core, n], g.sy, g.ry, across)

    def passing(g, c):
        return remote(g.buf.at[c], g.buf.at[c], g.sp, g.rp, partner)

    def gather_far(g):
        loop(half - 1, lambda i: g_spread(g, i + 1).start())

    def gather_side(g):
        loop(half - 1, lambda i: g_land(g, i + 1).wait_recv())
        crossing(g, near).start()

    def gather_pair(g):
        crossing(g, 1 - near).wait_recv()
        passing(g, core).start()

    def gather_end(g):
        passing(g, 1 - core).wait_recv()

    def gather_sent(g):
        loop(half - 1, lambda i: g_spread(g, i + 1).wait_send())
        crossing(g, near).wait_send()
        passing(g, core).wait_send()

    def gather(buf, sems, h):
        sz, rz, sy, ry, sp, rp = sems
        return types.SimpleNamespace(
            buf=buf, sz=sz.at[h], rz=rz.at[h], sy=sy.at[h], ry=ry.at[h], sp=sp.at[h], rp=rp.at[h]
        )

    def q_gather(h):
        return gather(r.gat.at[h], (r.qsz, r.qrz, r.qsy, r.qry, r.qsp, r.qrp), h)

    def kv_gather():
        return gather(r.gkv, (r.kgsz, r.kgrz, r.kgsy, r.kgry, r.kgsp, r.kgrp), 0)

    def o_gather(h):
        return r.agat.at[h], r.sa.at[h], r.ra.at[h]

    def stage_b(h):
        pair(h).wait_recv()
        r.ysum[h] = r.part[h, core, 1 - near] + r.recv1[h, 1 - near]
        cross(h).start()
        r.own[h] = r.part[h, core, near] + r.recv1[h, near]

    def stage_b_kv():
        pair_kv().wait_recv()
        r.kysum[...] = r.kpart[core, 1 - near] + r.krecv1[1 - near]
        cross_kv().start()
        r.kown[...] = r.kpart[core, near] + r.krecv1[near]

    def stage_c(h):
        cross(h).wait_recv()
        r.zbuf[h] = jnp.swapaxes(r.own[h] + r.yrecv[h], 0, 1)
        loop(half - 1, lambda i: long(h, i + 1).start())

    def stage_c_kv():
        cross_kv().wait_recv()
        r.kz[...] = r.kown[...] + r.kyrecv[...]
        loop(half - 1, lambda i: long_kv(i + 1).start())

    def stage_d(h):
        total = r.zbuf[h, pl.ds(far * tz, tz)]
        for i in range(1, half):
            long(h, i).wait_recv()
            total = total + r.zrecv[h, i - 1]
        r.gat[h, core, near, far] = total.astype(BF16)
        gather_far(q_gather(h))

    def stage_d_kv():
        total = r.kz[pl.ds(far * cfg.kuz, cfg.kuz)]
        for i in range(1, half):
            long_kv(i).wait_recv()
            total = total + r.kzrecv[i - 1]
        r.gkv[core, near, far] = total.astype(BF16)
        gather_far(kv_gather())

    def front(i):
        @pl.when(i < kvh)
        def _():
            project(i)
            pair(i).start()

        @pl.when(i < kvh + 1)
        def _():
            stage_b(i - 1)

        @pl.when(i == 1)
        def _():
            stage_b_kv()

        @pl.when((i >= 3) & (i < kvh + 3))
        def _():
            stage_c(i - 3)

        @pl.when(i == 3)
        def _():
            stage_c_kv()

            def caches(h):
                for copy in load_cache(h):
                    copy.start()

            loop(kvh, caches)
            loop(kvh, lambda h: load_wo(h).start())

        @pl.when(i >= 5)
        def _():
            stage_d(i - 5)

        @pl.when(i == 5)
        def _():
            stage_d_kv()

    project(0)
    pl.semaphore_wait(barrier, chips)
    pair(0).start()
    project_kv()
    pair_kv().start()
    loop(kvh + 4, lambda i: front(i + 1))
    gather_side(q_gather(0))
    gather_side(kv_gather())
    gather_side(q_gather(1))
    gather_pair(q_gather(0))
    gather_pair(kv_gather())
    gather_end(kv_gather())

    first_row = lax.broadcasted_iota(jnp.int32, (STAT, rows), 0) == 0
    deep = tz * group

    def send_pair(h):
        return (
            remote(
                r.pval.at[h, 1 - core], r.pgot.at[h], r.s_pv.at[h], r.r_pv.at[h], partner
            ),
            remote(
                r.pstat.at[h, 1 - core], r.pgots.at[h], r.s_ps.at[h], r.r_ps.at[h], partner
            ),
        )

    def send_own(h, k):
        return (
            remote(
                r.oval.at[h, side(k), up(k // 2)], r.ogot.at[h, k],
                r.s_ov.at[h, k], r.r_ov.at[h, k], chip_at(k),
            ),
            remote(
                r.ostat.at[h, side(k)], r.ogots.at[h, k],
                r.s_os.at[h, k], r.r_os.at[h, k], chip_at(k),
            ),
        )

    def start(copies):
        for copy in copies:
            copy.start()

    def receive(copies):
        for copy in copies:
            copy.wait_recv()

    def sent(copies):
        for copy in copies:
            copy.wait_send()

    def merge_pair(h):
        receive(send_pair(h))
        for n in range(SIDES):
            a, b = r.pstat[h, core, n], r.pgots[h, n]
            top = jnp.maximum(a[:1], b[:1])
            fa, fb = jnp.exp2(a[:1] - top), jnp.exp2(b[:1] - top)
            stat = jnp.where(first_row, top, a * fa + b * fb)
            col = jnp.where(first_row, fa, fb).T
            value = r.pval[h, core, n] * col[:, 0:1] + r.pgot[h, n] * col[:, 1:2]
            r.oval[h, n] = value.astype(BF16).reshape(half, deep, HD)
            r.ostat[h, n] = stat[:2]
        loop(chips - 1, lambda k: start(send_own(h, k + 1)))

    def merge_own(h):
        loop(chips - 1, lambda k: receive(send_own(h, k + 1)))
        stats = [r.ostat[h, near], *[r.ogots[h, k] for k in range(1, chips)]]
        top = functools.reduce(jnp.maximum, [s[:1] for s in stats])
        factors = [jnp.exp2(s[:1] - top) for s in stats]
        total = functools.reduce(jnp.add, [s[1:2] * f for s, f in zip(stats, factors)])
        depth = r.gt.shape[1]
        row = lax.broadcasted_iota(jnp.int32, (depth, rows), 0)
        table = jnp.zeros((depth, rows), F32)
        for k, f in enumerate(factors):
            table = jnp.where(row == k, f / total, table)
        r.gt[...] = table.T
        col = r.gt[pl.ds(pl.multiple_of(far * deep, 8), deep), :]
        value = r.oval[h, near, far].astype(F32) * col[:, 0:1]
        for k in range(1, chips):
            value = value + r.ogot[h, k].astype(F32) * col[:, k : k + 1]
        r.agat[h, core, near, far] = value.astype(BF16).reshape(tz, group, HD)
        spread_out(*o_gather(h))

    width = 2 * blk
    steps = cfg.pre_dev // width
    blocks = 2 * SIDES

    def attend(h, between):
        def query(b):
            return r.gat[h, b // SIDES, b % SIDES].reshape(rows, HD)

        def self_kv(e):
            unit = 2 * h + e
            f, j = unit // cfg.kuz, lax.rem(unit, cfg.kuz)
            return jnp.concatenate(
                [r.gkv[c, s, f, j] for c in range(2) for s in range(SIDES)], axis=0
            )

        self_k, self_v = self_kv(0), self_kv(1)

        def score(b, j, q, run):
            s = nt(q, r.pkb[h, j * width : (j + 1) * width, :])
            for e in range(2):
                at = 2 * j + e
                x = s[:, e * blk : (e + 1) * blk] * (r.ks[h, at] * const)
                r.scr[b % 2][:, at * blk : (at + 1) * blk] = x
                run = jnp.maximum(run, x)
            return run

        def small_scores(b, q):
            demo, bias = [], []
            for t in range(tq):
                tok = b * tq + t
                k = r.dkb[h, r.tasks[tok]]
                s = nt(q[t * group : (t + 1) * group], k) * const
                demo.append(s + r.dmask[tok : tok + 1, :])
                bias.append(jnp.broadcast_to(r.smask[tok : tok + 1, :], (group, qtok)))
            own = nt(q, self_k) * const + jnp.concatenate(bias, axis=0)
            return jnp.concatenate(demo, axis=0), own

        def first():
            return jnp.full((rows, blk), NEG, F32)

        def finish(b, e):
            total = e.total + jnp.sum(e.sums, axis=1, keepdims=True)
            value = nn(r.wts[b % 2][...], r.pvb[h]) + nn(e.w_self, self_v)
            value = value + jnp.concatenate(
                [
                    nn(e.w_demo[t * group : (t + 1) * group], r.dvb[h, r.tasks[b * tq + t]])
                    for t in range(tq)
                ],
                axis=0,
            )
            lane = lax.broadcasted_iota(jnp.int32, (rows, HD), 1)
            c, n = b // SIDES, b % SIDES
            r.pstat[h, c, n] = jnp.where(lane == 0, e.top, total).T[:STAT]
            r.pval[h, c, n] = value

        q = query(0)
        run = first()
        for j in range(steps):
            run = score(0, j, q, run)
        s_demo, s_self = small_scores(0, q)
        before = None
        for b in range(blocks):
            e = types.SimpleNamespace()
            e.top = jnp.maximum(
                jnp.max(run, axis=1, keepdims=True),
                jnp.maximum(
                    jnp.max(s_demo, axis=1, keepdims=True), jnp.max(s_self, axis=1, keepdims=True)
                ),
            )
            e_demo, e_self = jnp.exp2(s_demo - e.top), jnp.exp2(s_self - e.top)
            e.total = jnp.sum(e_demo, axis=1, keepdims=True)
            e.total = e.total + jnp.sum(e_self, axis=1, keepdims=True)
            e.w_demo, e.w_self = e_demo.astype(BF16), e_self.astype(BF16)
            e.sums = jnp.zeros((rows, blk), F32)
            if b + 1 < blocks:
                q = query(b + 1)
                run = first()
            for j in range(steps):
                for p in range(2):
                    at = 2 * j + p
                    lanes = slice(at * blk, (at + 1) * blk)
                    x = jnp.exp2(r.scr[b % 2][:, lanes] - e.top)
                    e.sums = e.sums + x
                    r.wts[b % 2][:, lanes] = (x * r.vs[h, at]).astype(BF16)
                if b + 1 < blocks:
                    run = score(b + 1, j, q, run)
                if j == 0 and before is not None:
                    finish(b - 1, before)
            if b + 1 < blocks:
                s_demo, s_self = small_scores(b + 1, q)
            before = e
            between(b)
        finish(blocks - 1, before)
        start(send_pair(h))

    def relay(h):
        pass_on(*o_gather(h), r.sh.at[h], r.rh.at[h])

    def mix(h):
        arrived(r.agat.at[h], r.sh.at[h], r.rh.at[h]).wait_recv()
        load_wo(h).wait()
        r.flat[...] = r.agat[h].reshape(qtok * group, HD).astype(F32)
        left = jnp.concatenate(
            [r.flat[pl.ds(j, qtok, stride=group), :].astype(BF16) for j in range(group)], axis=1
        )
        r.acc[...] += nn(left, r.wob[h])

    chores = (
        (0, 0, lambda: gather_side(q_gather(2))),
        (0, 1, lambda: gather_pair(q_gather(1))),
        (0, 2, lambda: gather_side(q_gather(3))),
        (1, 0, lambda: merge_pair(0)),
        (1, 1, lambda: gather_pair(q_gather(2))),
        (2, 0, lambda: merge_pair(1)),
        (2, 1, lambda: gather_pair(q_gather(3))),
        (3, 0, lambda: merge_pair(2)),
        (3, 2, lambda: merge_own(0)),
    )

    def middle(h):
        gather_end(q_gather(h))

        def between(b):
            for at, block, chore in chores:
                if block == b:
                    pl.when(h == at)(chore)

        attend(h, between)

    def cached(h):
        for copy in load_cache(h):
            copy.wait()

    loop(kvh, cached)
    loop(kvh, middle)
    merge_pair(kvh - 1)

    def tail(i):
        @pl.when((i >= 2) & (i < kvh))
        def _():
            merge_own(i - 1)

        @pl.when((i >= 3) & (i < kvh + 3))
        def _():
            relay(i - 3)

        @pl.when(i == 3)
        def _():
            merge_own(kvh - 1)

        @pl.when(i >= 4)
        def _():
            mix(i - 4)

    loop(kvh + 4, tail)
    r.out[...] = r.acc[...].astype(BF16)

    def drain(h):
        pair(h).wait_send()
        cross(h).wait_send()
        loop(half - 1, lambda i: long(h, i + 1).wait_send())
        gather_sent(q_gather(h))
        buf, send, recv = o_gather(h)
        loop(chips - 1, lambda k: spreading(buf, send, recv, k + 1).wait_send())
        forward(r.agat.at[h], r.sh.at[h], r.rh.at[h]).wait_send()
        sent(send_pair(h))
        loop(chips - 1, lambda k: sent(send_own(h, k + 1)))

    loop(kvh, drain)
    pair_kv().wait_send()
    cross_kv().wait_send()
    loop(half - 1, lambda i: long_kv(i + 1).wait_send())
    gather_sent(kv_gather())


def body(
    hidden, w_query, w_key, w_value, w_out, prefix_keys, prefix_values, key_scales, value_scales,
    demo_keys, demo_values, task_ids, demo_lengths, offsets,
):
    devices = lax.axis_size("seq")
    chips = devices // 2
    half = chips // SIDES
    qtok, depth = hidden.shape
    kvh = prefix_keys.shape[1] // HD
    group = w_query.shape[1] // HD // kvh
    tasks, demo_dev = demo_keys.shape[:2]
    pre_dev = prefix_keys.shape[0]
    tq = qtok // (2 * SIDES)
    tz = tq // half
    ku = 2 * kvh
    kuz = ku // half
    rows = tq * group
    cols = w_out.shape[1]
    cw = 4 * HD
    nch = group * HD // cw
    cfg = types.SimpleNamespace(
        kvh=kvh, group=group, half=half, devices=devices, tq=tq, tz=tz, qtok=qtok,
        blk=pre_dev // key_scales.shape[0], rows=rows, nch=nch, cw=cw, demo_dev=demo_dev,
        pre_dev=pre_dev, kuz=kuz,
    )
    smem = pl.BlockSpec(memory_space=pltpu.SMEM)
    hbm = pl.BlockSpec(memory_space=pltpu.HBM)
    ins = ["tasks", "lens", "offs", "ks", "vs"]
    ins += ["hid", "wq", "wk", "wv", "wo", "pk", "pv", "dk", "dv"]
    v = pltpu.VMEM

    def dma(*shape):
        return pltpu.SemaphoreType.DMA(shape)

    scratch = dict(
        hidb=v(hidden.shape, BF16), wkb=v(w_key.shape, BF16), wvb=v(w_value.shape, BF16),
        wqb=v((kvh * nch, depth, cw), BF16), wob=v((kvh, group * HD, cols), BF16),
        pkb=v((kvh, pre_dev, HD), BF16), pvb=v((kvh, pre_dev, HD), BF16),
        dkb=v((kvh, tasks, demo_dev, HD), BF16), dvb=v((kvh, tasks, demo_dev, HD), BF16),
        part=v((kvh, 2, SIDES, group, tq, HD), F32), recv1=v((kvh, SIDES, group, tq, HD), F32),
        own=v((kvh, group, tq, HD), F32), ysum=v((kvh, group, tq, HD), F32),
        yrecv=v((kvh, group, tq, HD), F32), zbuf=v((kvh, tq, group, HD), F32),
        zrecv=v((kvh, half - 1, tz, group, HD), F32),
        gat=v((kvh, 2, SIDES, half, tz, group, HD), BF16),
        kpart=v((2, SIDES, ku, tq, HD), F32), krecv1=v((SIDES, ku, tq, HD), F32),
        kown=v((ku, tq, HD), F32), kysum=v((ku, tq, HD), F32), kyrecv=v((ku, tq, HD), F32),
        kz=v((ku, tq, HD), F32), kzrecv=v((half - 1, kuz, tq, HD), F32),
        gkv=v((2, SIDES, half, kuz, tq, HD), BF16),
        scr0=v((rows, pre_dev), F32), scr1=v((rows, pre_dev), F32),
        wts0=v((rows, pre_dev), BF16), wts1=v((rows, pre_dev), BF16),
        dmask=v((qtok, demo_dev), F32), smask=v((qtok, qtok), F32),
        pval=v((kvh, 2, SIDES, rows, HD), F32), pstat=v((kvh, 2, SIDES, STAT, rows), F32),
        pgot=v((kvh, SIDES, rows, HD), F32), pgots=v((kvh, SIDES, STAT, rows), F32),
        oval=v((kvh, SIDES, half, tz * group, HD), BF16), ostat=v((kvh, SIDES, 2, rows), F32),
        ogot=v((kvh, chips, tz * group, HD), BF16), ogots=v((kvh, chips, 2, rows), F32),
        gt=v((rows, max(STAT, chips)), F32),
        agat=v((kvh, 2, SIDES, half, tz, group, HD), BF16),
        flat=v((qtok * group, HD), F32), acc=v((qtok, cols), F32),
        s_in=dma(3), s_wq=dma(kvh * nch), s_wo=dma(kvh),
        c_pk=dma(kvh), c_pv=dma(kvh), c_dk=dma(kvh), c_dv=dma(kvh),
        s1=dma(kvh), r1=dma(kvh), sy=dma(kvh), ry=dma(kvh),
        sz=dma(kvh, half - 1), rz=dma(kvh, half - 1),
        ks1=dma(1), kr1=dma(1), ksy=dma(1), kry=dma(1), ksz=dma(half - 1), krz=dma(half - 1),
        **{
            f"{g}{d}{e}": dma(n, half) if e == "z" else dma(n)
            for g, n in (("q", kvh), ("kg", 1))
            for d in "sr"
            for e in "zyp"
        },
        **{f"{d}_{e}": dma(kvh) for d in "sr" for e in ("pv", "ps")},
        **{f"{d}_{e}": dma(kvh, chips) for d in "sr" for e in ("ov", "os")},
        sa=dma(kvh, chips), ra=dma(kvh, chips), sh=dma(kvh), rh=dma(kvh),
    )
    names = [*ins, "out", *scratch]

    def run(*refs):
        named = dict(zip(names, refs))
        named["scr"] = (named["scr0"], named["scr1"])
        named["wts"] = (named["wts0"], named["wts1"])
        kernel(cfg, list(named), *named.values())

    return pl.pallas_call(
        run,
        name="fused",
        out_shape=jax.ShapeDtypeStruct((qtok, cols), BF16),
        in_specs=[smem] * 5 + [hbm] * 9,
        out_specs=pl.BlockSpec(memory_space=pltpu.VMEM),
        scratch_shapes=list(scratch.values()),
        compiler_params=pltpu.CompilerParams(
            collective_id=0, has_side_effects=True, vmem_limit_bytes=63 << 20
        ),
    )(
        task_ids, demo_lengths, offsets, key_scales.T, value_scales.T,
        hidden, w_query, w_key, w_value, w_out,
        prefix_keys, prefix_values, demo_keys, demo_values,
    )


def solution(mesh):
    placed = (
        P("groups", "seq"),
        P("seq", None),
        P("seq", None),
        P("seq", None),
        P(None, "seq"),
        P(("groups", "seq"), None),
        P(("groups", "seq"), None),
        P(("groups", "seq"), None),
        P(("groups", "seq"), None),
        P("groups", "seq", None),
        P("groups", "seq", None),
        P("groups"),
        P("groups"),
        P("groups"),
    )
    return jax.shard_map(
        body, mesh=mesh, in_specs=placed, out_specs=P("groups", "seq"), check_vma=False
    )
```

```python
import functools
import math
import types

import jax
import jax.numpy as jnp
from jax import lax
from jax.experimental import pallas as pl
from jax.experimental.pallas import tpu as pltpu
from jax.sharding import PartitionSpec as P

HD = 128
NEG = -1e30
SIDES = 2
STAT = 8
F32 = jnp.float32
BF16 = jnp.bfloat16


def nt(a, b):
    return lax.dot_general(a, b, (((1,), (1,)), ((), ())), preferred_element_type=F32)


def nn(a, b):
    return jnp.dot(a, b, preferred_element_type=F32)


def loop(n, step):
    def wrapped(i, carry):
        step(i)
        return carry

    lax.fori_loop(0, n, wrapped, 0)


def remote(src, dst, send, recv, dev):
    return pltpu.make_async_remote_copy(
        src_ref=src,
        dst_ref=dst,
        send_sem=send,
        recv_sem=recv,
        device_id={"seq": dev},
        device_id_type=pl.DeviceIdType.MESH,
    )


def kernel(cfg, names, *refs):
    r = types.SimpleNamespace(**dict(zip(names, refs)))
    kvh, group, half, devices = cfg.kvh, cfg.group, cfg.half, cfg.devices
    tq, tz, qtok, blk, rows = cfg.tq, cfg.tz, cfg.qtok, cfg.blk, cfg.rows
    nch, cw = cfg.nch, cfg.cw
    index = lax.axis_index("seq")
    chip, core = index // 2, lax.rem(index, 2)
    far, near = chip // SIDES, lax.rem(chip, SIDES)
    const = math.log2(math.e) / math.sqrt(HD)

    def device(f, n, c):
        return (f * SIDES + n) * 2 + c

    partner = device(far, near, 1 - core)
    across = device(far, 1 - near, core)

    def up(i):
        return lax.rem(far + i, half)

    def down(i):
        return lax.rem(far - i + half, half)

    def load_wq(k):
        src = r.wq.at[:, pl.ds(pl.multiple_of(k * cw, HD), cw)]
        return pltpu.make_async_copy(src, r.wqb.at[k], r.s_wq.at[k])

    def load_wo(h):
        deep = group * HD
        src = r.wo.at[pl.ds(pl.multiple_of(h * deep, HD), deep), :]
        return pltpu.make_async_copy(src, r.wob.at[h], r.s_wo.at[h])

    def load_cache(h):
        lanes = pl.ds(pl.multiple_of(h * HD, HD), HD)
        return (
            pltpu.make_async_copy(r.pk.at[:, lanes], r.pkb.at[h], r.c_pk.at[0]),
            pltpu.make_async_copy(r.dk.at[:, :, lanes], r.dkb.at[h], r.c_dk.at[0]),
            pltpu.make_async_copy(r.pv.at[:, lanes], r.pvb.at[h], r.c_pv.at[0]),
            pltpu.make_async_copy(r.dv.at[:, :, lanes], r.dvb.at[h], r.c_dv.at[0]),
        )

    small = [
        pltpu.make_async_copy(src, dst, r.s_in.at[i])
        for i, (src, dst) in enumerate(((r.hid, r.hidb), (r.wk, r.wkb), (r.wv, r.wvb)))
    ]
    small[0].start()
    loop(nch, lambda k: load_wq(k).start())
    small[1].start()
    small[2].start()
    loop((kvh - 1) * nch, lambda k: load_wq(k + nch).start())

    barrier = pltpu.get_barrier_semaphore()

    def hello(dev):
        pl.semaphore_signal(
            barrier, inc=1, device_id={"seq": dev}, device_id_type=pl.DeviceIdType.MESH
        )

    hello(partner)
    chips = SIDES * half

    def side(k):
        return lax.rem(near + lax.rem(k, 2), 2)

    def chip_at(k):
        return device(up(k // 2), side(k), core)

    def chip_from(k):
        return down(k // 2), side(k)

    loop(chips - 1, lambda k: hello(chip_at(k + 1)))

    lane_d = lax.broadcasted_iota(jnp.int32, (1, cfg.demo_dev), 1)
    lane_t = lax.broadcasted_iota(jnp.int32, (1, qtok), 1)

    def spread(t, carry):
        here = lane_t == t
        return tuple(jnp.where(here, v[t], old) for v, old in zip((r.tasks, r.offs), carry))

    zero = jnp.zeros((1, qtok), jnp.int32)
    task_all, off_all = lax.fori_loop(0, qtok, spread, (zero, zero))
    mine = lax.rem(lane_t, devices) == index

    def mask(t):
        task = r.tasks[t]
        left = r.lens[task] - index * cfg.demo_dev
        r.dmask[pl.ds(t, 1), :] = jnp.where(lane_d < left, 0.0, NEG)
        keep = mine & (task_all == task) & (off_all <= r.offs[t])
        r.smask[pl.ds(t, 1), :] = jnp.where(keep, 0.0, NEG)

    loop(qtok, mask)
    r.acc[...] = jnp.zeros_like(r.acc)
    small[0].wait()

    def project(h):
        def chunk(n):
            k = h * nch + n
            load_wq(k).wait()
            res = nn(r.hidb[...], r.wqb[k])
            per = cw // HD
            for c in range(2):
                for s in range(SIDES):
                    at = (c * SIDES + s) * tq
                    for u in range(per):
                        r.part[h, c, s, n * per + u] = res[at : at + tq, u * HD : (u + 1) * HD]

        loop(nch, chunk)

    def project_kv():
        for copy in small[1:]:
            copy.wait()
        for e, w in enumerate((r.wkb, r.wvb)):
            res = nn(r.hidb[...], w[...])
            for c in range(2):
                for s in range(SIDES):
                    at = (c * SIDES + s) * tq
                    for h in range(kvh):
                        r.kpart[c, s, 2 * h + e] = res[at : at + tq, h * HD : (h + 1) * HD]

    def pair(h):
        return remote(r.part.at[h, 1 - core], r.recv1.at[h], r.s1.at[h], r.r1.at[h], partner)

    def pair_kv():
        return remote(r.kpart.at[1 - core], r.krecv1, r.ks1.at[0], r.kr1.at[0], partner)

    def cross(h):
        return remote(r.ysum.at[h], r.yrecv.at[h], r.sy.at[h], r.ry.at[h], across)

    def cross_kv():
        return remote(r.kysum, r.kyrecv, r.ksy.at[0], r.kry.at[0], across)

    def long(h, i):
        return remote(
            r.zbuf.at[h, pl.ds(up(i) * tz, tz)], r.zrecv.at[h, i - 1],
            r.sz.at[h], r.rz.at[h], device(up(i), near, core),
        )

    def long_all(h):
        return remote(r.zrecv.at[h], r.zrecv.at[h], r.sz.at[h], r.rz.at[h], partner)

    def long_kv_all():
        return remote(r.kzrecv, r.kzrecv, r.ksz.at[0], r.krz.at[0], partner)

    def long_kv(i):
        return remote(
            r.kz.at[pl.ds(up(i) * cfg.kuz, cfg.kuz)], r.kzrecv.at[i - 1],
            r.ksz.at[0], r.krz.at[0], device(up(i), near, core),
        )

    def spreading(buf, send, recv, k):
        piece = buf.at[core, near, far]
        return remote(piece, piece, send, recv, chip_at(k))

    def spread_out(buf, send, recv):
        loop(chips - 1, lambda k: spreading(buf, send, recv, k + 1).start())

    def spread_all(send, recv):
        pieces = r.ogot.at[0, pl.ds(1, chips - 1)]
        return remote(pieces, pieces, send, recv, partner)

    def forward(buf, send, recv):
        return remote(buf.at[core], buf.at[core], send, recv, partner)

    def arrived(buf, send, recv):
        return remote(buf.at[1 - core], buf.at[1 - core], send, recv, partner)

    def pass_on(buf, send, recv, fsend, frecv):
        spread_all(send, recv).wait_recv()
        forward(buf, fsend, frecv).start()

    def g_spread(g, i):
        piece = g.buf.at[core, near, far]
        return remote(piece, piece, g.sz, g.rz, device(up(i), near, core))

    def g_all(g):
        pieces = g.buf.at[core, near, pl.ds(0, half - 1)]
        return remote(pieces, pieces, g.sz, g.rz, partner)

    def crossing(g, n):
        return remote(g.buf.at[core, n], g.buf.at[core, n], g.sy, g.ry, across)

    def passing(g, c):
        return remote(g.buf.at[c], g.buf.at[c], g.sp, g.rp, partner)

    def gather_far(g):
        loop(half - 1, lambda i: g_spread(g, i + 1).start())

    def gather_side(g):
        g_all(g).wait_recv()
        crossing(g, near).start()

    def gather_pair(g):
        crossing(g, 1 - near).wait_recv()
        passing(g, core).start()

    def gather_end(g):
        passing(g, 1 - core).wait_recv()

    def gather_sent(g):
        g_all(g).wait_send()
        crossing(g, near).wait_send()
        passing(g, core).wait_send()

    def gather(buf, sems, h):
        sz, rz, sy, ry, sp, rp = sems
        return types.SimpleNamespace(
            buf=buf, sz=sz.at[h], rz=rz.at[h], sy=sy.at[h], ry=ry.at[h], sp=sp.at[h], rp=rp.at[h]
        )

    def q_gather(h):
        return gather(r.gat.at[h], (r.qsz, r.qrz, r.qsy, r.qry, r.qsp, r.qrp), h)

    def kv_gather():
        return gather(r.gkv, (r.kgsz, r.kgrz, r.kgsy, r.kgry, r.kgsp, r.kgrp), 0)

    def o_gather(h):
        return r.agat.at[h], r.sa.at[h], r.ra.at[h]

    def stage_b(h):
        pair(h).wait_recv()
        r.ysum[h] = r.part[h, core, 1 - near] + r.recv1[h, 1 - near]
        cross(h).start()
        r.own[h] = r.part[h, core, near] + r.recv1[h, near]

    def stage_b_kv():
        pair_kv().wait_recv()
        r.kysum[...] = r.kpart[core, 1 - near] + r.krecv1[1 - near]
        cross_kv().start()
        r.kown[...] = r.kpart[core, near] + r.krecv1[near]

    def stage_c(h):
        cross(h).wait_recv()
        r.zbuf[h] = jnp.swapaxes(r.own[h] + r.yrecv[h], 0, 1)
        loop(half - 1, lambda i: long(h, i + 1).start())

    def stage_c_kv():
        cross_kv().wait_recv()
        r.kz[...] = r.kown[...] + r.kyrecv[...]
        loop(half - 1, lambda i: long_kv(i + 1).start())

    def stage_d(h):
        total = r.zbuf[h, pl.ds(far * tz, tz)]
        long_all(h).wait_recv()
        for i in range(1, half):
            total = total + r.zrecv[h, i - 1]
        r.gat[h, core, near, far] = total.astype(BF16)

        @pl.when(h < kvh - 1)
        def _():
            gather_far(q_gather(h))

        @pl.when(h == kvh - 1)
        def _():
            spread_out(r.gat.at[h], r.sg.at[0], r.rg.at[0])

    def stage_d_kv():
        total = r.kz[pl.ds(far * cfg.kuz, cfg.kuz)]
        long_kv_all().wait_recv()
        for i in range(1, half):
            total = total + r.kzrecv[i - 1]
        r.gkv[core, near, far] = total.astype(BF16)
        gather_far(kv_gather())

    def front(i):
        @pl.when(i < kvh)
        def _():
            project(i)
            pair(i).start()

        @pl.when(i < kvh + 1)
        def _():
            stage_b(i - 1)

        @pl.when(i == 1)
        def _():
            stage_b_kv()

        @pl.when((i >= 3) & (i < kvh + 3))
        def _():
            stage_c(i - 3)

        @pl.when(i == 3)
        def _():
            stage_c_kv()

            def caches(h):
                for copy in load_cache(h):
                    copy.start()

            loop(kvh, caches)
            loop(kvh, lambda h: load_wo(h).start())

        @pl.when(i >= 5)
        def _():
            stage_d(i - 5)

        @pl.when(i == 5)
        def _():
            stage_d_kv()

    project(0)
    pl.semaphore_wait(barrier, chips)
    pair(0).start()
    project_kv()
    pair_kv().start()
    loop(kvh + 4, lambda i: front(i + 1))
    gather_side(q_gather(0))
    gather_side(kv_gather())
    gather_side(q_gather(1))
    gather_pair(q_gather(0))
    gather_pair(kv_gather())
    gather_end(kv_gather())

    first_row = lax.broadcasted_iota(jnp.int32, (STAT, rows), 0) == 0
    deep = tz * group

    def send_pair(h):
        return (
            remote(
                r.pval.at[h, 1 - core], r.pgot.at[h], r.s_pv.at[h], r.r_pv.at[h], partner
            ),
            remote(
                r.pstat.at[h, 1 - core], r.pgots.at[h], r.s_ps.at[h], r.r_ps.at[h], partner
            ),
        )

    def send_own(h, k):
        return (
            remote(
                r.oval.at[h, side(k), up(k // 2)], r.ogot.at[h, k],
                r.s_ov.at[h], r.r_ov.at[h], chip_at(k),
            ),
            remote(
                r.ostat.at[h, side(k)], r.ogots.at[h, k],
                r.s_os.at[h], r.r_os.at[h], chip_at(k),
            ),
        )

    def send_own_all(h):
        every = pl.ds(1, chips - 1)
        return (
            remote(
                r.ogot.at[h, every], r.ogot.at[h, every], r.s_ov.at[h], r.r_ov.at[h], partner
            ),
            remote(
                r.ogots.at[h, every], r.ogots.at[h, every], r.s_os.at[h], r.r_os.at[h], partner
            ),
        )

    def start(copies):
        for copy in copies:
            copy.start()

    def receive(copies):
        for copy in copies:
            copy.wait_recv()

    def sent(copies):
        for copy in copies:
            copy.wait_send()

    def merge_pair(h):
        receive(send_pair(h))
        for n in range(SIDES):
            a, b = r.pstat[h, core, n], r.pgots[h, n]
            top = jnp.maximum(a[:1], b[:1])
            fa, fb = jnp.exp2(a[:1] - top), jnp.exp2(b[:1] - top)
            stat = jnp.where(first_row, top, a * fa + b * fb)
            col = jnp.where(first_row, fa, fb).T
            value = r.pval[h, core, n] * col[:, 0:1] + r.pgot[h, n] * col[:, 1:2]
            r.oval[h, n] = value.astype(BF16).reshape(half, deep, HD)
            r.ostat[h, n] = stat[:2]
        loop(chips - 1, lambda k: start(send_own(h, k + 1)))

    def merge_own(h):
        receive(send_own_all(h))
        stats = [r.ostat[h, near], *[r.ogots[h, k] for k in range(1, chips)]]
        top = functools.reduce(jnp.maximum, [s[:1] for s in stats])
        factors = [jnp.exp2(s[:1] - top) for s in stats]
        total = functools.reduce(jnp.add, [s[1:2] * f for s, f in zip(stats, factors)])
        depth = r.gt.shape[1]
        row = lax.broadcasted_iota(jnp.int32, (depth, rows), 0)
        table = jnp.zeros((depth, rows), F32)
        for k, f in enumerate(factors):
            table = jnp.where(row == k, f / total, table)
        r.gt[...] = table.T
        col = r.gt[pl.ds(pl.multiple_of(far * deep, 8), deep), :]
        value = r.oval[h, near, far].astype(F32) * col[:, 0:1]
        for k in range(1, chips):
            value = value + r.ogot[h, k].astype(F32) * col[:, k : k + 1]
        r.agat[h, core, near, far] = value.astype(BF16).reshape(tz, group, HD)
        spread_out(*o_gather(h))

    width = 2 * blk
    steps = cfg.pre_dev // width
    blocks = 2 * SIDES

    def attend(h, between):
        def query(b):
            return r.gat[h, b // SIDES, b % SIDES].reshape(rows, HD)

        def self_kv(e):
            unit = 2 * h + e
            f, j = unit // cfg.kuz, lax.rem(unit, cfg.kuz)
            return jnp.concatenate(
                [r.gkv[c, s, f, j] for c in range(2) for s in range(SIDES)], axis=0
            )

        self_k, self_v = self_kv(0), self_kv(1)

        def score(b, j, q, run):
            s = nt(q, r.pkb[h, j * width : (j + 1) * width, :])
            for e in range(2):
                at = 2 * j + e
                x = s[:, e * blk : (e + 1) * blk] * (r.ks[h, at] * const)
                r.scr[b % 2][:, at * blk : (at + 1) * blk] = x
                run = jnp.maximum(run, x)
            return run

        def small_scores(b, q):
            demo, bias = [], []
            for t in range(tq):
                tok = b * tq + t
                k = r.dkb[h, r.tasks[tok]]
                s = nt(q[t * group : (t + 1) * group], k) * const
                demo.append(s + r.dmask[tok : tok + 1, :])
                bias.append(jnp.broadcast_to(r.smask[tok : tok + 1, :], (group, qtok)))
            own = nt(q, self_k) * const + jnp.concatenate(bias, axis=0)
            return jnp.concatenate(demo, axis=0), own

        def first():
            return jnp.full((rows, blk), NEG, F32)

        def finish(b, e):
            total = e.total + jnp.sum(e.sums, axis=1, keepdims=True)
            value = nn(r.wts[b % 2][...], r.pvb[h]) + nn(e.w_self, self_v)
            value = value + jnp.concatenate(
                [
                    nn(e.w_demo[t * group : (t + 1) * group], r.dvb[h, r.tasks[b * tq + t]])
                    for t in range(tq)
                ],
                axis=0,
            )
            lane = lax.broadcasted_iota(jnp.int32, (rows, HD), 1)
            c, n = b // SIDES, b % SIDES
            r.pstat[h, c, n] = jnp.where(lane == 0, e.top, total).T[:STAT]
            r.pval[h, c, n] = value

        q = query(0)
        run = first()
        for j in range(steps):
            run = score(0, j, q, run)
        s_demo, s_self = small_scores(0, q)
        before = None
        for b in range(blocks):
            e = types.SimpleNamespace()
            e.top = jnp.maximum(
                jnp.max(run, axis=1, keepdims=True),
                jnp.maximum(
                    jnp.max(s_demo, axis=1, keepdims=True), jnp.max(s_self, axis=1, keepdims=True)
                ),
            )
            e_demo, e_self = jnp.exp2(s_demo - e.top), jnp.exp2(s_self - e.top)
            e.total = jnp.sum(e_demo, axis=1, keepdims=True)
            e.total = e.total + jnp.sum(e_self, axis=1, keepdims=True)
            e.w_demo, e.w_self = e_demo.astype(BF16), e_self.astype(BF16)
            e.sums = jnp.zeros((rows, blk), F32)
            if b + 1 < blocks:
                q = query(b + 1)
                run = first()
            for j in range(steps):
                for p in range(2):
                    at = 2 * j + p
                    lanes = slice(at * blk, (at + 1) * blk)
                    x = jnp.exp2(r.scr[b % 2][:, lanes] - e.top)
                    e.sums = e.sums + x
                    r.wts[b % 2][:, lanes] = (x * r.vs[h, at]).astype(BF16)
                if b + 1 < blocks:
                    run = score(b + 1, j, q, run)
                if j == 0 and before is not None:
                    finish(b - 1, before)
            if b + 1 < blocks:
                s_demo, s_self = small_scores(b + 1, q)
            before = e
            between(b)
        finish(blocks - 1, before)
        start(send_pair(h))

    def relay(h):
        pass_on(*o_gather(h), r.sh.at[h], r.rh.at[h])

    def mix(h):
        arrived(r.agat.at[h], r.sh.at[h], r.rh.at[h]).wait_recv()
        load_wo(h).wait()
        r.flat[...] = r.agat[h].reshape(qtok * group, HD).astype(F32)
        left = jnp.concatenate(
            [r.flat[pl.ds(j, qtok, stride=group), :].astype(BF16) for j in range(group)], axis=1
        )
        r.acc[...] += nn(left, r.wob[h])

    last = kvh - 1

    def last_query():
        pass_on(r.gat.at[last], r.sg.at[0], r.rg.at[0], r.qsp.at[last], r.qrp.at[last])

    chores = (
        (0, 0, lambda: gather_side(q_gather(2))),
        (0, 1, lambda: gather_pair(q_gather(1))),
        (1, 0, lambda: merge_pair(0)),
        (1, 1, lambda: gather_pair(q_gather(2))),
        (2, 0, lambda: merge_pair(1)),
        (1, 2, last_query),
        (3, 0, lambda: merge_pair(2)),
        (3, 2, lambda: merge_own(0)),
    )

    def middle(h):
        gather_end(q_gather(h))

        def between(b):
            for at, block, chore in chores:
                if block == b:
                    pl.when(h == at)(chore)

        attend(h, between)

    for buf, sem in (
        (r.pkb, r.c_pk), (r.dkb, r.c_dk), (r.pvb, r.c_pv), (r.dvb, r.c_dv),
    ):
        pltpu.make_async_copy(buf, buf, sem.at[0]).wait()

    loop(kvh, middle)
    merge_pair(kvh - 1)

    def tail(i):
        @pl.when((i >= 2) & (i < kvh))
        def _():
            merge_own(i - 1)

        @pl.when((i >= 3) & (i < kvh + 3))
        def _():
            relay(i - 3)

        @pl.when(i == 3)
        def _():
            merge_own(kvh - 1)

        @pl.when(i >= 4)
        def _():
            mix(i - 4)

    loop(kvh + 4, tail)
    r.out[...] = r.acc[...].astype(BF16)

    def drain(h):
        pair(h).wait_send()
        cross(h).wait_send()
        long_all(h).wait_send()
        passing(q_gather(h), core).wait_send()

        @pl.when(h < kvh - 1)
        def _():
            g_all(q_gather(h)).wait_send()
            crossing(q_gather(h), near).wait_send()

        buf, send, recv = o_gather(h)
        spread_all(send, recv).wait_send()
        forward(r.agat.at[h], r.sh.at[h], r.rh.at[h]).wait_send()
        sent(send_pair(h))
        sent(send_own_all(h))

    loop(kvh, drain)
    spread_all(r.sg.at[0], r.rg.at[0]).wait_send()
    pair_kv().wait_send()
    cross_kv().wait_send()
    long_kv_all().wait_send()
    gather_sent(kv_gather())


def body(
    hidden, w_query, w_key, w_value, w_out, prefix_keys, prefix_values, key_scales, value_scales,
    demo_keys, demo_values, task_ids, demo_lengths, offsets,
):
    devices = lax.axis_size("seq")
    chips = devices // 2
    half = chips // SIDES
    qtok, depth = hidden.shape
    kvh = prefix_keys.shape[1] // HD
    group = w_query.shape[1] // HD // kvh
    tasks, demo_dev = demo_keys.shape[:2]
    pre_dev = prefix_keys.shape[0]
    tq = qtok // (2 * SIDES)
    tz = tq // half
    ku = 2 * kvh
    kuz = ku // half
    rows = tq * group
    cols = w_out.shape[1]
    cw = 4 * HD
    nch = group * HD // cw
    cfg = types.SimpleNamespace(
        kvh=kvh, group=group, half=half, devices=devices, tq=tq, tz=tz, qtok=qtok,
        blk=pre_dev // key_scales.shape[0], rows=rows, nch=nch, cw=cw, demo_dev=demo_dev,
        pre_dev=pre_dev, kuz=kuz,
    )
    smem = pl.BlockSpec(memory_space=pltpu.SMEM)
    hbm = pl.BlockSpec(memory_space=pltpu.HBM)
    ins = ["tasks", "lens", "offs", "ks", "vs"]
    ins += ["hid", "wq", "wk", "wv", "wo", "pk", "pv", "dk", "dv"]
    v = pltpu.VMEM

    def dma(*shape):
        return pltpu.SemaphoreType.DMA(shape)

    scratch = dict(
        hidb=v(hidden.shape, BF16), wkb=v(w_key.shape, BF16), wvb=v(w_value.shape, BF16),
        wqb=v((kvh * nch, depth, cw), BF16), wob=v((kvh, group * HD, cols), BF16),
        pkb=v((kvh, pre_dev, HD), BF16), pvb=v((kvh, pre_dev, HD), BF16),
        dkb=v((kvh, tasks, demo_dev, HD), BF16), dvb=v((kvh, tasks, demo_dev, HD), BF16),
        part=v((kvh, 2, SIDES, group, tq, HD), F32), recv1=v((kvh, SIDES, group, tq, HD), F32),
        own=v((kvh, group, tq, HD), F32), ysum=v((kvh, group, tq, HD), F32),
        yrecv=v((kvh, group, tq, HD), F32), zbuf=v((kvh, tq, group, HD), F32),
        zrecv=v((kvh, half - 1, tz, group, HD), F32),
        gat=v((kvh, 2, SIDES, half, tz, group, HD), BF16),
        kpart=v((2, SIDES, ku, tq, HD), F32), krecv1=v((SIDES, ku, tq, HD), F32),
        kown=v((ku, tq, HD), F32), kysum=v((ku, tq, HD), F32), kyrecv=v((ku, tq, HD), F32),
        kz=v((ku, tq, HD), F32), kzrecv=v((half - 1, kuz, tq, HD), F32),
        gkv=v((2, SIDES, half, kuz, tq, HD), BF16),
        scr0=v((rows, pre_dev), F32), scr1=v((rows, pre_dev), F32),
        wts0=v((rows, pre_dev), BF16), wts1=v((rows, pre_dev), BF16),
        dmask=v((qtok, demo_dev), F32), smask=v((qtok, qtok), F32),
        pval=v((kvh, 2, SIDES, rows, HD), F32), pstat=v((kvh, 2, SIDES, STAT, rows), F32),
        pgot=v((kvh, SIDES, rows, HD), F32), pgots=v((kvh, SIDES, STAT, rows), F32),
        oval=v((kvh, SIDES, half, tz * group, HD), BF16), ostat=v((kvh, SIDES, 2, rows), F32),
        ogot=v((kvh, chips, tz * group, HD), BF16), ogots=v((kvh, chips, 2, rows), F32),
        gt=v((rows, max(STAT, chips)), F32),
        agat=v((kvh, 2, SIDES, half, tz, group, HD), BF16),
        flat=v((qtok * group, HD), F32), acc=v((qtok, cols), F32),
        s_in=dma(3), s_wq=dma(kvh * nch), s_wo=dma(kvh),
        c_pk=dma(1), c_pv=dma(1), c_dk=dma(1), c_dv=dma(1),
        s1=dma(kvh), r1=dma(kvh), sy=dma(kvh), ry=dma(kvh),
        sz=dma(kvh), rz=dma(kvh),
        ks1=dma(1), kr1=dma(1), ksy=dma(1), kry=dma(1), ksz=dma(1), krz=dma(1),
        **{
            f"{g}{d}{e}": dma(n)
            for g, n in (("q", kvh), ("kg", 1))
            for d in "sr"
            for e in "zyp"
        },
        **{f"{d}_{e}": dma(kvh) for d in "sr" for e in ("pv", "ps")},
        **{f"{d}_{e}": dma(kvh) for d in "sr" for e in ("ov", "os")},
        sa=dma(kvh), ra=dma(kvh), sg=dma(1), rg=dma(1), sh=dma(kvh), rh=dma(kvh),
    )
    names = [*ins, "out", *scratch]

    def run(*refs):
        named = dict(zip(names, refs))
        named["scr"] = (named["scr0"], named["scr1"])
        named["wts"] = (named["wts0"], named["wts1"])
        kernel(cfg, list(named), *named.values())

    return pl.pallas_call(
        run,
        name="fused",
        out_shape=jax.ShapeDtypeStruct((qtok, cols), BF16),
        in_specs=[smem] * 5 + [hbm] * 9,
        out_specs=pl.BlockSpec(memory_space=pltpu.VMEM),
        scratch_shapes=list(scratch.values()),
        compiler_params=pltpu.CompilerParams(
            collective_id=0, has_side_effects=True, vmem_limit_bytes=63 << 20
        ),
    )(
        task_ids, demo_lengths, offsets, key_scales.T, value_scales.T,
        hidden, w_query, w_key, w_value, w_out,
        prefix_keys, prefix_values, demo_keys, demo_values,
    )


def solution(mesh):
    placed = (
        P("groups", "seq"),
        P("seq", None),
        P("seq", None),
        P("seq", None),
        P(None, "seq"),
        P(("groups", "seq"), None),
        P(("groups", "seq"), None),
        P(("groups", "seq"), None),
        P(("groups", "seq"), None),
        P("groups", "seq", None),
        P("groups", "seq", None),
        P("groups"),
        P("groups"),
        P("groups"),
    )
    return jax.shard_map(
        body, mesh=mesh, in_specs=placed, out_specs=P("groups", "seq"), check_vma=False
    )
```

```python
import functools
import math
import types

import jax
import jax.numpy as jnp
from jax import lax
from jax.experimental import pallas as pl
from jax.experimental.pallas import tpu as pltpu
from jax.sharding import PartitionSpec as P

HD = 128
NEG = -1e30
SIDES = 2
STAT = 8
F32 = jnp.float32
BF16 = jnp.bfloat16


def nt(a, b):
    return lax.dot_general(a, b, (((1,), (1,)), ((), ())), preferred_element_type=F32)


def nn(a, b):
    return jnp.dot(a, b, preferred_element_type=F32)


def loop(n, step):
    def wrapped(i, carry):
        step(i)
        return carry

    lax.fori_loop(0, n, wrapped, 0)


def remote(src, dst, send, recv, dev):
    return pltpu.make_async_remote_copy(
        src_ref=src,
        dst_ref=dst,
        send_sem=send,
        recv_sem=recv,
        device_id={"seq": dev},
        device_id_type=pl.DeviceIdType.MESH,
    )


def kernel(cfg, names, *refs):
    r = types.SimpleNamespace(**dict(zip(names, refs)))
    kvh, group, half, devices = cfg.kvh, cfg.group, cfg.half, cfg.devices
    tq, tz, qtok, blk, rows = cfg.tq, cfg.tz, cfg.qtok, cfg.blk, cfg.rows
    nch, cw = cfg.nch, cfg.cw
    index = lax.axis_index("seq")
    chip, core = index // 2, lax.rem(index, 2)
    far, near = chip // SIDES, lax.rem(chip, SIDES)
    const = math.log2(math.e) / math.sqrt(HD)

    def device(f, n, c):
        return (f * SIDES + n) * 2 + c

    partner = device(far, near, 1 - core)
    across = device(far, 1 - near, core)

    def up(i):
        return lax.rem(far + i, half)

    def down(i):
        return lax.rem(far - i + half, half)

    def load_wq(k):
        src = r.wq.at[:, pl.ds(pl.multiple_of(k * cw, HD), cw)]
        return pltpu.make_async_copy(src, r.wqb.at[k], r.s_wq.at[k])

    def load_wo(h):
        deep = group * HD
        src = r.wo.at[pl.ds(pl.multiple_of(h * deep, HD), deep), :]
        return pltpu.make_async_copy(src, r.wob.at[h], r.s_wo.at[h])

    def load_cache(h):
        lanes = pl.ds(pl.multiple_of(h * HD, HD), HD)
        return (
            pltpu.make_async_copy(r.pk.at[:, lanes], r.pkb.at[h], r.c_pk.at[0]),
            pltpu.make_async_copy(r.dk.at[:, :, lanes], r.dkb.at[h], r.c_dk.at[0]),
            pltpu.make_async_copy(r.pv.at[:, lanes], r.pvb.at[h], r.c_pv.at[0]),
            pltpu.make_async_copy(r.dv.at[:, :, lanes], r.dvb.at[h], r.c_dv.at[0]),
        )

    small = [
        pltpu.make_async_copy(src, dst, r.s_in.at[i])
        for i, (src, dst) in enumerate(((r.hid, r.hidb), (r.wk, r.wkb), (r.wv, r.wvb)))
    ]
    scalars = [
        pltpu.make_async_copy(src, dst, r.s_sc.at[i])
        for i, (src, dst) in enumerate(
            (
                (r.tasks_in, r.tasks), (r.lens_in, r.lens), (r.offs_in, r.offs),
                (r.ks_in, r.ks), (r.vs_in, r.vs),
            )
        )
    ]
    small[0].start()
    for copy in scalars:
        copy.start()
    loop(nch, lambda k: load_wq(k).start())
    small[1].start()
    small[2].start()
    loop((kvh - 1) * nch, lambda k: load_wq(k + nch).start())

    barrier = pltpu.get_barrier_semaphore()

    def hello(dev):
        pl.semaphore_signal(
            barrier, inc=1, device_id={"seq": dev}, device_id_type=pl.DeviceIdType.MESH
        )

    hello(partner)
    chips = SIDES * half

    def side(k):
        return lax.rem(near + lax.rem(k, 2), 2)

    def chip_at(k):
        return device(up(k // 2), side(k), core)

    def chip_from(k):
        return down(k // 2), side(k)

    loop(chips - 1, lambda k: hello(chip_at(k + 1)))

    for copy in scalars:
        copy.wait()
    lane_d = lax.broadcasted_iota(jnp.int32, (1, cfg.demo_dev), 1)
    lane_t = lax.broadcasted_iota(jnp.int32, (1, qtok), 1)

    def spread(t, carry):
        here = lane_t == t
        return tuple(jnp.where(here, v[t], old) for v, old in zip((r.tasks, r.offs), carry))

    zero = jnp.zeros((1, qtok), jnp.int32)
    task_all, off_all = lax.fori_loop(0, qtok, spread, (zero, zero))
    mine = lax.rem(lane_t, devices) == index

    def mask(t):
        task = r.tasks[t]
        left = r.lens[task] - index * cfg.demo_dev
        r.dmask[pl.ds(t, 1), :] = jnp.where(lane_d < left, 0.0, NEG)
        keep = mine & (task_all == task) & (off_all <= r.offs[t])
        r.smask[pl.ds(t, 1), :] = jnp.where(keep, 0.0, NEG)

    loop(qtok, mask)
    r.acc[...] = jnp.zeros_like(r.acc)
    small[0].wait()

    def project(h):
        def chunk(n):
            k = h * nch + n
            load_wq(k).wait()
            res = nn(r.hidb[...], r.wqb[k])
            per = cw // HD
            for c in range(2):
                for s in range(SIDES):
                    at = (c * SIDES + s) * tq
                    for u in range(per):
                        r.part[h, c, s, n * per + u] = res[at : at + tq, u * HD : (u + 1) * HD]

        loop(nch, chunk)

    def project_kv():
        for copy in small[1:]:
            copy.wait()
        for e, w in enumerate((r.wkb, r.wvb)):
            res = nn(r.hidb[...], w[...])
            for c in range(2):
                for s in range(SIDES):
                    at = (c * SIDES + s) * tq
                    for h in range(kvh):
                        r.kpart[c, s, 2 * h + e] = res[at : at + tq, h * HD : (h + 1) * HD]

    def pair(h):
        return remote(r.part.at[h, 1 - core], r.recv1.at[h], r.s1.at[h], r.r1.at[h], partner)

    def pair_kv():
        return remote(r.kpart.at[1 - core], r.krecv1, r.ks1.at[0], r.kr1.at[0], partner)

    def cross(h):
        return remote(r.ysum.at[h], r.yrecv.at[h], r.sy.at[h], r.ry.at[h], across)

    def cross_kv():
        return remote(r.kysum, r.kyrecv, r.ksy.at[0], r.kry.at[0], across)

    def long(h, i):
        return remote(
            r.zbuf.at[h, pl.ds(up(i) * tz, tz)], r.zrecv.at[h, i - 1],
            r.sz.at[h], r.rz.at[h], device(up(i), near, core),
        )

    def long_all(h):
        return remote(r.zrecv.at[h], r.zrecv.at[h], r.sz.at[h], r.rz.at[h], partner)

    def long_kv_all():
        return remote(r.kzrecv, r.kzrecv, r.ksz.at[0], r.krz.at[0], partner)

    def long_kv(i):
        return remote(
            r.kz.at[pl.ds(up(i) * cfg.kuz, cfg.kuz)], r.kzrecv.at[i - 1],
            r.ksz.at[0], r.krz.at[0], device(up(i), near, core),
        )

    def spreading(buf, send, recv, k):
        piece = buf.at[core, near, far]
        return remote(piece, piece, send, recv, chip_at(k))

    def spread_out(buf, send, recv):
        loop(chips - 1, lambda k: spreading(buf, send, recv, k + 1).start())

    def spread_all(send, recv):
        pieces = r.ogot.at[0, pl.ds(1, chips - 1)]
        return remote(pieces, pieces, send, recv, partner)

    def forward(buf, send, recv):
        return remote(buf.at[core], buf.at[core], send, recv, partner)

    def arrived(buf, send, recv):
        return remote(buf.at[1 - core], buf.at[1 - core], send, recv, partner)

    def pass_on(buf, send, recv, fsend, frecv):
        spread_all(send, recv).wait_recv()
        forward(buf, fsend, frecv).start()

    def g_spread(g, i):
        piece = g.buf.at[core, near, far]
        return remote(piece, piece, g.sz, g.rz, device(up(i), near, core))

    def g_all(g):
        pieces = g.buf.at[core, near, pl.ds(0, half - 1)]
        return remote(pieces, pieces, g.sz, g.rz, partner)

    def crossing(g, n):
        return remote(g.buf.at[core, n], g.buf.at[core, n], g.sy, g.ry, across)

    def passing(g, c):
        return remote(g.buf.at[c], g.buf.at[c], g.sp, g.rp, partner)

    def gather_far(g):
        loop(half - 1, lambda i: g_spread(g, i + 1).start())

    def gather_side(g):
        g_all(g).wait_recv()
        crossing(g, near).start()

    def gather_pair(g):
        crossing(g, 1 - near).wait_recv()
        passing(g, core).start()

    def gather_end(g):
        passing(g, 1 - core).wait_recv()

    def gather_sent(g):
        g_all(g).wait_send()
        crossing(g, near).wait_send()
        passing(g, core).wait_send()

    def gather(buf, sems, h):
        sz, rz, sy, ry, sp, rp = sems
        return types.SimpleNamespace(
            buf=buf, sz=sz.at[h], rz=rz.at[h], sy=sy.at[h], ry=ry.at[h], sp=sp.at[h], rp=rp.at[h]
        )

    def q_gather(h):
        return gather(r.gat.at[h], (r.qsz, r.qrz, r.qsy, r.qry, r.qsp, r.qrp), h)

    def kv_gather():
        return gather(r.gkv, (r.kgsz, r.kgrz, r.kgsy, r.kgry, r.kgsp, r.kgrp), 0)

    def o_gather(h):
        return r.agat.at[h], r.sa.at[h], r.ra.at[h]

    def stage_b(h):
        pair(h).wait_recv()
        r.ysum[h] = r.part[h, core, 1 - near] + r.recv1[h, 1 - near]
        cross(h).start()
        r.own[h] = r.part[h, core, near] + r.recv1[h, near]

    def stage_b_kv():
        pair_kv().wait_recv()
        r.kysum[...] = r.kpart[core, 1 - near] + r.krecv1[1 - near]
        cross_kv().start()
        r.kown[...] = r.kpart[core, near] + r.krecv1[near]

    def stage_c(h):
        cross(h).wait_recv()
        r.zbuf[h] = jnp.swapaxes(r.own[h] + r.yrecv[h], 0, 1)
        loop(half - 1, lambda i: long(h, i + 1).start())

    def stage_c_kv():
        cross_kv().wait_recv()
        r.kz[...] = r.kown[...] + r.kyrecv[...]
        loop(half - 1, lambda i: long_kv(i + 1).start())

    direct = (kvh - 1,)

    def is_direct(h):
        return functools.reduce(jnp.logical_or, [h == d for d in direct], h < 0)

    def stage_d(h):
        total = r.zbuf[h, pl.ds(far * tz, tz)]
        long_all(h).wait_recv()
        for i in range(1, half):
            total = total + r.zrecv[h, i - 1]
        r.gat[h, core, near, far] = total.astype(BF16)

        @pl.when(is_direct(h))
        def _():
            spread_out(r.gat.at[h], r.qsz.at[h], r.qrz.at[h])

        @pl.when(jnp.logical_not(is_direct(h)))
        def _():
            gather_far(q_gather(h))

    def stage_d_kv():
        total = r.kz[pl.ds(far * cfg.kuz, cfg.kuz)]
        long_kv_all().wait_recv()
        for i in range(1, half):
            total = total + r.kzrecv[i - 1]
        r.gkv[core, near, far] = total.astype(BF16)
        gather_far(kv_gather())

    def query_far(h):
        if h not in direct:
            gather_side(q_gather(h))

    def query_near(h):
        if h in direct:
            pass_on(r.gat.at[h], r.qsz.at[h], r.qrz.at[h], r.qsp.at[h], r.qrp.at[h])
        else:
            gather_pair(q_gather(h))

    def front(i):
        @pl.when(i < kvh)
        def _():
            project(i)
            pair(i).start()

        @pl.when(i < kvh + 1)
        def _():
            stage_b(i - 1)

        @pl.when(i == 1)
        def _():
            stage_b_kv()

        @pl.when((i >= 3) & (i < kvh + 3))
        def _():
            stage_c(i - 3)

        @pl.when(i == 3)
        def _():
            stage_c_kv()

            def caches(h):
                for copy in load_cache(h):
                    copy.start()

            loop(kvh, caches)
            loop(kvh, lambda h: load_wo(h).start())

        @pl.when(i == 8)
        def _():
            query_far(0)
            gather_side(kv_gather())

        @pl.when(i >= 5)
        def _():
            stage_d(i - 5)

        @pl.when(i == 5)
        def _():
            stage_d_kv()

        @pl.when(i == 8)
        def _():
            query_far(1)

    project(0)
    pl.semaphore_wait(barrier, chips)
    pair(0).start()
    project_kv()
    pair_kv().start()
    loop(kvh + 4, lambda i: front(i + 1))
    first_row = lax.broadcasted_iota(jnp.int32, (STAT, rows), 0) == 0
    deep = tz * group

    def send_pair(h):
        return (
            remote(
                r.pval.at[h, 1 - core], r.pgot.at[h], r.s_pv.at[h], r.r_pv.at[h], partner
            ),
            remote(
                r.pstat.at[h, 1 - core], r.pgots.at[h], r.s_ps.at[h], r.r_ps.at[h], partner
            ),
        )

    def send_own(h, k):
        return (
            remote(
                r.oval.at[h, side(k), up(k // 2)], r.ogot.at[h, k],
                r.s_ov.at[h], r.r_ov.at[h], chip_at(k),
            ),
            remote(
                r.ostat.at[h, side(k)], r.ogots.at[h, k],
                r.s_os.at[h], r.r_os.at[h], chip_at(k),
            ),
        )

    def send_own_all(h):
        every = pl.ds(1, chips - 1)
        return (
            remote(
                r.ogot.at[h, every], r.ogot.at[h, every], r.s_ov.at[h], r.r_ov.at[h], partner
            ),
            remote(
                r.ogots.at[h, every], r.ogots.at[h, every], r.s_os.at[h], r.r_os.at[h], partner
            ),
        )

    def start(copies):
        for copy in copies:
            copy.start()

    def receive(copies):
        for copy in copies:
            copy.wait_recv()

    def sent(copies):
        for copy in copies:
            copy.wait_send()

    def merge_pair(h):
        receive(send_pair(h))
        for n in range(SIDES):
            a, b = r.pstat[h, core, n], r.pgots[h, n]
            top = jnp.maximum(a[:1], b[:1])
            fa, fb = jnp.exp2(a[:1] - top), jnp.exp2(b[:1] - top)
            stat = jnp.where(first_row, top, a * fa + b * fb)
            col = jnp.where(first_row, fa, fb).T
            value = r.pval[h, core, n] * col[:, 0:1] + r.pgot[h, n] * col[:, 1:2]
            r.oval[h, n] = value.astype(BF16).reshape(half, deep, HD)
            r.ostat[h, n] = stat[:2]
        loop(chips - 1, lambda k: start(send_own(h, k + 1)))

    def merge_own(h):
        receive(send_own_all(h))
        stats = [r.ostat[h, near], *[r.ogots[h, k] for k in range(1, chips)]]
        top = functools.reduce(jnp.maximum, [s[:1] for s in stats])
        factors = [jnp.exp2(s[:1] - top) for s in stats]
        total = functools.reduce(jnp.add, [s[1:2] * f for s, f in zip(stats, factors)])
        depth = r.gt.shape[1]
        row = lax.broadcasted_iota(jnp.int32, (depth, rows), 0)
        table = jnp.zeros((depth, rows), F32)
        for k, f in enumerate(factors):
            table = jnp.where(row == k, f / total, table)
        r.gt[...] = table.T
        col = r.gt[pl.ds(pl.multiple_of(far * deep, 8), deep), :]
        value = r.oval[h, near, far].astype(F32) * col[:, 0:1]
        for k in range(1, chips):
            value = value + r.ogot[h, k].astype(F32) * col[:, k : k + 1]
        r.agat[h, core, near, far] = value.astype(BF16).reshape(tz, group, HD)
        spread_out(*o_gather(h))

    width = 2 * blk
    steps = cfg.pre_dev // width
    blocks = 2 * SIDES

    def attend(h, between):
        def query(b):
            return r.gat[h, b // SIDES, b % SIDES].reshape(rows, HD)

        def self_kv(e):
            unit = 2 * h + e
            f, j = unit // cfg.kuz, lax.rem(unit, cfg.kuz)
            return jnp.concatenate(
                [r.gkv[c, s, f, j] for c in range(2) for s in range(SIDES)], axis=0
            )

        self_k, self_v = self_kv(0), self_kv(1)

        def score(b, j, q, run):
            s = nt(q, r.pkb[h, j * width : (j + 1) * width, :])
            for e in range(2):
                at = 2 * j + e
                x = s[:, e * blk : (e + 1) * blk] * (r.ks[h, at] * const)
                r.scr[b % 2][:, at * blk : (at + 1) * blk] = x
                run = jnp.maximum(run, x)
            return run

        def small_scores(b, q):
            demo, bias = [], []
            for t in range(tq):
                tok = b * tq + t
                k = r.dkb[h, r.tasks[tok]]
                s = nt(q[t * group : (t + 1) * group], k) * const
                demo.append(s + r.dmask[tok : tok + 1, :])
                bias.append(jnp.broadcast_to(r.smask[tok : tok + 1, :], (group, qtok)))
            own = nt(q, self_k) * const + jnp.concatenate(bias, axis=0)
            return jnp.concatenate(demo, axis=0), own

        def first():
            return jnp.full((rows, blk), NEG, F32)

        def finish(b, e):
            total = e.total + jnp.sum(e.sums, axis=1, keepdims=True)
            value = nn(r.wts[b % 2][...], r.pvb[h]) + nn(e.w_self, self_v)
            value = value + jnp.concatenate(
                [
                    nn(e.w_demo[t * group : (t + 1) * group], r.dvb[h, r.tasks[b * tq + t]])
                    for t in range(tq)
                ],
                axis=0,
            )
            lane = lax.broadcasted_iota(jnp.int32, (rows, HD), 1)
            c, n = b // SIDES, b % SIDES
            r.pstat[h, c, n] = jnp.where(lane == 0, e.top, total).T[:STAT]
            r.pval[h, c, n] = value

        q = query(0)
        run = first()
        for j in range(steps):
            run = score(0, j, q, run)
        s_demo, s_self = small_scores(0, q)
        before = None
        for b in range(blocks):
            e = types.SimpleNamespace()
            e.top = jnp.maximum(
                jnp.max(run, axis=1, keepdims=True),
                jnp.maximum(
                    jnp.max(s_demo, axis=1, keepdims=True), jnp.max(s_self, axis=1, keepdims=True)
                ),
            )
            e_demo, e_self = jnp.exp2(s_demo - e.top), jnp.exp2(s_self - e.top)
            e.total = jnp.sum(e_demo, axis=1, keepdims=True)
            e.total = e.total + jnp.sum(e_self, axis=1, keepdims=True)
            e.w_demo, e.w_self = e_demo.astype(BF16), e_self.astype(BF16)
            e.sums = jnp.zeros((rows, blk), F32)
            if b + 1 < blocks:
                q = query(b + 1)
                run = first()
            for j in range(steps):
                for p in range(2):
                    at = 2 * j + p
                    lanes = slice(at * blk, (at + 1) * blk)
                    x = jnp.exp2(r.scr[b % 2][:, lanes] - e.top)
                    e.sums = e.sums + x
                    r.wts[b % 2][:, lanes] = (x * r.vs[h, at]).astype(BF16)
                if b + 1 < blocks:
                    run = score(b + 1, j, q, run)
                if j == 0 and before is not None:
                    finish(b - 1, before)
            if b + 1 < blocks:
                s_demo, s_self = small_scores(b + 1, q)
            before = e
            between(b)
        finish(blocks - 1, before)
        start(send_pair(h))

    def relay(h):
        pass_on(*o_gather(h), r.sh.at[h], r.rh.at[h])

    def mix(h):
        arrived(r.agat.at[h], r.sh.at[h], r.rh.at[h]).wait_recv()
        load_wo(h).wait()
        r.flat[...] = r.agat[h].reshape(qtok * group, HD).astype(F32)
        left = jnp.concatenate(
            [r.flat[pl.ds(j, qtok, stride=group), :].astype(BF16) for j in range(group)], axis=1
        )
        r.acc[...] += nn(left, r.wob[h])

    chores = (
        (0, 0, lambda: query_far(2)),
        (0, 1, lambda: query_near(1)),
        (0, 2, lambda: query_far(3)),
        (1, 0, lambda: merge_pair(0)),
        (1, 1, lambda: query_near(2)),
        (2, 0, lambda: merge_pair(1)),
        (1, 2, lambda: query_near(3)),
        (3, 0, lambda: merge_pair(2)),
        (3, 2, lambda: merge_own(0)),
    )

    def middle(h):
        gather_end(q_gather(h))

        def between(b):
            for at, block, chore in chores:
                if block == b:
                    pl.when(h == at)(chore)

        attend(h, between)

    for buf, sem in (
        (r.pkb, r.c_pk), (r.dkb, r.c_dk), (r.pvb, r.c_pv), (r.dvb, r.c_dv),
    ):
        pltpu.make_async_copy(buf, buf, sem.at[0]).wait()

    query_near(0)
    gather_pair(kv_gather())
    gather_end(kv_gather())
    loop(kvh, middle)
    merge_pair(kvh - 1)

    def tail(i):
        @pl.when((i >= 2) & (i < kvh))
        def _():
            merge_own(i - 1)

        @pl.when((i >= 3) & (i < kvh + 3))
        def _():
            relay(i - 3)

        @pl.when(i == 3)
        def _():
            merge_own(kvh - 1)

        @pl.when(i >= 4)
        def _():
            mix(i - 4)

    loop(kvh + 4, tail)
    r.out[...] = r.acc[...].astype(BF16)

    def drain(h):
        pair(h).wait_send()
        cross(h).wait_send()
        long_all(h).wait_send()
        passing(q_gather(h), core).wait_send()

        @pl.when(is_direct(h))
        def _():
            spread_all(r.qsz.at[h], r.qrz.at[h]).wait_send()

        @pl.when(jnp.logical_not(is_direct(h)))
        def _():
            g_all(q_gather(h)).wait_send()
            crossing(q_gather(h), near).wait_send()

        buf, send, recv = o_gather(h)
        spread_all(send, recv).wait_send()
        forward(r.agat.at[h], r.sh.at[h], r.rh.at[h]).wait_send()
        sent(send_pair(h))
        sent(send_own_all(h))

    loop(kvh, drain)
    pair_kv().wait_send()
    cross_kv().wait_send()
    long_kv_all().wait_send()
    gather_sent(kv_gather())


def body(
    hidden, w_query, w_key, w_value, w_out, prefix_keys, prefix_values, key_scales, value_scales,
    demo_keys, demo_values, task_ids, demo_lengths, offsets,
):
    devices = lax.axis_size("seq")
    chips = devices // 2
    half = chips // SIDES
    qtok, depth = hidden.shape
    kvh = prefix_keys.shape[1] // HD
    group = w_query.shape[1] // HD // kvh
    tasks, demo_dev = demo_keys.shape[:2]
    pre_dev = prefix_keys.shape[0]
    tq = qtok // (2 * SIDES)
    tz = tq // half
    ku = 2 * kvh
    kuz = ku // half
    rows = tq * group
    cols = w_out.shape[1]
    cw = 4 * HD
    nch = group * HD // cw
    cfg = types.SimpleNamespace(
        kvh=kvh, group=group, half=half, devices=devices, tq=tq, tz=tz, qtok=qtok,
        blk=pre_dev // key_scales.shape[0], rows=rows, nch=nch, cw=cw, demo_dev=demo_dev,
        pre_dev=pre_dev, kuz=kuz,
    )
    hbm = pl.BlockSpec(memory_space=pltpu.HBM)
    ins = ["tasks_in", "lens_in", "offs_in", "ks_in", "vs_in"]
    ins += ["hid", "wq", "wk", "wv", "wo", "pk", "pv", "dk", "dv"]
    v = pltpu.VMEM

    def dma(*shape):
        return pltpu.SemaphoreType.DMA(shape)

    nblk = key_scales.shape[0]
    smem = pltpu.SMEM
    scratch = dict(
        tasks=smem((qtok,), jnp.int32), lens=smem((tasks,), jnp.int32),
        offs=smem((qtok,), jnp.int32), ks=smem((kvh, nblk), F32), vs=smem((kvh, nblk), F32),
        s_sc=dma(5),
        hidb=v(hidden.shape, BF16), wkb=v(w_key.shape, BF16), wvb=v(w_value.shape, BF16),
        wqb=v((kvh * nch, depth, cw), BF16), wob=v((kvh, group * HD, cols), BF16),
        pkb=v((kvh, pre_dev, HD), BF16), pvb=v((kvh, pre_dev, HD), BF16),
        dkb=v((kvh, tasks, demo_dev, HD), BF16), dvb=v((kvh, tasks, demo_dev, HD), BF16),
        part=v((kvh, 2, SIDES, group, tq, HD), F32), recv1=v((kvh, SIDES, group, tq, HD), F32),
        own=v((kvh, group, tq, HD), F32), ysum=v((kvh, group, tq, HD), F32),
        yrecv=v((kvh, group, tq, HD), F32), zbuf=v((kvh, tq, group, HD), F32),
        zrecv=v((kvh, half - 1, tz, group, HD), F32),
        gat=v((kvh, 2, SIDES, half, tz, group, HD), BF16),
        kpart=v((2, SIDES, ku, tq, HD), F32), krecv1=v((SIDES, ku, tq, HD), F32),
        kown=v((ku, tq, HD), F32), kysum=v((ku, tq, HD), F32), kyrecv=v((ku, tq, HD), F32),
        kz=v((ku, tq, HD), F32), kzrecv=v((half - 1, kuz, tq, HD), F32),
        gkv=v((2, SIDES, half, kuz, tq, HD), BF16),
        scr0=v((rows, pre_dev), F32), scr1=v((rows, pre_dev), F32),
        wts0=v((rows, pre_dev), BF16), wts1=v((rows, pre_dev), BF16),
        dmask=v((qtok, demo_dev), F32), smask=v((qtok, qtok), F32),
        pval=v((kvh, 2, SIDES, rows, HD), F32), pstat=v((kvh, 2, SIDES, STAT, rows), F32),
        pgot=v((kvh, SIDES, rows, HD), F32), pgots=v((kvh, SIDES, STAT, rows), F32),
        oval=v((kvh, SIDES, half, tz * group, HD), BF16), ostat=v((kvh, SIDES, 2, rows), F32),
        ogot=v((kvh, chips, tz * group, HD), BF16), ogots=v((kvh, chips, 2, rows), F32),
        gt=v((rows, max(STAT, chips)), F32),
        agat=v((kvh, 2, SIDES, half, tz, group, HD), BF16),
        flat=v((qtok * group, HD), F32), acc=v((qtok, cols), F32),
        s_in=dma(3), s_wq=dma(kvh * nch), s_wo=dma(kvh),
        c_pk=dma(1), c_pv=dma(1), c_dk=dma(1), c_dv=dma(1),
        s1=dma(kvh), r1=dma(kvh), sy=dma(kvh), ry=dma(kvh),
        sz=dma(kvh), rz=dma(kvh),
        ks1=dma(1), kr1=dma(1), ksy=dma(1), kry=dma(1), ksz=dma(1), krz=dma(1),
        **{
            f"{g}{d}{e}": dma(n)
            for g, n in (("q", kvh), ("kg", 1))
            for d in "sr"
            for e in "zyp"
        },
        **{f"{d}_{e}": dma(kvh) for d in "sr" for e in ("pv", "ps")},
        **{f"{d}_{e}": dma(kvh) for d in "sr" for e in ("ov", "os")},
        sa=dma(kvh), ra=dma(kvh), sh=dma(kvh), rh=dma(kvh),
    )
    names = [*ins, "out", *scratch]

    def run(*refs):
        named = dict(zip(names, refs))
        named["scr"] = (named["scr0"], named["scr1"])
        named["wts"] = (named["wts0"], named["wts1"])
        kernel(cfg, list(named), *named.values())

    return pl.pallas_call(
        run,
        name="fused",
        out_shape=jax.ShapeDtypeStruct((qtok, cols), BF16),
        in_specs=[hbm] * 14,
        out_specs=pl.BlockSpec(memory_space=pltpu.VMEM),
        scratch_shapes=list(scratch.values()),
        compiler_params=pltpu.CompilerParams(
            collective_id=0, has_side_effects=True, vmem_limit_bytes=63 << 20
        ),
    )(
        task_ids, demo_lengths, offsets, key_scales.T, value_scales.T,
        hidden, w_query, w_key, w_value, w_out,
        prefix_keys, prefix_values, demo_keys, demo_values,
    )


def solution(mesh):
    placed = (
        P("groups", "seq"),
        P("seq", None),
        P("seq", None),
        P("seq", None),
        P(None, "seq"),
        P(("groups", "seq"), None),
        P(("groups", "seq"), None),
        P(("groups", "seq"), None),
        P(("groups", "seq"), None),
        P("groups", "seq", None),
        P("groups", "seq", None),
        P("groups"),
        P("groups"),
        P("groups"),
    )
    return jax.shard_map(
        body, mesh=mesh, in_specs=placed, out_specs=P("groups", "seq"), check_vma=False
    )
```

```python
import functools
import math
import types

import jax
import jax.numpy as jnp
from jax import lax
from jax.experimental import pallas as pl
from jax.experimental.pallas import tpu as pltpu
from jax.sharding import PartitionSpec as P

HD = 128
NEG = -1e30
SIDES = 2
STAT = 8
F32 = jnp.float32
BF16 = jnp.bfloat16


def nt(a, b):
    return lax.dot_general(a, b, (((1,), (1,)), ((), ())), preferred_element_type=F32)


def nn(a, b):
    return jnp.dot(a, b, preferred_element_type=F32)


def loop(n, step):
    def wrapped(i, carry):
        step(i)
        return carry

    lax.fori_loop(0, n, wrapped, 0)


def remote(src, dst, send, recv, dev):
    return pltpu.make_async_remote_copy(
        src_ref=src,
        dst_ref=dst,
        send_sem=send,
        recv_sem=recv,
        device_id={"seq": dev},
        device_id_type=pl.DeviceIdType.MESH,
    )


def kernel(cfg, names, *refs):
    r = types.SimpleNamespace(**dict(zip(names, refs)))
    kvh, group, half, devices = cfg.kvh, cfg.group, cfg.half, cfg.devices
    tq, tz, qtok, blk, rows = cfg.tq, cfg.tz, cfg.qtok, cfg.blk, cfg.rows
    nch, cw = cfg.nch, cfg.cw
    index = lax.axis_index("seq")
    chip, core = index // 2, lax.rem(index, 2)
    far, near = chip // SIDES, lax.rem(chip, SIDES)
    const = math.log2(math.e) / math.sqrt(HD)

    def device(f, n, c):
        return (f * SIDES + n) * 2 + c

    partner = device(far, near, 1 - core)
    across = device(far, 1 - near, core)

    def up(i):
        return lax.rem(far + i, half)

    def down(i):
        return lax.rem(far - i + half, half)

    def load_wq(k):
        src = r.wq.at[:, pl.ds(pl.multiple_of(k * cw, HD), cw)]
        return pltpu.make_async_copy(src, r.wqb.at[k], r.s_wq.at[k])

    def load_wo(h):
        deep = group * HD
        src = r.wo.at[pl.ds(pl.multiple_of(h * deep, HD), deep), :]
        return pltpu.make_async_copy(src, r.wob.at[h], r.s_wo.at[h])

    def load_cache(h):
        lanes = pl.ds(pl.multiple_of(h * HD, HD), HD)
        return (
            pltpu.make_async_copy(r.pk.at[:, lanes], r.pkb.at[h], r.c_pk.at[0]),
            pltpu.make_async_copy(r.dk.at[:, :, lanes], r.dkb.at[h], r.c_dk.at[0]),
            pltpu.make_async_copy(r.pv.at[:, lanes], r.pvb.at[h], r.c_pv.at[0]),
            pltpu.make_async_copy(r.dv.at[:, :, lanes], r.dvb.at[h], r.c_dv.at[0]),
        )

    small = [
        pltpu.make_async_copy(src, dst, r.s_in.at[i])
        for i, (src, dst) in enumerate(((r.hid, r.hidb), (r.wk, r.wkb), (r.wv, r.wvb)))
    ]
    scalars = [
        pltpu.make_async_copy(src, dst, r.s_sc.at[i])
        for i, (src, dst) in enumerate(
            (
                (r.tasks_in, r.tasks), (r.lens_in, r.lens), (r.offs_in, r.offs),
                (r.ks_in, r.ks), (r.vs_in, r.vs),
            )
        )
    ]
    small[0].start()
    for copy in scalars:
        copy.start()
    loop(nch, lambda k: load_wq(k).start())
    small[1].start()
    small[2].start()
    loop((kvh - 1) * nch, lambda k: load_wq(k + nch).start())

    barrier = pltpu.get_barrier_semaphore()

    def hello(dev):
        pl.semaphore_signal(
            barrier, inc=1, device_id={"seq": dev}, device_id_type=pl.DeviceIdType.MESH
        )

    hello(partner)
    chips = SIDES * half

    def side(k):
        return lax.rem(near + lax.rem(k, 2), 2)

    def chip_at(k):
        return device(up(k // 2), side(k), core)

    def chip_from(k):
        return down(k // 2), side(k)

    loop(chips - 1, lambda k: hello(chip_at(k + 1)))

    for copy in scalars:
        copy.wait()
    lane_d = lax.broadcasted_iota(jnp.int32, (1, cfg.demo_dev), 1)
    lane_t = lax.broadcasted_iota(jnp.int32, (1, qtok), 1)

    def spread(t, carry):
        here = lane_t == t
        return tuple(jnp.where(here, v[t], old) for v, old in zip((r.tasks, r.offs), carry))

    zero = jnp.zeros((1, qtok), jnp.int32)
    task_all, off_all = lax.fori_loop(0, qtok, spread, (zero, zero))
    mine = lax.rem(lane_t, devices) == index

    def mask(t):
        task = r.tasks[t]
        left = r.lens[task] - index * cfg.demo_dev
        r.dmask[pl.ds(t, 1), :] = jnp.where(lane_d < left, 0.0, NEG)
        keep = mine & (task_all == task) & (off_all <= r.offs[t])
        r.smask[pl.ds(t, 1), :] = jnp.where(keep, 0.0, NEG)

    loop(qtok, mask)
    r.acc[...] = jnp.zeros_like(r.acc)
    small[0].wait()

    def project(h):
        def chunk(n):
            k = h * nch + n
            load_wq(k).wait()
            res = nn(r.hidb[...], r.wqb[k])
            per = cw // HD
            for c in range(2):
                for s in range(SIDES):
                    at = (c * SIDES + s) * tq
                    for u in range(per):
                        r.part[h, c, s, n * per + u] = res[at : at + tq, u * HD : (u + 1) * HD]

        loop(nch, chunk)

    def project_kv():
        for copy in small[1:]:
            copy.wait()
        for e, w in enumerate((r.wkb, r.wvb)):
            res = nn(r.hidb[...], w[...])
            for c in range(2):
                for s in range(SIDES):
                    at = (c * SIDES + s) * tq
                    for h in range(kvh):
                        r.kpart[c, s, 2 * h + e] = res[at : at + tq, h * HD : (h + 1) * HD]

    def pair(h):
        return remote(r.part.at[h, 1 - core], r.recv1.at[h], r.s1.at[h], r.r1.at[h], partner)

    def pair_kv():
        return remote(r.kpart.at[1 - core], r.krecv1, r.ks1.at[0], r.kr1.at[0], partner)

    def cross(h):
        return remote(r.ysum.at[h], r.yrecv.at[h], r.sy.at[h], r.ry.at[h], across)

    def cross_kv():
        return remote(r.kysum, r.kyrecv, r.ksy.at[0], r.kry.at[0], across)

    def long(h, i):
        return remote(
            r.zbuf.at[h, pl.ds(up(i) * tz, tz)], r.zrecv.at[h, i - 1],
            r.sz.at[h], r.rz.at[h], device(up(i), near, core),
        )

    def long_all(h):
        return remote(r.zrecv.at[h], r.zrecv.at[h], r.sz.at[h], r.rz.at[h], partner)

    def long_kv_all():
        return remote(r.kzrecv, r.kzrecv, r.ksz.at[0], r.krz.at[0], partner)

    def long_kv(i):
        return remote(
            r.kz.at[pl.ds(up(i) * cfg.kuz, cfg.kuz)], r.kzrecv.at[i - 1],
            r.ksz.at[0], r.krz.at[0], device(up(i), near, core),
        )

    def spreading(buf, send, recv, k):
        piece = buf.at[core, near, far]
        return remote(piece, piece, send, recv, chip_at(k))

    def spread_out(buf, send, recv):
        loop(chips - 1, lambda k: spreading(buf, send, recv, k + 1).start())

    def spread_all(send, recv):
        pieces = r.ogot.at[0, pl.ds(1, chips - 1)]
        return remote(pieces, pieces, send, recv, partner)

    def forward(buf, send, recv):
        return remote(buf.at[core], buf.at[core], send, recv, partner)

    def arrived(buf, send, recv):
        return remote(buf.at[1 - core], buf.at[1 - core], send, recv, partner)

    def pass_on(buf, send, recv, fsend, frecv):
        spread_all(send, recv).wait_recv()
        forward(buf, fsend, frecv).start()

    def g_spread(g, i):
        piece = g.buf.at[core, near, far]
        return remote(piece, piece, g.sz, g.rz, device(up(i), near, core))

    def g_all(g):
        pieces = g.buf.at[core, near, pl.ds(0, half - 1)]
        return remote(pieces, pieces, g.sz, g.rz, partner)

    def crossing(g, n):
        return remote(g.buf.at[core, n], g.buf.at[core, n], g.sy, g.ry, across)

    def passing(g, c):
        return remote(g.buf.at[c], g.buf.at[c], g.sp, g.rp, partner)

    def gather_far(g):
        loop(half - 1, lambda i: g_spread(g, i + 1).start())

    def gather_side(g):
        g_all(g).wait_recv()
        crossing(g, near).start()

    def gather_pair(g):
        crossing(g, 1 - near).wait_recv()
        passing(g, core).start()

    def gather_end(g):
        passing(g, 1 - core).wait_recv()

    def gather_sent(g):
        g_all(g).wait_send()
        crossing(g, near).wait_send()
        passing(g, core).wait_send()

    def gather(buf, sems, h):
        sz, rz, sy, ry, sp, rp = sems
        return types.SimpleNamespace(
            buf=buf, sz=sz.at[h], rz=rz.at[h], sy=sy.at[h], ry=ry.at[h], sp=sp.at[h], rp=rp.at[h]
        )

    def q_gather(h):
        return gather(r.gat.at[h], (r.qsz, r.qrz, r.qsy, r.qry, r.qsp, r.qrp), h)

    def kv_gather():
        return gather(r.gkv, (r.kgsz, r.kgrz, r.kgsy, r.kgry, r.kgsp, r.kgrp), 0)

    def o_gather(h):
        return r.agat.at[h], r.sa.at[h], r.ra.at[h]

    def stage_b(h):
        pair(h).wait_recv()
        r.ysum[h] = r.part[h, core, 1 - near] + r.recv1[h, 1 - near]
        cross(h).start()
        r.own[h] = r.part[h, core, near] + r.recv1[h, near]

    def stage_b_kv():
        pair_kv().wait_recv()
        r.kysum[...] = r.kpart[core, 1 - near] + r.krecv1[1 - near]
        cross_kv().start()
        r.kown[...] = r.kpart[core, near] + r.krecv1[near]

    def stage_c(h):
        cross(h).wait_recv()
        r.zbuf[h] = jnp.swapaxes(r.own[h] + r.yrecv[h], 0, 1)
        loop(half - 1, lambda i: long(h, i + 1).start())

    def stage_c_kv():
        cross_kv().wait_recv()
        r.kz[...] = r.kown[...] + r.kyrecv[...]
        loop(half - 1, lambda i: long_kv(i + 1).start())

    direct = (kvh - 1,)

    def is_direct(h):
        return functools.reduce(jnp.logical_or, [h == d for d in direct], h < 0)

    def stage_d(h):
        total = r.zbuf[h, pl.ds(far * tz, tz)]
        long_all(h).wait_recv()
        for i in range(1, half):
            total = total + r.zrecv[h, i - 1]
        r.gat[h, core, near, far] = total.astype(BF16)

        @pl.when(is_direct(h))
        def _():
            spread_out(r.gat.at[h], r.qsz.at[h], r.qrz.at[h])

        @pl.when(jnp.logical_not(is_direct(h)))
        def _():
            gather_far(q_gather(h))

    def stage_d_kv():
        total = r.kz[pl.ds(far * cfg.kuz, cfg.kuz)]
        long_kv_all().wait_recv()
        for i in range(1, half):
            total = total + r.kzrecv[i - 1]
        r.gkv[core, near, far] = total.astype(BF16)
        gather_far(kv_gather())

    def query_far(h):
        if h not in direct:
            gather_side(q_gather(h))

    def query_near(h):
        if h in direct:
            pass_on(r.gat.at[h], r.qsz.at[h], r.qrz.at[h], r.qsp.at[h], r.qrp.at[h])
        else:
            gather_pair(q_gather(h))

    def front(i):
        @pl.when(i < kvh)
        def _():
            project(i)
            pair(i).start()

        @pl.when(i < kvh + 1)
        def _():
            stage_b(i - 1)

        @pl.when(i == 1)
        def _():
            stage_b_kv()

        @pl.when((i >= 3) & (i < kvh + 3))
        def _():
            stage_c(i - 3)

        @pl.when(i == 3)
        def _():
            stage_c_kv()

            def caches(h):
                for copy in load_cache(h):
                    copy.start()

            loop(kvh, caches)
            loop(kvh, lambda h: load_wo(h).start())

        @pl.when(i == 8)
        def _():
            query_far(0)
            gather_side(kv_gather())

        @pl.when(i >= 5)
        def _():
            stage_d(i - 5)

        @pl.when(i == 5)
        def _():
            stage_d_kv()

        @pl.when(i == 8)
        def _():
            query_far(1)

    project(0)
    pl.semaphore_wait(barrier, chips)
    pair(0).start()
    project_kv()
    pair_kv().start()
    loop(kvh + 4, lambda i: front(i + 1))
    first_row = lax.broadcasted_iota(jnp.int32, (STAT, rows), 0) == 0
    deep = tz * group

    def send_pair(h):
        return (
            remote(
                r.pval.at[h, 1 - core], r.pgot.at[h], r.s_pv.at[h], r.r_pv.at[h], partner
            ),
            remote(
                r.pstat.at[h, 1 - core], r.pgots.at[h], r.s_ps.at[h], r.r_ps.at[h], partner
            ),
        )

    def send_own(h, k):
        return (
            remote(
                r.oval.at[h, side(k), up(k // 2)], r.ogot.at[h, k],
                r.s_ov.at[h], r.r_ov.at[h], chip_at(k),
            ),
            remote(
                r.ostat.at[h, side(k)], r.ogots.at[h, k],
                r.s_os.at[h], r.r_os.at[h], chip_at(k),
            ),
        )

    def send_own_all(h):
        every = pl.ds(1, chips - 1)
        return (
            remote(
                r.ogot.at[h, every], r.ogot.at[h, every], r.s_ov.at[h], r.r_ov.at[h], partner
            ),
            remote(
                r.ogots.at[h, every], r.ogots.at[h, every], r.s_os.at[h], r.r_os.at[h], partner
            ),
        )

    def start(copies):
        for copy in copies:
            copy.start()

    def receive(copies):
        for copy in copies:
            copy.wait_recv()

    def sent(copies):
        for copy in copies:
            copy.wait_send()

    def merge_pair(h):
        receive(send_pair(h))
        for n in range(SIDES):
            a, b = r.pstat[h, core, n], r.pgots[h, n]
            top = jnp.maximum(a[:1], b[:1])
            fa, fb = jnp.exp2(a[:1] - top), jnp.exp2(b[:1] - top)
            stat = jnp.where(first_row, top, a * fa + b * fb)
            col = jnp.where(first_row, fa, fb).T
            value = r.pval[h, core, n] * col[:, 0:1] + r.pgot[h, n] * col[:, 1:2]
            r.oval[h, n] = value.astype(BF16).reshape(half, deep, HD)
            r.ostat[h, n] = stat[:2]
        loop(chips - 1, lambda k: start(send_own(h, k + 1)))

    def merge_own(h):
        receive(send_own_all(h))
        stats = [r.ostat[h, near], *[r.ogots[h, k] for k in range(1, chips)]]
        top = functools.reduce(jnp.maximum, [s[:1] for s in stats])
        factors = [jnp.exp2(s[:1] - top) for s in stats]
        total = functools.reduce(jnp.add, [s[1:2] * f for s, f in zip(stats, factors)])
        depth = r.gt.shape[1]
        row = lax.broadcasted_iota(jnp.int32, (depth, rows), 0)
        table = jnp.zeros((depth, rows), F32)
        for k, f in enumerate(factors):
            table = jnp.where(row == k, f / total, table)
        r.gt[...] = table.T
        col = r.gt[pl.ds(pl.multiple_of(far * deep, 8), deep), :]
        value = r.oval[h, near, far].astype(F32) * col[:, 0:1]
        for k in range(1, chips):
            value = value + r.ogot[h, k].astype(F32) * col[:, k : k + 1]
        r.agat[h, core, near, far] = value.astype(BF16).reshape(tz, group, HD)
        spread_out(*o_gather(h))

    width = 2 * blk
    steps = cfg.pre_dev // width
    blocks = 2 * SIDES

    def attend(h, between):
        def part(b):
            return 1 - core if b < SIDES else core

        def base(b):
            return (part(b) * SIDES + b % SIDES) * tq

        def query(b):
            return r.gat[h, part(b), b % SIDES].reshape(rows, HD)

        def self_kv(e):
            unit = 2 * h + e
            f, j = unit // cfg.kuz, lax.rem(unit, cfg.kuz)
            return jnp.concatenate(
                [r.gkv[c, s, f, j] for c in range(2) for s in range(SIDES)], axis=0
            )

        self_k, self_v = self_kv(0), self_kv(1)

        def score(b, j, q, run):
            s = nt(q, r.pkb[h, j * width : (j + 1) * width, :])
            for e in range(2):
                at = 2 * j + e
                x = s[:, e * blk : (e + 1) * blk] * (r.ks[h, at] * const)
                r.scr[b % 2][:, at * blk : (at + 1) * blk] = x
                run = jnp.maximum(run, x)
            return run

        def small_scores(b, q):
            demo, bias = [], []
            for t in range(0, tq, 2):
                tok = base(b) + t
                k = jnp.concatenate([r.dkb[h, r.tasks[tok + p]] for p in range(2)], axis=0)
                s = nt(q[t * group : (t + 2) * group], k) * const
                for p in range(2):
                    x = s[p * group : (p + 1) * group, p * cfg.demo_dev : (p + 1) * cfg.demo_dev]
                    demo.append(x + r.dmask[pl.ds(tok + p, 1), :])
            for t in range(tq):
                tok = base(b) + t
                bias.append(jnp.broadcast_to(r.smask[pl.ds(tok, 1), :], (group, qtok)))
            own = nt(q, self_k) * const + jnp.concatenate(bias, axis=0)
            return jnp.concatenate(demo, axis=0), own

        def first():
            return jnp.full((rows, blk), NEG, F32)

        def finish(b, e):
            total = e.total + jnp.sum(e.sums, axis=1, keepdims=True)
            value = nn(r.wts[b % 2][...], r.pvb[h]) + nn(e.w_self, self_v)
            value = value + jnp.concatenate(
                [
                    nn(e.w_demo[t * group : (t + 1) * group], r.dvb[h, r.tasks[base(b) + t]])
                    for t in range(tq)
                ],
                axis=0,
            )
            lane = lax.broadcasted_iota(jnp.int32, (rows, HD), 1)
            c, n = part(b), b % SIDES
            r.pstat[h, c, n] = jnp.where(lane == 0, e.top, total).T[:STAT]
            r.pval[h, c, n] = value
            if b == SIDES - 1:
                start(send_pair(h))

        q = query(0)
        run = first()
        for j in range(steps):
            run = score(0, j, q, run)
        s_demo, s_self = small_scores(0, q)
        before = None
        for b in range(blocks):
            e = types.SimpleNamespace()
            e.top = jnp.maximum(
                jnp.max(run, axis=1, keepdims=True),
                jnp.maximum(
                    jnp.max(s_demo, axis=1, keepdims=True), jnp.max(s_self, axis=1, keepdims=True)
                ),
            )
            e_demo, e_self = jnp.exp2(s_demo - e.top), jnp.exp2(s_self - e.top)
            e.total = jnp.sum(e_demo, axis=1, keepdims=True)
            e.total = e.total + jnp.sum(e_self, axis=1, keepdims=True)
            e.w_demo, e.w_self = e_demo.astype(BF16), e_self.astype(BF16)
            e.sums = jnp.zeros((rows, blk), F32)
            if b + 1 < blocks:
                q = query(b + 1)
                run = first()
            for j in range(steps):
                for p in range(2):
                    at = 2 * j + p
                    lanes = slice(at * blk, (at + 1) * blk)
                    x = jnp.exp2(r.scr[b % 2][:, lanes] - e.top)
                    e.sums = e.sums + x
                    r.wts[b % 2][:, lanes] = (x * r.vs[h, at]).astype(BF16)
                if b + 1 < blocks:
                    run = score(b + 1, j, q, run)
                if j == 0 and before is not None:
                    finish(b - 1, before)
            if b + 1 < blocks:
                s_demo, s_self = small_scores(b + 1, q)
            before = e
            between(b)
        finish(blocks - 1, before)

    def relay(h):
        pass_on(*o_gather(h), r.sh.at[h], r.rh.at[h])

    def mix(h):
        arrived(r.agat.at[h], r.sh.at[h], r.rh.at[h]).wait_recv()
        load_wo(h).wait()
        r.flat[...] = r.agat[h].reshape(qtok * group, HD).astype(F32)
        left = jnp.concatenate(
            [r.flat[pl.ds(j, qtok, stride=group), :].astype(BF16) for j in range(group)], axis=1
        )
        r.acc[...] += nn(left, r.wob[h])

    chores = (
        (0, 0, lambda: query_far(2)),
        (0, 1, lambda: query_near(1)),
        (0, 2, lambda: query_far(3)),
        (1, 0, lambda: merge_pair(0)),
        (1, 1, lambda: query_near(2)),
        (2, 0, lambda: merge_pair(1)),
        (1, 2, lambda: query_near(3)),
        (3, 0, lambda: merge_pair(2)),
        (3, 2, lambda: merge_own(0)),
    )

    def middle(h):
        gather_end(q_gather(h))

        def between(b):
            for at, block, chore in chores:
                if block == b:
                    pl.when(h == at)(chore)

        attend(h, between)

    for buf, sem in (
        (r.pkb, r.c_pk), (r.dkb, r.c_dk), (r.pvb, r.c_pv), (r.dvb, r.c_dv),
    ):
        pltpu.make_async_copy(buf, buf, sem.at[0]).wait()

    query_near(0)
    gather_pair(kv_gather())
    gather_end(kv_gather())
    loop(kvh, middle)
    merge_pair(kvh - 1)

    def tail(i):
        @pl.when((i >= 2) & (i < kvh))
        def _():
            merge_own(i - 1)

        @pl.when((i >= 3) & (i < kvh + 3))
        def _():
            relay(i - 3)

        @pl.when(i == 3)
        def _():
            merge_own(kvh - 1)

        @pl.when(i >= 4)
        def _():
            mix(i - 4)

    loop(kvh + 4, tail)
    r.out[...] = r.acc[...].astype(BF16)

    def drain(h):
        pair(h).wait_send()
        cross(h).wait_send()
        long_all(h).wait_send()
        passing(q_gather(h), core).wait_send()

        @pl.when(is_direct(h))
        def _():
            spread_all(r.qsz.at[h], r.qrz.at[h]).wait_send()

        @pl.when(jnp.logical_not(is_direct(h)))
        def _():
            g_all(q_gather(h)).wait_send()
            crossing(q_gather(h), near).wait_send()

        buf, send, recv = o_gather(h)
        spread_all(send, recv).wait_send()
        forward(r.agat.at[h], r.sh.at[h], r.rh.at[h]).wait_send()
        sent(send_pair(h))
        sent(send_own_all(h))

    loop(kvh, drain)
    pair_kv().wait_send()
    cross_kv().wait_send()
    long_kv_all().wait_send()
    gather_sent(kv_gather())


def body(
    hidden, w_query, w_key, w_value, w_out, prefix_keys, prefix_values, key_scales, value_scales,
    demo_keys, demo_values, task_ids, demo_lengths, offsets,
):
    devices = lax.axis_size("seq")
    chips = devices // 2
    half = chips // SIDES
    qtok, depth = hidden.shape
    kvh = prefix_keys.shape[1] // HD
    group = w_query.shape[1] // HD // kvh
    tasks, demo_dev = demo_keys.shape[:2]
    pre_dev = prefix_keys.shape[0]
    tq = qtok // (2 * SIDES)
    tz = tq // half
    ku = 2 * kvh
    kuz = ku // half
    rows = tq * group
    cols = w_out.shape[1]
    cw = 4 * HD
    nch = group * HD // cw
    cfg = types.SimpleNamespace(
        kvh=kvh, group=group, half=half, devices=devices, tq=tq, tz=tz, qtok=qtok,
        blk=pre_dev // key_scales.shape[0], rows=rows, nch=nch, cw=cw, demo_dev=demo_dev,
        pre_dev=pre_dev, kuz=kuz,
    )
    hbm = pl.BlockSpec(memory_space=pltpu.HBM)
    ins = ["tasks_in", "lens_in", "offs_in", "ks_in", "vs_in"]
    ins += ["hid", "wq", "wk", "wv", "wo", "pk", "pv", "dk", "dv"]
    v = pltpu.VMEM

    def dma(*shape):
        return pltpu.SemaphoreType.DMA(shape)

    nblk = key_scales.shape[0]
    smem = pltpu.SMEM
    scratch = dict(
        tasks=smem((qtok,), jnp.int32), lens=smem((tasks,), jnp.int32),
        offs=smem((qtok,), jnp.int32), ks=smem((kvh, nblk), F32), vs=smem((kvh, nblk), F32),
        s_sc=dma(5),
        hidb=v(hidden.shape, BF16), wkb=v(w_key.shape, BF16), wvb=v(w_value.shape, BF16),
        wqb=v((kvh * nch, depth, cw), BF16), wob=v((kvh, group * HD, cols), BF16),
        pkb=v((kvh, pre_dev, HD), BF16), pvb=v((kvh, pre_dev, HD), BF16),
        dkb=v((kvh, tasks, demo_dev, HD), BF16), dvb=v((kvh, tasks, demo_dev, HD), BF16),
        part=v((kvh, 2, SIDES, group, tq, HD), F32), recv1=v((kvh, SIDES, group, tq, HD), F32),
        own=v((kvh, group, tq, HD), F32), ysum=v((kvh, group, tq, HD), F32),
        yrecv=v((kvh, group, tq, HD), F32), zbuf=v((kvh, tq, group, HD), F32),
        zrecv=v((kvh, half - 1, tz, group, HD), F32),
        gat=v((kvh, 2, SIDES, half, tz, group, HD), BF16),
        kpart=v((2, SIDES, ku, tq, HD), F32), krecv1=v((SIDES, ku, tq, HD), F32),
        kown=v((ku, tq, HD), F32), kysum=v((ku, tq, HD), F32), kyrecv=v((ku, tq, HD), F32),
        kz=v((ku, tq, HD), F32), kzrecv=v((half - 1, kuz, tq, HD), F32),
        gkv=v((2, SIDES, half, kuz, tq, HD), BF16),
        scr0=v((rows, pre_dev), F32), scr1=v((rows, pre_dev), F32),
        wts0=v((rows, pre_dev), BF16), wts1=v((rows, pre_dev), BF16),
        dmask=v((qtok, demo_dev), F32), smask=v((qtok, qtok), F32),
        pval=v((kvh, 2, SIDES, rows, HD), F32), pstat=v((kvh, 2, SIDES, STAT, rows), F32),
        pgot=v((kvh, SIDES, rows, HD), F32), pgots=v((kvh, SIDES, STAT, rows), F32),
        oval=v((kvh, SIDES, half, tz * group, HD), BF16), ostat=v((kvh, SIDES, 2, rows), F32),
        ogot=v((kvh, chips, tz * group, HD), BF16), ogots=v((kvh, chips, 2, rows), F32),
        gt=v((rows, max(STAT, chips)), F32),
        agat=v((kvh, 2, SIDES, half, tz, group, HD), BF16),
        flat=v((qtok * group, HD), F32), acc=v((qtok, cols), F32),
        s_in=dma(3), s_wq=dma(kvh * nch), s_wo=dma(kvh),
        c_pk=dma(1), c_pv=dma(1), c_dk=dma(1), c_dv=dma(1),
        s1=dma(kvh), r1=dma(kvh), sy=dma(kvh), ry=dma(kvh),
        sz=dma(kvh), rz=dma(kvh),
        ks1=dma(1), kr1=dma(1), ksy=dma(1), kry=dma(1), ksz=dma(1), krz=dma(1),
        **{
            f"{g}{d}{e}": dma(n)
            for g, n in (("q", kvh), ("kg", 1))
            for d in "sr"
            for e in "zyp"
        },
        **{f"{d}_{e}": dma(kvh) for d in "sr" for e in ("pv", "ps")},
        **{f"{d}_{e}": dma(kvh) for d in "sr" for e in ("ov", "os")},
        sa=dma(kvh), ra=dma(kvh), sh=dma(kvh), rh=dma(kvh),
    )
    names = [*ins, "out", *scratch]

    def run(*refs):
        named = dict(zip(names, refs))
        named["scr"] = (named["scr0"], named["scr1"])
        named["wts"] = (named["wts0"], named["wts1"])
        kernel(cfg, list(named), *named.values())

    return pl.pallas_call(
        run,
        name="fused",
        out_shape=jax.ShapeDtypeStruct((qtok, cols), BF16),
        in_specs=[hbm] * 14,
        out_specs=pl.BlockSpec(memory_space=pltpu.VMEM),
        scratch_shapes=list(scratch.values()),
        compiler_params=pltpu.CompilerParams(
            collective_id=0, has_side_effects=True, vmem_limit_bytes=63 << 20
        ),
    )(
        task_ids, demo_lengths, offsets, key_scales.T, value_scales.T,
        hidden, w_query, w_key, w_value, w_out,
        prefix_keys, prefix_values, demo_keys, demo_values,
    )


def solution(mesh):
    placed = (
        P("groups", "seq"),
        P("seq", None),
        P("seq", None),
        P("seq", None),
        P(None, "seq"),
        P(("groups", "seq"), None),
        P(("groups", "seq"), None),
        P(("groups", "seq"), None),
        P(("groups", "seq"), None),
        P("groups", "seq", None),
        P("groups", "seq", None),
        P("groups"),
        P("groups"),
        P("groups"),
    )
    return jax.shard_map(
        body, mesh=mesh, in_specs=placed, out_specs=P("groups", "seq"), check_vma=False
    )
```
